32 devices in a mesh: dp: 8 (over y, x, core), fsdp: 4 (over z).
Axes of the slice: x: 2, y: 2, z: 4, core: 2. Of those that a mesh axis runs over, the one named last changes fastest.
Arguments:
- patches: bfloat16 [32768, 768], P(('dp', 'fsdp')), may hold values from -6 to 6
- segments: int32 [32768], P(('dp', 'fsdp')), may hold values from 0 to 16, as said below
- send_slot: int32 [32, 16], P(('dp', 'fsdp')), may hold values from 0 to 15, each once within a row
- visible: int32 [512, 49], P(('dp', 'fsdp')), may hold values from 0 to 195, as said below
- enc_gain: bfloat16 [2, 768], P(None, ('dp', 'fsdp')), may hold values from 0.25 to 1.75
- enc_shift: bfloat16 [6, 768], P(None, ('dp', 'fsdp')), may hold values from -3 to 3
- enc_hidden: bfloat16 [3072], P(('dp', 'fsdp')), may hold values from -3 to 3
- enc_qkv: bfloat16 [768, 2304], P(('dp', 'fsdp')), may hold values from -0.21875 to 0.21875
- enc_out: bfloat16 [768, 768], P(('dp', 'fsdp')), may hold values from -0.875 to 0.875
- enc_up: bfloat16 [768, 3072], P(('dp', 'fsdp')), may hold values from -0.21875 to 0.21875
- enc_down: bfloat16 [3072, 768], P(('dp', 'fsdp')), may hold values from -0.109375 to 0.109375
- embedding: bfloat16 [768, 512], P(('dp', 'fsdp')), may hold values from -0.21875 to 0.21875
- mask_token: bfloat16 [512], P(('dp', 'fsdp')), may hold values from -4 to 4
- dec_gain: bfloat16 [2, 512], P(None, ('dp', 'fsdp')), may hold values from 0.25 to 1.75
- dec_shift: bfloat16 [7, 512], P(None, ('dp', 'fsdp')), may hold values from -3 to 3
- dec_hidden: bfloat16 [2048], P(('dp', 'fsdp')), may hold values from -3 to 3
- dec_qkv: bfloat16 [512, 1536], P(('dp', 'fsdp')), may hold values from -0.25 to 0.25
- dec_out: bfloat16 [512, 512], P(('dp', 'fsdp')), may hold values from -2 to 2
- dec_up: bfloat16 [512, 2048], P(('dp', 'fsdp')), may hold values from -0.25 to 0.25
- dec_down: bfloat16 [2048, 512], P(('dp', 'fsdp')), may hold values from -0.125 to 0.125
- cotangent: bfloat16 [100352, 512], P(('dp', 'fsdp')), may hold values from -6 to 6
Outputs:
- decoded: bfloat16 [100352, 512], P(('dp', 'fsdp'))
- grad_patches: float32 [32768, 768], P(('dp', 'fsdp'))
- grad_enc_gain: float32 [2, 768], P(None, ('dp', 'fsdp'))
- grad_enc_shift: float32 [6, 768], P(None, ('dp', 'fsdp'))
- grad_enc_hidden: float32 [3072], P(('dp', 'fsdp'))
- grad_enc_qkv: float32 [768, 2304], P(('dp', 'fsdp'))
- grad_enc_out: float32 [768, 768], P(('dp', 'fsdp'))
- grad_enc_up: float32 [768, 3072], P(('dp', 'fsdp'))
- grad_enc_down: float32 [3072, 768], P(('dp', 'fsdp'))
- grad_embedding: float32 [768, 512], P(('dp', 'fsdp'))
- grad_mask_token: float32 [512], P(('dp', 'fsdp'))
- grad_dec_gain: float32 [2, 512], P(None, ('dp', 'fsdp'))
- grad_dec_shift: float32 [7, 512], P(None, ('dp', 'fsdp'))
- grad_dec_hidden: float32 [2048], P(('dp', 'fsdp'))
- grad_dec_qkv: float32 [512, 1536], P(('dp', 'fsdp'))
- grad_dec_out: float32 [512, 512], P(('dp', 'fsdp'))
- grad_dec_up: float32 [512, 2048], P(('dp', 'fsdp'))
- grad_dec_down: float32 [2048, 512], P(('dp', 'fsdp'))
The draws below stay inside these ranges and needn't reach their ends.
Inputs may be any that keep to these rules, and one draw needn't show every extreme that they name: `segments`: in the q-th aligned block of 512 rows of a device (q below 2), images 8 q to 8 q + 7 of that device each fill 49 consecutive rows, in increasing order; all other rows hold 16 (padding). `send_slot`: each row is a permutation. `visible`: each row holds 49 different patch indices.
All inputs are finite; a program needn't handle non-finite values.
Results may differ from the reference program's by a relative error of at most 0.015.
Values may be sent and summed in bfloat16 or wider, within the bound.
No kernel may reach another device: no remote copies, remote signals or barrier semaphores. Data moves between devices by JAX's collectives and lax.ppermute only.
A program may use at most 448 MiB of HBM per device.

```python
import jax
import jax.numpy as jnp
from jax import lax

ENC_HEADS = 12
ENC_HEAD = 64
ENC_HIDDEN = 3072
DEC_HEADS = 16
DEC_HEAD = 32
DEC_HIDDEN = 2048
SIDE = 14
VISIBLE = 49
SEQ_LEN = 512
IMG_SEQ = 8
SEQS_DEV = 2
ENC_WIDTH = 768
DEC_WIDTH = 512
PATCHES = 196
IMG_DEV = 16
ROWS_DEV = 1024
ROWS = 32768
IMAGES = 512
DEC_ROWS = 100352
N_DP = 8
N_FSDP = 4
DEVICES = 32


def draw_segments(key, part):
    block_count = ROWS // SEQ_LEN
    spare_rows = SEQ_LEN - IMG_SEQ * VISIBLE
    cut_points = jnp.sort(jax.random.randint(key, (block_count, IMG_SEQ), 0, spare_rows + 1), axis=1)
    starts = cut_points + jnp.arange(IMG_SEQ, dtype=jnp.int32)[None, :] * VISIBLE
    positions = jnp.arange(SEQ_LEN, dtype=jnp.int32)
    inside = (positions[None, None, :] >= starts[:, :, None]) & (positions[None, None, :] < starts[:, :, None] + VISIBLE)
    local_ids = jnp.arange(IMG_SEQ, dtype=jnp.int32)[None, :] + (jnp.arange(block_count, dtype=jnp.int32) % SEQS_DEV)[:, None] * IMG_SEQ
    seg_marks = jnp.where(jnp.any(inside, axis=1), jnp.sum(jnp.where(inside, local_ids[:, :, None], 0), axis=1), IMG_DEV)
    return seg_marks.reshape(ROWS).astype(jnp.int32)


def draw_visible(key, part):
    key_list = jax.random.split(key, IMAGES)

    def choose_patches(one_key):
        return jax.random.permutation(one_key, PATCHES)[:VISIBLE]
    return jax.vmap(choose_patches)(key_list).astype(jnp.int32)


def block_levels(stream_key, extent, shards, least, top_value):
    level, own = 1.0, jax.random.fold_in(stream_key, 6)
    for position, shards_of in shards:
        draws = jnp.exp(jax.random.uniform(jax.random.fold_in(own, position), (shards_of,), jnp.float32, least / len(shards), top_value / len(shards)))
        level = level * jnp.repeat(draws, extent[position] // shards_of).reshape([-1 if axis == position else 1 for axis in range(len(extent))])
    return level


def bell_draw(rng, extent, scale, bound, pieces=(), kind=jnp.bfloat16):
    array = scale * jax.random.normal(rng, extent, jnp.float32)
    if pieces:
        array = array * block_levels(rng, extent, pieces, -0.22, 0.18)
    return jnp.clip(array, -bound, bound).astype(kind)


def setup_inputs(seed: int = 0) -> dict:
    streams_of = jax.random.split(jax.random.key(seed), 22)
    patches = bell_draw(streams_of[0], (ROWS, ENC_WIDTH), 1.0, 6.0, ((0, 32),))
    segments = draw_segments(jax.random.fold_in(streams_of[21], 71), 0)
    send_slot = jax.vmap(lambda own: jax.random.permutation(own, IMG_DEV))(jax.random.split(streams_of[2], DEVICES)).reshape((DEVICES, IMG_DEV)).astype(jnp.int32)
    visible = draw_visible(jax.random.fold_in(streams_of[21], 71), 0)
    enc_gain = jnp.clip(1.0 + 0.15 * jax.random.normal(streams_of[4], (2, ENC_WIDTH), jnp.float32), 0.25, 1.75).astype(jnp.bfloat16)
    enc_shift = bell_draw(streams_of[5], (6, ENC_WIDTH), 0.5, 3.0, ((1, 32),))
    enc_hidden = bell_draw(streams_of[6], (ENC_HIDDEN,), 0.5, 3.0, ((0, 32),))
    enc_qkv = bell_draw(streams_of[7], (ENC_WIDTH, 3 * ENC_WIDTH), ENC_WIDTH ** -0.5, 0.21875, ((0, 32),))
    enc_out = bell_draw(streams_of[8], (ENC_WIDTH, ENC_WIDTH), (ENC_WIDTH * 3 // VISIBLE) ** -0.5, 0.875, ((0, 32),))
    enc_up = bell_draw(streams_of[9], (ENC_WIDTH, ENC_HIDDEN), ENC_WIDTH ** -0.5, 0.21875, ((0, 32),))
    enc_down = bell_draw(streams_of[10], (ENC_HIDDEN, ENC_WIDTH), ENC_HIDDEN ** -0.5, 0.109375, ((0, 32),))
    embedding = bell_draw(streams_of[11], (ENC_WIDTH, DEC_WIDTH), ENC_WIDTH ** -0.5, 0.21875, ((0, 32),))
    mask_token = bell_draw(streams_of[12], (DEC_WIDTH,), 1.0, 4.0, ((0, 32),))
    dec_gain = jnp.clip(1.0 + 0.15 * jax.random.normal(streams_of[13], (2, DEC_WIDTH), jnp.float32), 0.25, 1.75).astype(jnp.bfloat16)
    dec_shift = bell_draw(streams_of[14], (7, DEC_WIDTH), 0.5, 3.0, ((1, 32),))
    dec_hidden = bell_draw(streams_of[15], (DEC_HIDDEN,), 0.5, 3.0, ((0, 32),))
    dec_qkv = bell_draw(streams_of[16], (DEC_WIDTH, 3 * DEC_WIDTH), DEC_WIDTH ** -0.5, 0.25, ((0, 32),))
    dec_out = bell_draw(streams_of[17], (DEC_WIDTH, DEC_WIDTH), (DEC_WIDTH * 4 // PATCHES) ** -0.5, 2.0, ((0, 32),))
    dec_up = bell_draw(streams_of[18], (DEC_WIDTH, DEC_HIDDEN), DEC_WIDTH ** -0.5, 0.25, ((0, 32),))
    dec_down = bell_draw(streams_of[19], (DEC_HIDDEN, DEC_WIDTH), DEC_HIDDEN ** -0.5, 0.125, ((0, 32),))
    cotangent = bell_draw(streams_of[20], (DEC_ROWS, DEC_WIDTH), 1.0, 6.0, ((0, 32),))
    return {"patches": patches, "segments": segments, "send_slot": send_slot, "visible": visible, "enc_gain": enc_gain, "enc_shift": enc_shift, "enc_hidden": enc_hidden, "enc_qkv": enc_qkv, "enc_out": enc_out, "enc_up": enc_up, "enc_down": enc_down, "embedding": embedding, "mask_token": mask_token, "dec_gain": dec_gain, "dec_shift": dec_shift, "dec_hidden": dec_hidden, "dec_qkv": dec_qkv, "dec_out": dec_out, "dec_up": dec_up, "dec_down": dec_down, "cotangent": cotangent}


highest = lax.Precision.HIGHEST

@jax.custom_vjp
def low(v):
    return lax.optimization_barrier(v.astype(jnp.bfloat16)).astype(jnp.float32)

@jax.custom_vjp
def low_back(v):
    return v

def low_keep(v):
    return (low(v), None)

def low_pass(kept, grad):
    return (grad,)

def back_keep(v):
    return (v, None)

def back_low(kept, grad):
    return (low(grad),)
low.defvjp(low_keep, low_pass)
low_back.defvjp(back_keep, back_low)

def normed(values, norm_gain, norm_shift):
    center = values - lax.optimization_barrier(jnp.mean(values, axis=-1, keepdims=True))
    spread = lax.optimization_barrier(jnp.mean(center * center, axis=-1, keepdims=True))
    return center * lax.rsqrt(spread + 1e-06) * norm_gain + norm_shift

def project(values, weight):
    return jnp.einsum('...i,io->...o', values, weight, precision=highest)

def position_table(side_cells, model_width):
    quarter = model_width // 4
    frequency = 1.0 / 10000.0 ** (jnp.arange(quarter, dtype=jnp.float32) / quarter)
    cell_ids = jnp.arange(side_cells * side_cells, dtype=jnp.int32)
    grid_rows = (cell_ids // side_cells).astype(jnp.float32)[:, None] * frequency[None, :]
    grid_cols = (cell_ids % side_cells).astype(jnp.float32)[:, None] * frequency[None, :]
    return jnp.concatenate([jnp.sin(grid_rows), jnp.cos(grid_rows), jnp.sin(grid_cols), jnp.cos(grid_cols)], axis=1)

def attend(mixed, allowed, head_count, head_size):
    batch_size, length, triple = mixed.shape
    split_heads = mixed.reshape(batch_size, length, 3, head_count, head_size)
    queries = split_heads[:, :, 0]
    key_heads = split_heads[:, :, 1]
    value_heads = split_heads[:, :, 2]
    scores = jnp.einsum('bqhd,bkhd->bhqk', queries, key_heads, precision=highest) * head_size ** (-0.5)
    if allowed is not None:
        scores = jnp.where(allowed[:, None], scores, -1000000000.0)
    weights = low(jax.nn.softmax(low_back(scores), axis=-1))
    merged = jnp.einsum('bhqk,bkhd->bqhd', weights, value_heads, precision=highest)
    return low(low_back(merged.reshape(batch_size, length, triple // 3)))

def block(inputs, allowed, norm_gain, shifts, hidden_bias, qkv_weight, out_weight, up_weight, down_weight, head_count, head_size):
    first_low = low(normed(inputs, norm_gain[0], shifts[0]))
    qkv_bias = jnp.concatenate([shifts[2], jnp.zeros_like(shifts[2]), shifts[3]])
    mixed = low(low_back(project(first_low, qkv_weight) + qkv_bias))
    attended = attend(mixed, allowed, head_count, head_size)
    middle = inputs + low_back(project(attended, out_weight) + shifts[4])
    second_low = low(normed(middle, norm_gain[1], shifts[1]))
    hidden = low(jax.nn.gelu(low_back(project(second_low, up_weight) + hidden_bias), approximate=False))
    return middle + low_back(project(hidden, down_weight) + shifts[5])

def forward(patches, enc_gain, enc_shift, enc_hidden, enc_qkv, enc_out, enc_up, enc_down, embedding, mask_token, dec_gain, dec_shift, dec_hidden, dec_qkv, dec_out, dec_up, dec_down, segments, send_slot, visible):
    device_count = N_DP * N_FSDP
    enc_inputs = patches.reshape(device_count, SEQS_DEV, SEQ_LEN, ENC_WIDTH)
    seg_marks = segments.reshape(device_count, SEQS_DEV, SEQ_LEN)

    def encode(operand):
        block_in, marks_one = operand
        allowed = marks_one[:, :, None] == marks_one[:, None, :]
        return block(block_in, allowed, enc_gain, enc_shift, enc_hidden, enc_qkv, enc_out, enc_up, enc_down, ENC_HEADS, ENC_HEAD)
    encoded = lax.map(jax.checkpoint(encode), (enc_inputs, seg_marks))
    sent = low(low_back(encoded.reshape(ROWS, ENC_WIDTH)))
    per_peer = IMG_DEV // N_DP
    local_marks = segments.reshape(device_count, ROWS_DEV)
    row_ids = jnp.arange(ROWS_DEV, dtype=jnp.int32)
    image_ids = jnp.arange(IMG_DEV, dtype=jnp.int32)
    starts = lax.optimization_barrier(jnp.min(jnp.where(local_marks[:, None, :] == image_ids[None, :, None], row_ids[None, None, :], ROWS_DEV), axis=2)).astype(jnp.int32)
    device_ids = jnp.arange(device_count, dtype=jnp.int32)
    owner_device = send_slot // per_peer * N_FSDP + (device_ids % N_FSDP)[:, None]
    owner_slot = (device_ids // N_FSDP)[:, None] * per_peer + send_slot % per_peer
    owner_image = (owner_device * IMG_DEV + owner_slot).reshape(device_count * IMG_DEV).astype(jnp.int32)
    source_rows = (device_ids[:, None, None] * ROWS_DEV + starts[:, :, None] + jnp.arange(VISIBLE, dtype=jnp.int32)[None, None, :]).reshape(device_count * IMG_DEV, VISIBLE).astype(jnp.int32)
    arrival = jnp.zeros((IMAGES, VISIBLE), jnp.int32).at[owner_image].set(source_rows)
    received = sent[arrival]
    embedded = low_back(project(received, embedding) + dec_shift[0])
    matches = visible[:, :, None] == jnp.arange(PATCHES, dtype=jnp.int32)[None, None, :]
    present = jnp.any(matches, axis=1)
    slot_index = lax.optimization_barrier(jnp.sum(jnp.where(matches, jnp.arange(VISIBLE, dtype=jnp.int32)[None, :, None], 0), axis=1)).astype(jnp.int32)
    spread = jnp.take_along_axis(embedded, slot_index[:, :, None], axis=1)
    dec_inputs = jnp.where(present[:, :, None], spread, mask_token) + position_table(SIDE, DEC_WIDTH)
    image_groups = dec_inputs.reshape(device_count, IMG_DEV, PATCHES, DEC_WIDTH)

    def decode(image_group):
        return block(image_group, None, dec_gain, dec_shift[1:], dec_hidden, dec_qkv, dec_out, dec_up, dec_down, DEC_HEADS, DEC_HEAD)
    decoded = lax.map(jax.checkpoint(decode), image_groups)
    return decoded.reshape(DEC_ROWS, DEC_WIDTH)

def reference(patches, segments, send_slot, visible, enc_gain, enc_shift, enc_hidden, enc_qkv, enc_out, enc_up, enc_down, embedding, mask_token, dec_gain, dec_shift, dec_hidden, dec_qkv, dec_out, dec_up, dec_down, cotangent):
    floats = tuple((member.astype(jnp.float32) for member in (patches, enc_gain, enc_shift, enc_hidden, enc_qkv, enc_out, enc_up, enc_down, embedding, mask_token, dec_gain, dec_shift, dec_hidden, dec_qkv, dec_out, dec_up, dec_down)))

    def wrapped(*parameters):
        return forward(*parameters, segments, send_slot, visible)
    decoded, pullback = jax.vjp(wrapped, *floats)
    gradients = pullback(cotangent.astype(jnp.float32))
    return (decoded.astype(jnp.bfloat16), gradients[0], gradients[1], gradients[2], gradients[3], gradients[4], gradients[5], gradients[6], gradients[7], gradients[8], gradients[9], gradients[10], gradients[11], gradients[12], gradients[13], gradients[14], gradients[15], gradients[16])
```

```python
import math

import jax
import jax.numpy as jnp
import numpy as np
from jax import lax
from jax.experimental import pallas as pl
from jax.experimental.pallas import tpu as pltpu
from jax.sharding import PartitionSpec as P

ENC_HEAD = 64
DEC_HEAD = 32
SIDE = 14
VISIBLE = 49
ROWS_DEV = 1024
IMG_DEV = 16
EW = 768
DW = 512
PATCHES = 196
RP = 208
ENC_GROUPS = 4
ENC_CHUNKS = 4
DEC_CHUNKS = 4
NEG = -1e30
F32 = jnp.float32
BF16 = jnp.bfloat16
BOTH = ("dp", "fsdp")
EPS = 1e-06

ERF_P = 0.44
ERF_C = (
    0.2482209555836147,
    0.2488711484441078,
    0.21731375919172816,
    0.21581153367593472,
    -0.020179333598664445,
    0.2966860302544493,
    -0.2779471828654498,
    0.07122327097163224,
)


def nn(a, b):
    return lax.dot_general(a, b, (((1,), (0,)), ((), ())), preferred_element_type=F32)


def nt(a, b):
    return lax.dot_general(a, b, (((1,), (1,)), ((), ())), preferred_element_type=F32)


def colsum(v):
    return jnp.sum(v, axis=0, keepdims=True)


def gelu_both(u):
    x = jnp.abs(u) * (1.0 / math.sqrt(2.0))
    t = 1.0 / (1.0 + ERF_P * x)
    r = jnp.full_like(t, ERF_C[-1])
    for coef in ERF_C[-2::-1]:
        r = r * t + coef
    e = jnp.exp(-(x * x))
    half = (0.5 * r) * (t * e)
    cdf = jnp.where(u >= 0, 1.0 - half, half)
    return u * cdf, cdf + u * (e * (1.0 / math.sqrt(2.0 * math.pi)))


def norm_stats(x):
    center = x - jnp.mean(x, axis=-1, keepdims=True)
    rstd = lax.rsqrt(jnp.mean(center * center, axis=-1, keepdims=True) + EPS)
    return center * rstd, rstd


def norm_back(xhat, rstd, gain, gy):
    d = gy * gain
    m1 = jnp.mean(d, axis=-1, keepdims=True)
    m2 = jnp.mean(d * xhat, axis=-1, keepdims=True)
    return rstd * (d - m1 - xhat * m2)


def lane_mask(shape, h, hd):
    lanes = lax.broadcasted_iota(jnp.int32, shape, 1)
    return (lanes >= h * hd) & (lanes < (h + 1) * hd)


def attend_fwd(q, k, v, hd, bias, pt_store):
    vt = jnp.transpose(v)
    outs = []
    zero = jnp.zeros_like(q)
    for h in range(128 // hd):
        qh = jnp.where(lane_mask(q.shape, h, hd), q, zero)
        st = bias(nt(k, qh))
        peak = jnp.max(st, axis=0, keepdims=True)
        e = jnp.exp((st - peak) * hd ** (-0.5))
        inv = 1.0 / jnp.sum(e, axis=0, keepdims=True)
        pt = (e * inv).astype(BF16)
        pt_store(h, pt)
        outs.append(nn(vt[h * hd : (h + 1) * hd], pt))
    return jnp.concatenate(outs, axis=0)


def attend_bwd(q, k, v, go, hd, pt_load):
    kt = jnp.transpose(k)
    zero = jnp.zeros_like(q)
    scale = hd ** (-0.5)
    gqt = []
    gk = gv = None
    for h in range(128 // hd):
        mask = lane_mask(q.shape, h, hd)
        qh = jnp.where(mask, q, zero)
        goh = jnp.where(mask, go, zero)
        pt = pt_load(h)
        gpt = nt(v, goh)
        p32 = pt.astype(F32)
        dot = jnp.sum(p32 * gpt, axis=0, keepdims=True)
        gst = (p32 * (gpt - dot)).astype(BF16)
        gvh = nn(pt, goh)
        gkh = nn(gst, qh)
        gv = gvh if gv is None else gv + gvh
        gk = gkh if gk is None else gk + gkh
        gqt.append(nn(kt[h * hd : (h + 1) * hd], gst))
    gq = jnp.transpose(jnp.concatenate(gqt, axis=0)) * scale
    return gq.astype(BF16), (gk * scale).astype(BF16), gv.astype(BF16)


D_IMGS = 2
DM = D_IMGS * RP
D_HG = DW // 128
D_HPG = 128 // DEC_HEAD


def dec_bias(st):
    head = st[: RP - 16]
    tail = st[RP - 16 :]
    keys = lax.broadcasted_iota(jnp.int32, tail.shape, 0) + (RP - 16)
    return jnp.concatenate([head, jnp.where(keys < PATCHES, tail, NEG)], axis=0)


def dec_kernel(
    recv_ref,
    visr_ref,
    visc_ref,
    cot_ref,
    pos_ref,
    par_ref,
    hid_ref,
    wq_ref,
    wk_ref,
    wv_ref,
    wo_ref,
    wup_ref,
    wdn_ref,
    emb_ref,
    out_ref,
    gyl_ref,
    gq_o,
    gk_o,
    gv_o,
    go_o,
    gup_o,
    gdn_o,
    gemb_o,
    small_o,
    ghid_o,
    xd_s,
    x2_s,
    y_s,
    ga_s,
    flat_s,
    q_s,
    k_s,
    v_s,
    o_s,
    ot_s,
    pt_s,
    a1_s,
    a1t_s,
    a2_s,
    a2t_s,
    gm_s,
    gmt_s,
    go_s,
    gq_s,
    gk_s,
    gv_s,
    aq,
    ak,
    av,
    ao,
    aup,
    adt,
    aemb,
):
    step = pl.program_id(0)
    last = pl.num_programs(0) - 1

    @pl.when(step == 0)
    def _():
        for ref in (aq, ak, av, ao, aup, adt, aemb, small_o, ghid_o):
            ref[...] = jnp.zeros_like(ref)
        flat_s[...] = jnp.zeros_like(flat_s)

    mask_tok = par_ref[0:1]
    gain1, gain2 = par_ref[1:2], par_ref[2:3]
    sh_emb, sh1, sh2 = par_ref[3:4], par_ref[4:5], par_ref[5:6]
    sh_q, sh_v, sh_o, sh_d = par_ref[6:7], par_ref[7:8], par_ref[8:9], par_ref[9:10]

    for i in range(D_IMGS):
        cells = lax.broadcasted_iota(jnp.int32, (RP, VISIBLE), 0)
        hot = visr_ref[i] == cells
        present = jnp.max(jnp.where(hot, 1.0, 0.0), axis=1, keepdims=True)
        placed = nn(jnp.where(hot, 1.0, 0.0).astype(BF16), recv_ref[i]).astype(BF16)
        z = nn(placed, emb_ref[...]) + sh_emb
        xd_s[pl.ds(i * RP, RP), :] = jnp.where(present > 0.5, z, mask_tok) + pos_ref[...]

    xhat1, rstd1 = norm_stats(xd_s[...])
    a1 = (xhat1 * gain1 + sh1).astype(BF16)
    a1_s[...] = a1
    for w_ref, bias, dst in ((wq_ref, sh_q, q_s), (wk_ref, None, k_s), (wv_ref, sh_v, v_s)):
        val = nn(a1, w_ref[...])
        val = (val if bias is None else val + bias).astype(BF16)
        for i in range(D_IMGS):
            for g in range(D_HG):
                dst[i * D_HG + g] = val[i * RP : (i + 1) * RP, g * 128 : (g + 1) * 128]
    a1t_s[...] = jnp.transpose(a1_s[...])

    def fwd_body(j, carry):
        def store(h, pt):
            pt_s[j * D_HPG + h] = pt

        ot = attend_fwd(q_s[j], k_s[j], v_s[j], DEC_HEAD, dec_bias, store)
        ot_s[j] = ot.astype(BF16)
        o_s[j] = jnp.transpose(ot).astype(BF16)
        return carry

    lax.fori_loop(0, D_IMGS * D_HG, fwd_body, 0)

    o_full = jnp.concatenate(
        [
            jnp.concatenate([o_s[i * D_HG + g] for g in range(D_HG)], axis=1)
            for i in range(D_IMGS)
        ],
        axis=0,
    )
    x2_s[...] = xd_s[...] + (nn(o_full, wo_ref[...]) + sh_o)
    xhat2, rstd2 = norm_stats(x2_s[...])
    a2 = (xhat2 * gain2 + sh2).astype(BF16)
    a2_s[...] = a2
    a2t_s[...] = jnp.transpose(a2_s[...])

    flat_s[pl.ds(0, D_IMGS * PATCHES), :] = cot_ref[...].astype(F32)
    rows = lax.broadcasted_iota(jnp.int32, (RP, DW), 0)
    for i in range(D_IMGS):
        part = flat_s[pl.ds(i * PATCHES, RP), :]
        gm_s[pl.ds(i * RP, RP), :] = jnp.where(rows < PATCHES, part, 0.0).astype(BF16)
    gmt_s[...] = jnp.transpose(gm_s[...])
    small_o[pl.ds(9, 1), :] += colsum(gm_s[...].astype(F32))

    y_s[...] = x2_s[...] + sh_d
    ga_s[...] = jnp.zeros_like(ga_s)

    def mlp_body(c, carry):
        wup = wup_ref[c]
        wdn = wdn_ref[c]
        u = nn(a2_s[...], wup) + hid_ref[c]
        hid, dgelu = gelu_both(u)
        hid = hid.astype(BF16)
        y_s[...] += nn(hid, wdn)
        gu = (nt(gm_s[...], wdn) * dgelu).astype(BF16)
        ga_s[...] += nt(gu, wup)
        adt[c] += nn(gmt_s[...], hid)
        aup[c] += nn(a2t_s[...], gu)
        ghid_o[c] += colsum(gu.astype(F32))
        return carry

    lax.fori_loop(0, DEC_CHUNKS, mlp_body, 0)

    for i in range(D_IMGS):
        flat_s[pl.ds(i * PATCHES, PATCHES), :] = y_s[pl.ds(i * RP, PATCHES), :]
    out_ref[...] = flat_s[pl.ds(0, D_IMGS * PATCHES), :].astype(BF16)

    ga2 = ga_s[...]
    xhat2, rstd2 = norm_stats(x2_s[...])
    small_o[pl.ds(2, 1), :] += colsum(ga2 * xhat2)
    small_o[pl.ds(5, 1), :] += colsum(ga2)
    gx2 = gm_s[...].astype(F32) + norm_back(xhat2, rstd2, gain2, ga2)
    x2_s[...] = gx2
    gpr = gx2.astype(BF16)
    small_o[pl.ds(8, 1), :] += colsum(gpr.astype(F32))
    go = nt(gpr, wo_ref[...]).astype(BF16)
    for i in range(D_IMGS):
        part = gpr[i * RP : (i + 1) * RP]
        for g in range(D_HG):
            j = i * D_HG + g
            ao[pl.ds(g * 128, 128), :] += nn(ot_s[j], part)
            go_s[j] = go[i * RP : (i + 1) * RP, g * 128 : (g + 1) * 128]

    def bwd_body(j, carry):
        gq, gk, gv = attend_bwd(
            q_s[j], k_s[j], v_s[j], go_s[j], DEC_HEAD, lambda h: pt_s[j * D_HPG + h]
        )
        gq_s[j] = gq
        gk_s[j] = gk
        gv_s[j] = gv
        return carry

    lax.fori_loop(0, D_IMGS * D_HG, bwd_body, 0)

    ga1 = None
    for src, w_ref, acc, row in ((gq_s, wq_ref, aq, 6), (gk_s, wk_ref, ak, None), (gv_s, wv_ref, av, 7)):
        full = jnp.concatenate(
            [
                jnp.concatenate([src[i * D_HG + g] for g in range(D_HG)], axis=1)
                for i in range(D_IMGS)
            ],
            axis=0,
        )
        if row is not None:
            small_o[pl.ds(row, 1), :] += colsum(full.astype(F32))
        acc[...] += nn(a1t_s[...], full)
        part = nt(full, w_ref[...])
        ga1 = part if ga1 is None else ga1 + part

    xhat1, rstd1 = norm_stats(xd_s[...])
    small_o[pl.ds(1, 1), :] += colsum(ga1 * xhat1)
    small_o[pl.ds(4, 1), :] += colsum(ga1)
    y_s[...] = x2_s[...] + norm_back(xhat1, rstd1, gain1, ga1)

    for i in range(D_IMGS):
        gx = y_s[pl.ds(i * RP, RP), :]
        cells = lax.broadcasted_iota(jnp.int32, (RP, VISIBLE), 0)
        hot = visr_ref[i] == cells
        present = jnp.max(jnp.where(hot, 1.0, 0.0), axis=1, keepdims=True)
        small_o[pl.ds(0, 1), :] += colsum(jnp.where(present > 0.5, 0.0, gx))
        cells_t = lax.broadcasted_iota(jnp.int32, (64, RP), 1)
        hot_t = jnp.where(visc_ref[i] == cells_t, 1.0, 0.0).astype(BF16)
        gz = nn(hot_t, gx.astype(BF16)).astype(BF16)
        small_o[pl.ds(3, 1), :] += colsum(gz.astype(F32))
        aemb[...] += lax.dot_general(
            recv_ref[i], gz[:VISIBLE], (((0,), (0,)), ((), ())), preferred_element_type=F32
        )
        gyl_ref[i] = nt(gz, emb_ref[...])[:VISIBLE].astype(BF16)

    @pl.when(step == last)
    def _():
        gq_o[...] = aq[...].astype(BF16)
        gk_o[...] = ak[...].astype(BF16)
        gv_o[...] = av[...].astype(BF16)
        go_o[...] = ao[...].astype(BF16)
        gup_o[...] = aup[...].astype(BF16)
        for c in range(DEC_CHUNKS):
            gdn_o[c] = jnp.transpose(adt[c]).astype(BF16)
        gemb_o[...] = aemb[...].astype(BF16)


def whole(shape):
    zeros = (0,) * len(shape)
    return pl.BlockSpec(shape, lambda *_: zeros, pipeline_mode=pl.Buffered(1))


def decoder(recv, visible, cot, pos, par, hid, wq, wk, wv, wo, wup, wdn, emb):
    images = recv.shape[0]
    visr = visible.reshape(images, 1, VISIBLE)
    visc = jnp.pad(visible, ((0, 0), (0, 64 - VISIBLE)), constant_values=-1).reshape(images, 64, 1)
    f, b = F32, BF16
    vm = pltpu.VMEM
    grp = D_IMGS * D_HG
    ins = [
        pl.BlockSpec((D_IMGS, VISIBLE, EW), lambda i: (i, 0, 0)),
        pl.BlockSpec((D_IMGS, 1, VISIBLE), lambda i: (i, 0, 0)),
        pl.BlockSpec((D_IMGS, 64, 1), lambda i: (i, 0, 0)),
        pl.BlockSpec((D_IMGS * PATCHES, DW), lambda i: (i, 0)),
    ] + [whole(a.shape) for a in (pos, par, hid, wq, wk, wv, wo, wup, wdn, emb)]
    square = jax.ShapeDtypeStruct((DW, DW), b)
    chunked = jax.ShapeDtypeStruct((DEC_CHUNKS, DW, DW), b)
    outs = [
        jax.ShapeDtypeStruct((images * PATCHES, DW), b),
        jax.ShapeDtypeStruct((images, VISIBLE, EW), b),
        square,
        square,
        square,
        square,
        chunked,
        chunked,
        jax.ShapeDtypeStruct((EW, DW), b),
        jax.ShapeDtypeStruct((16, DW), f),
        jax.ShapeDtypeStruct((DEC_CHUNKS, 1, DW), f),
    ]
    out_specs = [
        pl.BlockSpec((D_IMGS * PATCHES, DW), lambda i: (i, 0)),
        pl.BlockSpec((D_IMGS, VISIBLE, EW), lambda i: (i, 0, 0)),
    ] + [whole(o.shape) for o in outs[2:]]
    scratch = [
        vm((DM, DW), f),
        vm((DM, DW), f),
        vm((DM, DW), f),
        vm((DM, DW), f),
        vm((D_IMGS * PATCHES + 24, DW), f),
        vm((grp, RP, 128), b),
        vm((grp, RP, 128), b),
        vm((grp, RP, 128), b),
        vm((grp, RP, 128), b),
        vm((grp, 128, RP), b),
        vm((grp * D_HPG, RP, RP), b),
        vm((DM, DW), b),
        vm((DW, DM), b),
        vm((DM, DW), b),
        vm((DW, DM), b),
        vm((DM, DW), b),
        vm((DW, DM), b),
        vm((grp, RP, 128), b),
        vm((grp, RP, 128), b),
        vm((grp, RP, 128), b),
        vm((grp, RP, 128), b),
        vm((DW, DW), f),
        vm((DW, DW), f),
        vm((DW, DW), f),
        vm((DW, DW), f),
        vm((DEC_CHUNKS, DW, DW), f),
        vm((DEC_CHUNKS, DW, DW), f),
        vm((EW, DW), f),
    ]
    return pl.pallas_call(
        dec_kernel,
        grid=(images // D_IMGS,),
        in_specs=ins,
        out_specs=out_specs,
        out_shape=outs,
        scratch_shapes=scratch,
        compiler_params=pltpu.CompilerParams(
            dimension_semantics=("arbitrary",), vmem_limit_bytes=60 << 20
        ),
        name="decoder",
    )(recv, visr, visc, cot, pos, par, hid, wq, wk, wv, wo, wup, wdn, emb)


EM = ENC_GROUPS * RP
E_HB = 3
E_J = ENC_GROUPS * 2
E_HPG = 128 // ENC_HEAD
GROUP_IMGS = IMG_DEV // ENC_GROUPS
WIN = 56


def seg_of(i):
    return (
        jnp.where(i >= VISIBLE, 1, 0)
        + jnp.where(i >= 2 * VISIBLE, 1, 0)
        + jnp.where(i >= 3 * VISIBLE, 1, 0)
        + jnp.where(i >= 4 * VISIBLE, 1, 0)
    )


def enc_attn_kernel(
    start_ref,
    x_ref,
    par_ref,
    parb_ref,
    wq_ref,
    wk_ref,
    wv_ref,
    wo_ref,
    xc_o,
    q_o,
    k_o,
    v_o,
    pt_o,
    ot_o,
    x2_o,
    xf_s,
    xc_s,
    a1_s,
    o_s,
    bias_s,
):
    step = pl.program_id(0)

    @pl.when(step == 0)
    def _():
        xf_s[pl.ds(0, ROWS_DEV), :] = x_ref[...].astype(F32)
        for grp in range(ENC_GROUPS):
            xc_s[pl.ds(grp * RP + PATCHES, RP - PATCHES), :] = jnp.zeros((RP - PATCHES, EW), F32)
            for i in range(GROUP_IMGS):
                start = start_ref[grp * GROUP_IMGS + i]
                shift = lax.rem(start, 8)
                base = pl.multiple_of(start - shift, 8)
                part = pltpu.roll(xf_s[pl.ds(base, WIN), :], WIN - shift, 0)
                xc_s[pl.ds(grp * RP + i * VISIBLE, VISIBLE), :] = part[:VISIBLE]
        x = xc_s[...]
        xc_o[...] = x.astype(BF16)
        xhat, _ = norm_stats(x)
        a1_s[...] = (xhat * par_ref[0:1] + par_ref[2:3]).astype(BF16)
        x2_o[...] = x + par_ref[6:7]
        keys = lax.broadcasted_iota(jnp.int32, (RP, RP), 0)
        queries = lax.broadcasted_iota(jnp.int32, (RP, RP), 1)
        same = (seg_of(keys) == seg_of(queries)) & (keys < PATCHES)
        bias_s[...] = jnp.where(same, 0.0, NEG)

    for w_ref, row, dst in ((wq_ref, 4, q_o), (wk_ref, None, k_o), (wv_ref, 5, v_o)):
        val = nn(a1_s[...], w_ref[...])
        if row is not None:
            val = val + parb_ref[row : row + 1]
        val = val.astype(BF16)
        for grp in range(ENC_GROUPS):
            for half in range(2):
                dst[0, grp * 2 + half] = val[
                    grp * RP : (grp + 1) * RP, half * 128 : (half + 1) * 128
                ]

    def loop(j, carry):
        def store(h, pt):
            pt_o[0, j * E_HPG + h] = pt

        ot = attend_fwd(
            q_o[0, j], k_o[0, j], v_o[0, j], ENC_HEAD, lambda st: st + bias_s[...], store
        )
        ot_o[0, j] = ot.astype(BF16)
        o_s[j] = jnp.transpose(ot).astype(BF16)
        return carry

    lax.fori_loop(0, E_J, loop, 0)
    o_full = jnp.concatenate(
        [
            jnp.concatenate([o_s[grp * 2], o_s[grp * 2 + 1]], axis=1)
            for grp in range(ENC_GROUPS)
        ],
        axis=0,
    )
    x2_o[...] += nn(o_full, wo_ref[...])


def enc_attn(starts, x, par, wq, wk, wv, wo):
    f, b = F32, BF16
    vm = pltpu.VMEM
    col = pl.BlockSpec((EW, 256), lambda i, s: (0, i))
    row = pl.BlockSpec((256, EW), lambda i, s: (i, 0))
    grp = pl.BlockSpec((1, E_J, RP, 128), lambda i, s: (i, 0, 0, 0))
    outs = [
        (jax.ShapeDtypeStruct((EM, EW), b), whole((EM, EW))),
        (jax.ShapeDtypeStruct((E_HB, E_J, RP, 128), b), grp),
        (jax.ShapeDtypeStruct((E_HB, E_J, RP, 128), b), grp),
        (jax.ShapeDtypeStruct((E_HB, E_J, RP, 128), b), grp),
        (
            jax.ShapeDtypeStruct((E_HB, E_J * E_HPG, RP, RP), b),
            pl.BlockSpec((1, E_J * E_HPG, RP, RP), lambda i, s: (i, 0, 0, 0)),
        ),
        (
            jax.ShapeDtypeStruct((E_HB, E_J, 128, RP), b),
            pl.BlockSpec((1, E_J, 128, RP), lambda i, s: (i, 0, 0, 0)),
        ),
        (jax.ShapeDtypeStruct((EM, EW), f), whole((EM, EW))),
    ]
    return pl.pallas_call(
        enc_attn_kernel,
        grid_spec=pltpu.PrefetchScalarGridSpec(
            num_scalar_prefetch=1,
            grid=(E_HB,),
            in_specs=[
                whole(x.shape),
                whole(par.shape),
                pl.BlockSpec((8, 256), lambda i, s: (0, i)),
                col,
                col,
                col,
                row,
            ],
            out_specs=[o[1] for o in outs],
            scratch_shapes=[
                vm((ROWS_DEV + 16, EW), f),
                vm((EM, EW), f),
                vm((EM, EW), b),
                vm((E_J, RP, 128), b),
                vm((RP, RP), f),
            ],
        ),
        out_shape=[o[0] for o in outs],
        compiler_params=pltpu.CompilerParams(
            dimension_semantics=("arbitrary",), vmem_limit_bytes=60 << 20
        ),
        name="enc_attn",
    )(starts, x, par, par, wq, wk, wv, wo)


def enc_mlp_kernel(
    x2_ref, par_ref, hid_ref, wup_ref, wdn_ref, yl_o, hid_o, dg_o, a2_s, y_s
):
    step = pl.program_id(0)

    @pl.when(step == 0)
    def _():
        x2 = x2_ref[...]
        xhat, _ = norm_stats(x2)
        a2_s[...] = (xhat * par_ref[1:2] + par_ref[3:4]).astype(BF16)
        y_s[...] = x2 + par_ref[7:8]

    u = nn(a2_s[...], wup_ref[0]) + hid_ref[0]
    hid, dgelu = gelu_both(u)
    hid = hid.astype(BF16)
    hid_o[0] = hid
    dg_o[0] = dgelu.astype(BF16)
    y_s[...] += nn(hid, wdn_ref[0])

    @pl.when(step == pl.num_programs(0) - 1)
    def _():
        for grp in range(ENC_GROUPS):
            for i in range(GROUP_IMGS):
                part = y_s[pl.ds(grp * RP + i * VISIBLE, VISIBLE), :]
                yl_o[grp * GROUP_IMGS + i] = part.astype(BF16)


def enc_mlp(x2, par, hid, wup, wdn):
    f, b = F32, BF16
    chunk = pl.BlockSpec((1, EM, EW), lambda i: (i, 0, 0))
    wchunk = pl.BlockSpec((1, EW, EW), lambda i: (i, 0, 0))
    outs = [
        (jax.ShapeDtypeStruct((IMG_DEV, VISIBLE, EW), b), whole((IMG_DEV, VISIBLE, EW))),
        (jax.ShapeDtypeStruct((ENC_CHUNKS, EM, EW), b), chunk),
        (jax.ShapeDtypeStruct((ENC_CHUNKS, EM, EW), b), chunk),
    ]
    return pl.pallas_call(
        enc_mlp_kernel,
        grid=(ENC_CHUNKS,),
        in_specs=[
            whole(x2.shape),
            whole(par.shape),
            pl.BlockSpec((1, 1, EW), lambda i: (i, 0, 0)),
            wchunk,
            wchunk,
        ],
        out_specs=[o[1] for o in outs],
        out_shape=[o[0] for o in outs],
        scratch_shapes=[pltpu.VMEM((EM, EW), b), pltpu.VMEM((EM, EW), f)],
        compiler_params=pltpu.CompilerParams(
            dimension_semantics=("arbitrary",), vmem_limit_bytes=60 << 20
        ),
        name="enc_mlp",
    )(x2, par, hid, wup, wdn)


def enc_mlp_back_kernel(
    gy_ref,
    x2_ref,
    par_ref,
    hid_ref,
    dg_ref,
    wup_ref,
    wdn_ref,
    gx2_o,
    gup_o,
    gdn_o,
    small_o,
    ghid_o,
    gf_s,
    gm_s,
    a2t_s,
    ga_s,
):
    step = pl.program_id(0)

    @pl.when(step == 0)
    def _():
        for grp in range(ENC_GROUPS):
            gf_s[pl.ds(grp * RP + PATCHES, RP - PATCHES), :] = jnp.zeros((RP - PATCHES, EW), F32)
            for i in range(GROUP_IMGS):
                part = gy_ref[grp * GROUP_IMGS + i].astype(F32)
                gf_s[pl.ds(grp * RP + i * VISIBLE, VISIBLE), :] = part
        gm_s[...] = gf_s[...].astype(BF16)
        xhat, _ = norm_stats(x2_ref[...])
        a2 = (xhat * par_ref[1:2] + par_ref[3:4]).astype(BF16)
        a2t_s[...] = jnp.transpose(a2)
        ga_s[...] = jnp.zeros_like(ga_s)
        small_o[...] = jnp.zeros_like(small_o)
        small_o[pl.ds(7, 1), :] = colsum(gf_s[...])

    gu = (nt(gm_s[...], wdn_ref[0]) * dg_ref[0].astype(F32)).astype(BF16)
    ga_s[...] += nt(gu, wup_ref[0])
    gup_o[0] = nn(a2t_s[...], gu).astype(BF16)
    gdn_o[0] = nn(jnp.transpose(hid_ref[0]), gm_s[...]).astype(BF16)
    ghid_o[0] = colsum(gu.astype(F32))

    @pl.when(step == pl.num_programs(0) - 1)
    def _():
        ga2 = ga_s[...]
        xhat, rstd = norm_stats(x2_ref[...])
        small_o[pl.ds(1, 1), :] = colsum(ga2 * xhat)
        small_o[pl.ds(3, 1), :] = colsum(ga2)
        gx2 = gf_s[...] + norm_back(xhat, rstd, par_ref[1:2], ga2)
        gx2_o[...] = gx2
        small_o[pl.ds(6, 1), :] = colsum(gx2.astype(BF16).astype(F32))


def enc_mlp_back(gy, x2, par, hid, dg, wup, wdn):
    f, b = F32, BF16
    chunk = pl.BlockSpec((1, EM, EW), lambda i: (i, 0, 0))
    wchunk = pl.BlockSpec((1, EW, EW), lambda i: (i, 0, 0))
    outs = [
        (jax.ShapeDtypeStruct((EM, EW), f), whole((EM, EW))),
        (jax.ShapeDtypeStruct((ENC_CHUNKS, EW, EW), b), wchunk),
        (jax.ShapeDtypeStruct((ENC_CHUNKS, EW, EW), b), wchunk),
        (jax.ShapeDtypeStruct((8, EW), f), whole((8, EW))),
        (
            jax.ShapeDtypeStruct((ENC_CHUNKS, 1, EW), f),
            pl.BlockSpec((1, 1, EW), lambda i: (i, 0, 0)),
        ),
    ]
    return pl.pallas_call(
        enc_mlp_back_kernel,
        grid=(ENC_CHUNKS,),
        in_specs=[whole(gy.shape), whole(x2.shape), whole(par.shape), chunk, chunk, wchunk, wchunk],
        out_specs=[o[1] for o in outs],
        out_shape=[o[0] for o in outs],
        scratch_shapes=[
            pltpu.VMEM((EM, EW), f),
            pltpu.VMEM((EM, EW), b),
            pltpu.VMEM((EW, EM), b),
            pltpu.VMEM((EM, EW), f),
        ],
        compiler_params=pltpu.CompilerParams(
            dimension_semantics=("arbitrary",), vmem_limit_bytes=60 << 20
        ),
        name="enc_mlp_back",
    )(gy, x2, par, hid, dg, wup, wdn)


def enc_attn_back_kernel(
    start_ref,
    gx2_ref,
    xc_ref,
    par_ref,
    q_ref,
    k_ref,
    v_ref,
    pt_ref,
    ot_ref,
    wq_ref,
    wk_ref,
    wv_ref,
    wo_ref,
    gx_o,
    gwq_o,
    gwk_o,
    gwv_o,
    gwo_o,
    small_o,
    gb_o,
    gpr_s,
    a1t_s,
    ga_s,
    go_s,
    gq_s,
    gk_s,
    gv_s,
    gf_s,
):
    step = pl.program_id(0)

    @pl.when(step == 0)
    def _():
        gpr_s[...] = gx2_ref[...].astype(BF16)
        xhat, _ = norm_stats(xc_ref[...].astype(F32))
        a1 = (xhat * par_ref[0:1] + par_ref[2:3]).astype(BF16)
        a1t_s[...] = jnp.transpose(a1)
        ga_s[...] = jnp.zeros_like(ga_s)
        small_o[...] = jnp.zeros_like(small_o)

    go = nt(gpr_s[...], wo_ref[...]).astype(BF16)
    for half in range(2):
        acc = None
        for grp in range(ENC_GROUPS):
            rows = slice(grp * RP, (grp + 1) * RP)
            go_s[grp * 2 + half] = go[rows, half * 128 : (half + 1) * 128]
            part = nn(ot_ref[0, grp * 2 + half], gpr_s[pl.ds(grp * RP, RP), :])
            acc = part if acc is None else acc + part
        gwo_o[pl.ds(half * 128, 128), :] = acc.astype(BF16)

    def loop(j, carry):
        gq, gk, gv = attend_bwd(
            q_ref[0, j],
            k_ref[0, j],
            v_ref[0, j],
            go_s[j],
            ENC_HEAD,
            lambda h: pt_ref[0, j * E_HPG + h],
        )
        gq_s[j] = gq
        gk_s[j] = gk
        gv_s[j] = gv
        return carry

    lax.fori_loop(0, E_J, loop, 0)
    gb_o[...] = jnp.zeros_like(gb_o)
    ga1 = ga_s[...]
    for src, w_ref, dst, row in (
        (gq_s, wq_ref, gwq_o, 4),
        (gk_s, wk_ref, gwk_o, None),
        (gv_s, wv_ref, gwv_o, 5),
    ):
        full = jnp.concatenate(
            [
                jnp.concatenate([src[grp * 2], src[grp * 2 + 1]], axis=1)
                for grp in range(ENC_GROUPS)
            ],
            axis=0,
        )
        if row is not None:
            gb_o[pl.ds(row, 1), :] = colsum(full.astype(F32))
        dst[...] = nn(a1t_s[...], full).astype(BF16)
        ga1 = ga1 + nt(full, w_ref[...])
    ga_s[...] = ga1

    @pl.when(step == pl.num_programs(0) - 1)
    def _():
        ga = ga_s[...]
        xhat, rstd = norm_stats(xc_ref[...].astype(F32))
        small_o[pl.ds(0, 1), :] = colsum(ga * xhat)
        small_o[pl.ds(2, 1), :] = colsum(ga)
        ga_s[...] = gx2_ref[...] + norm_back(xhat, rstd, par_ref[0:1], ga)
        gf_s[...] = jnp.zeros_like(gf_s)
        rows = lax.broadcasted_iota(jnp.int32, (WIN, EW), 0)
        for grp in range(ENC_GROUPS):
            for i in range(GROUP_IMGS):
                start = start_ref[grp * GROUP_IMGS + i]
                shift = lax.rem(start, 8)
                base = pl.multiple_of(start - shift, 8)
                first = grp * RP + i * VISIBLE
                part = jnp.where(rows < VISIBLE, ga_s[pl.ds(first, WIN), :], 0.0)
                gf_s[pl.ds(base, WIN), :] += pltpu.roll(part, shift, 0)
        gx_o[...] = gf_s[pl.ds(0, ROWS_DEV), :]


def enc_attn_back(starts, gx2, xc, par, q, k, v, pt, ot, wq, wk, wv, wo):
    f, b = F32, BF16
    vm = pltpu.VMEM
    col = pl.BlockSpec((EW, 256), lambda i, s: (0, i))
    row = pl.BlockSpec((256, EW), lambda i, s: (i, 0))
    grp = pl.BlockSpec((1, E_J, RP, 128), lambda i, s: (i, 0, 0, 0))
    square = jax.ShapeDtypeStruct((EW, EW), b)
    outs = [
        (jax.ShapeDtypeStruct((ROWS_DEV, EW), f), whole((ROWS_DEV, EW))),
        (square, col),
        (square, col),
        (square, col),
        (square, row),
        (jax.ShapeDtypeStruct((8, EW), f), whole((8, EW))),
        (jax.ShapeDtypeStruct((8, EW), f), pl.BlockSpec((8, 256), lambda i, s: (0, i))),
    ]
    return pl.pallas_call(
        enc_attn_back_kernel,
        grid_spec=pltpu.PrefetchScalarGridSpec(
            num_scalar_prefetch=1,
            grid=(E_HB,),
            in_specs=[
                whole(gx2.shape),
                whole(xc.shape),
                whole(par.shape),
                grp,
                grp,
                grp,
                pl.BlockSpec((1, E_J * E_HPG, RP, RP), lambda i, s: (i, 0, 0, 0)),
                pl.BlockSpec((1, E_J, 128, RP), lambda i, s: (i, 0, 0, 0)),
                col,
                col,
                col,
                row,
            ],
            out_specs=[o[1] for o in outs],
            scratch_shapes=[
                vm((EM, EW), b),
                vm((EW, EM), b),
                vm((EM, EW), f),
                vm((E_J, RP, 128), b),
                vm((E_J, RP, 128), b),
                vm((E_J, RP, 128), b),
                vm((E_J, RP, 128), b),
                vm((ROWS_DEV + 16, EW), f),
            ],
        ),
        out_shape=[o[0] for o in outs],
        compiler_params=pltpu.CompilerParams(
            dimension_semantics=("arbitrary",), vmem_limit_bytes=60 << 20
        ),
        name="enc_attn_back",
    )(starts, gx2, xc, par, q, k, v, pt, ot, wq, wk, wv, wo)


def position_rows():
    quarter = DW // 4
    frequency = 1.0 / 10000.0 ** (np.arange(quarter) / quarter)
    cells = np.arange(PATCHES)
    by_row = (cells // SIDE)[:, None] * frequency[None, :]
    by_col = (cells % SIDE)[:, None] * frequency[None, :]
    table = np.concatenate([np.sin(by_row), np.cos(by_row), np.sin(by_col), np.cos(by_col)], axis=1)
    return np.pad(table, ((0, RP - PATCHES), (0, 0))).astype(np.float32)


def small_rows(parts, width):
    flat = jnp.concatenate([p.reshape(-1) for p in parts])
    return jnp.pad(flat, (0, 8 * width - flat.shape[0])).reshape(8, width)


def col_blocks(w, width):
    return [w[:, i : i + width] for i in range(0, w.shape[1], width)]


def per_device(v, n):
    rows = v.shape[0]
    return v.reshape(rows, n, -1).transpose(1, 0, 2).reshape(n, -1)


def all_devices(v, rows):
    n = v.shape[0]
    return v.reshape(n, rows, -1).transpose(1, 0, 2).reshape(rows, -1)


def scatter_sum(packed):
    n, rows, width = packed.shape
    flat = packed.reshape(n * rows, width)
    flat = lax.psum_scatter(flat, "dp", scatter_dimension=0, tiled=True)
    return lax.psum_scatter(flat, "fsdp", scatter_dimension=0, tiled=True)


def make_body(n):
    er, dr = EW // n, DW // n

    def gather(v):
        full = lax.all_gather(v, BOTH, axis=0, tiled=True)
        return full.reshape(n, v.shape[0], v.shape[1])

    def body(
        patches,
        segments,
        send_slot,
        visible,
        enc_gain,
        enc_shift,
        enc_hidden,
        enc_qkv,
        enc_out,
        enc_up,
        enc_down,
        embedding,
        mask_token,
        dec_gain,
        dec_shift,
        dec_hidden,
        dec_qkv,
        dec_out,
        dec_up,
        dec_down,
        cotangent,
    ):
        pack_a = jnp.concatenate(
            col_blocks(enc_qkv, EW) + [enc_out, small_rows((enc_gain, enc_shift, enc_hidden), EW)]
        )
        pack_b = jnp.concatenate(col_blocks(enc_up, EW) + [enc_down])
        pack_d = jnp.concatenate(
            col_blocks(dec_qkv, DW)
            + [dec_out]
            + col_blocks(dec_up, DW)
            + [
                dec_down,
                embedding,
                small_rows((mask_token, dec_gain, dec_shift, dec_hidden), DW),
            ]
        )
        full_a = gather(pack_a)
        full_b = gather(pack_b)
        full_d = gather(pack_d)

        wq, wk, wv, wo = [full_a[:, i * er : (i + 1) * er].reshape(EW, EW) for i in range(4)]
        small = full_a[:, 4 * er :].reshape(n, -1).astype(F32)
        par = all_devices(small[:, : 8 * er], 8)
        hid = small[:, 8 * er : 12 * er].reshape(ENC_CHUNKS, 1, EW)
        wup = full_b[:, : 4 * er].reshape(n, 4, er, EW).transpose(1, 0, 2, 3).reshape(4, EW, EW)
        wdn = full_b[:, 4 * er :].reshape(4, EW, EW)

        row_ids = jnp.arange(ROWS_DEV, dtype=jnp.int32)
        image_ids = jnp.arange(IMG_DEV, dtype=jnp.int32)
        starts = jnp.min(
            jnp.where(segments[None, :] == image_ids[:, None], row_ids[None, :], ROWS_DEV), axis=1
        )
        hot = send_slot[0][None, :] == image_ids[:, None]
        slot_starts = jnp.sum(jnp.where(hot, starts[None, :], 0), axis=1).astype(jnp.int32)

        xc, q, k, v, pt, ot, x2 = enc_attn(slot_starts, patches, par, wq, wk, wv, wo)
        outgoing, hidden, dgelu = enc_mlp(x2, par, hid, wup, wdn)
        received = lax.all_to_all(outgoing, "dp", split_axis=0, concat_axis=0, tiled=True)

        dq, dk, dv, do = [full_d[:, i * dr : (i + 1) * dr].reshape(DW, DW) for i in range(4)]
        dup = (
            full_d[:, 4 * dr : 8 * dr]
            .reshape(n, 4, dr, DW)
            .transpose(1, 0, 2, 3)
            .reshape(4, DW, DW)
        )
        ddn = full_d[:, 8 * dr : 12 * dr].reshape(4, DW, DW)
        emb = full_d[:, 12 * dr : 12 * dr + er].reshape(EW, DW)
        dsmall = full_d[:, 12 * dr + er :].reshape(n, -1).astype(F32)
        dpar = jnp.concatenate([all_devices(dsmall[:, : 10 * dr], 10), jnp.zeros((6, DW), F32)])
        dhid = dsmall[:, 10 * dr : 14 * dr].reshape(DEC_CHUNKS, 1, DW)
        pos = jnp.asarray(position_rows())

        decoded, gyl, gdq, gdk, gdv, gdo, gdup, gddn, gemb, gdsmall, gdhid = decoder(
            received, visible, cotangent, pos, dpar, dhid, dq, dk, dv, do, dup, ddn, emb
        )
        returned = lax.all_to_all(gyl, "dp", split_axis=0, concat_axis=0, tiled=True)

        def rows_of(v, width):
            return v.reshape(n, -1, width)

        def small_pack(vals, width):
            flat = jnp.concatenate(vals, axis=1)
            flat = jnp.pad(flat, ((0, 0), (0, 8 * width - flat.shape[1])))
            return flat.astype(BF16).reshape(n, 8, width)

        dsum = scatter_sum(
            jnp.concatenate(
                [rows_of(g, DW) for g in (gdq, gdk, gdv, gdo)]
                + [rows_of(gdup[i], DW) for i in range(4)]
                + [
                    rows_of(gddn, DW),
                    rows_of(gemb, DW),
                    small_pack(
                        [per_device(gdsmall[:10], n), gdhid.reshape(n, -1)],
                        DW,
                    ),
                ],
                axis=1,
            )
        ).astype(F32)

        gx2, gup, gdn, sm1, ghid = enc_mlp_back(returned, x2, par, hidden, dgelu, wup, wdn)
        bsum = scatter_sum(
            jnp.concatenate(
                [rows_of(gup[i], EW) for i in range(4)] + [rows_of(gdn, EW)], axis=1
            )
        ).astype(F32)
        gx, gwq, gwk, gwv, gwo, sm2, gb = enc_attn_back(
            slot_starts, gx2, xc, par, q, k, v, pt, ot, wq, wk, wv, wo
        )
        asum = scatter_sum(
            jnp.concatenate(
                [rows_of(g, EW) for g in (gwq, gwk, gwv, gwo)]
                + [small_pack([per_device(sm1 + sm2 + gb, n), ghid.reshape(n, -1)], EW)],
                axis=1,
            )
        ).astype(F32)

        def cut(v, r, count, first=0):
            return jnp.concatenate(
                [v[(first + i) * r : (first + i + 1) * r] for i in range(count)], axis=1
            )

        esm = asum[4 * er :].reshape(-1)
        dsm = dsum[12 * dr + er :].reshape(-1)
        return (
            decoded,
            gx,
            esm[: 2 * er].reshape(2, er),
            esm[2 * er : 8 * er].reshape(6, er),
            esm[8 * er : 12 * er],
            cut(asum, er, 3),
            asum[3 * er : 4 * er],
            cut(bsum, er, 4),
            bsum[4 * er :],
            dsum[12 * dr : 12 * dr + er],
            dsm[:dr],
            dsm[dr : 3 * dr].reshape(2, dr),
            dsm[3 * dr : 10 * dr].reshape(7, dr),
            dsm[10 * dr : 14 * dr],
            cut(dsum, dr, 3),
            dsum[3 * dr : 4 * dr],
            cut(dsum, dr, 4, 4),
            dsum[8 * dr : 12 * dr],
        )

    return body


def solution(mesh):
    n = mesh.shape["dp"] * mesh.shape["fsdp"]
    rows, vec, cols = P(BOTH, None), P(BOTH), P(None, BOTH)
    return jax.shard_map(
        make_body(n),
        mesh=mesh,
        in_specs=(rows, vec, rows, rows, cols, cols, vec, rows, rows, rows, rows)
        + (rows, vec, cols, cols, vec, rows, rows, rows, rows, rows),
        out_specs=(rows, rows, cols, cols, vec, rows, rows, rows, rows)
        + (rows, vec, cols, cols, vec, rows, rows, rows, rows),
        check_vma=False,
    )
```

```python
import math

import jax
import jax.numpy as jnp
import numpy as np
from jax import lax
from jax.experimental import pallas as pl
from jax.experimental.pallas import tpu as pltpu
from jax.sharding import PartitionSpec as P

ENC_HEAD = 64
DEC_HEAD = 32
SIDE = 14
VISIBLE = 49
ROWS_DEV = 1024
IMG_DEV = 16
EW = 768
DW = 512
PATCHES = 196
RP = 208
ENC_GROUPS = 4
ENC_CHUNKS = 4
DEC_CHUNKS = 4
NEG = -1e30
F32 = jnp.float32
BF16 = jnp.bfloat16
BOTH = ("dp", "fsdp")
EPS = 1e-06

ERF_P = 0.44
ERF_C = (
    0.2482209555836147,
    0.2488711484441078,
    0.21731375919172816,
    0.21581153367593472,
    -0.020179333598664445,
    0.2966860302544493,
    -0.2779471828654498,
    0.07122327097163224,
)


def nn(a, b):
    return lax.dot_general(a, b, (((1,), (0,)), ((), ())), preferred_element_type=F32)


def nt(a, b):
    return lax.dot_general(a, b, (((1,), (1,)), ((), ())), preferred_element_type=F32)


def colsum(v):
    return jnp.sum(v, axis=0, keepdims=True)


def gelu_both(u):
    t = 1.0 / (1.0 + (ERF_P / math.sqrt(2.0)) * jnp.abs(u))
    r = jnp.full_like(t, 0.5 * ERF_C[-1])
    for coef in ERF_C[-2::-1]:
        r = r * t + 0.5 * coef
    e = jnp.exp2((u * u) * (-0.5 * math.log2(math.e)))
    tail = (r * t) * e
    cdf = jnp.where(u >= 0, 1.0 - tail, tail)
    return u * cdf, cdf + (u * (1.0 / math.sqrt(2.0 * math.pi))) * e


def norm_stats(x):
    center = x - jnp.mean(x, axis=-1, keepdims=True)
    rstd = lax.rsqrt(jnp.mean(center * center, axis=-1, keepdims=True) + EPS)
    return center * rstd, rstd


def norm_back(xhat, rstd, gain, gy):
    d = gy * gain
    m1 = jnp.mean(d, axis=-1, keepdims=True)
    m2 = jnp.mean(d * xhat, axis=-1, keepdims=True)
    return rstd * (d - m1 - xhat * m2)


def lane_mask(shape, h, hd):
    lanes = lax.broadcasted_iota(jnp.int32, shape, 1)
    return (lanes >= h * hd) & (lanes < (h + 1) * hd)


def attend_fwd(q, k, v, hd, bias, pt_store):
    vt = jnp.transpose(v)
    heads = 128 // hd
    zero = jnp.zeros_like(q)
    c = hd ** (-0.5) * math.log2(math.e)
    pts = []
    for h in range(heads):
        sh = bias(nt(k, jnp.where(lane_mask(q.shape, h, hd), q, zero)))
        peak = jnp.max(sh, axis=0, keepdims=True)
        e = jnp.exp2((sh - peak) * c)
        inv = 1.0 / jnp.sum(e, axis=0, keepdims=True)
        pt = (e * inv).astype(BF16)
        pt_store(h, pt)
        pts.append(pt)
    outs = [nn(vt[h * hd : (h + 1) * hd], pts[h]) for h in range(heads)]
    return jnp.concatenate(outs, axis=0)


def attend_bwd(q, k, v, go, hd, pt_load):
    kt = jnp.transpose(k)
    heads = 128 // hd
    zero = jnp.zeros_like(q)
    scale = hd ** (-0.5)
    masks = [lane_mask(q.shape, h, hd) for h in range(heads)]
    vst = jnp.concatenate([jnp.where(m, v, zero) for m in masks], axis=0)
    gpt = nt(vst, go)
    gps = [gpt[h * RP : (h + 1) * RP] for h in range(heads)]
    gsts = []
    pts = [pt_load(h) for h in range(heads)]
    for h in range(heads):
        p32 = pts[h].astype(F32)
        dot = jnp.sum(p32 * gps[h], axis=0, keepdims=True)
        gsts.append((p32 * (gps[h] - dot)).astype(BF16))
    gv = gk = None
    for h in range(heads):
        gvh = nn(pts[h], go)
        gv = gvh if gv is None else jnp.where(masks[h], gvh, gv)
    for h in range(heads):
        gkh = nn(gsts[h], q)
        gk = gkh if gk is None else jnp.where(masks[h], gkh, gk)
    gqt = [nn(kt[h * hd : (h + 1) * hd], gsts[h]) for h in range(heads)]
    gq = jnp.transpose(jnp.concatenate(gqt, axis=0)) * scale
    return gq.astype(BF16), (gk * scale).astype(BF16), gv.astype(BF16)


D_IMGS = 2
DM = D_IMGS * RP
D_HG = DW // 128
D_HPG = 128 // DEC_HEAD


def dec_bias(st):
    head = st[: RP - 16]
    tail = st[RP - 16 :]
    keys = lax.broadcasted_iota(jnp.int32, tail.shape, 0) + (RP - 16)
    return jnp.concatenate([head, jnp.where(keys < PATCHES, tail, NEG)], axis=0)


def dec_kernel(
    recv_ref,
    visr_ref,
    visc_ref,
    cot_ref,
    pos_ref,
    par_ref,
    hid_ref,
    wq_ref,
    wk_ref,
    wv_ref,
    wo_ref,
    wup_ref,
    wdn_ref,
    emb_ref,
    out_ref,
    gyl_ref,
    gq_o,
    gk_o,
    gv_o,
    go_o,
    gup_o,
    gdn_o,
    gemb_o,
    small_o,
    ghid_o,
    xd_s,
    x2_s,
    y_s,
    ga_s,
    flat_s,
    q_s,
    k_s,
    v_s,
    o_s,
    ot_s,
    pt_s,
    a1_s,
    a1t_s,
    a2_s,
    a2t_s,
    gm_s,
    gmt_s,
    go_s,
    gq_s,
    gk_s,
    gv_s,
    aq,
    ak,
    av,
    ao,
    aup,
    adt,
    aemb,
):
    step = pl.program_id(0)
    last = pl.num_programs(0) - 1

    @pl.when(step == 0)
    def _():
        for ref in (aq, ak, av, ao, aup, adt, aemb, small_o, ghid_o):
            ref[...] = jnp.zeros_like(ref)
        flat_s[...] = jnp.zeros_like(flat_s)

    mask_tok = par_ref[0:1]
    gain1, gain2 = par_ref[1:2], par_ref[2:3]
    sh_emb, sh1, sh2 = par_ref[3:4], par_ref[4:5], par_ref[5:6]
    sh_q, sh_v, sh_o, sh_d = par_ref[6:7], par_ref[7:8], par_ref[8:9], par_ref[9:10]

    for i in range(D_IMGS):
        cells = lax.broadcasted_iota(jnp.int32, (RP, VISIBLE), 0)
        hot = visr_ref[i] == cells
        present = jnp.max(jnp.where(hot, 1.0, 0.0), axis=1, keepdims=True)
        placed = nn(jnp.where(hot, 1.0, 0.0).astype(BF16), recv_ref[i]).astype(BF16)
        z = nn(placed, emb_ref[...]) + sh_emb
        xd_s[pl.ds(i * RP, RP), :] = jnp.where(present > 0.5, z, mask_tok) + pos_ref[...]

    xhat1, rstd1 = norm_stats(xd_s[...])
    a1 = (xhat1 * gain1 + sh1).astype(BF16)
    a1_s[...] = a1
    for w_ref, bias, dst in ((wq_ref, sh_q, q_s), (wk_ref, None, k_s), (wv_ref, sh_v, v_s)):
        val = nn(a1, w_ref[...])
        val = (val if bias is None else val + bias).astype(BF16)
        for i in range(D_IMGS):
            for g in range(D_HG):
                dst[i * D_HG + g] = val[i * RP : (i + 1) * RP, g * 128 : (g + 1) * 128]
    a1t_s[...] = jnp.transpose(a1_s[...])

    def fwd_body(j, carry):
        def store(h, pt):
            pt_s[j * D_HPG + h] = pt

        ot = attend_fwd(q_s[j], k_s[j], v_s[j], DEC_HEAD, dec_bias, store)
        ot_s[j] = ot.astype(BF16)
        o_s[j] = jnp.transpose(ot).astype(BF16)
        return carry

    lax.fori_loop(0, D_IMGS * D_HG, fwd_body, 0, unroll=4)

    o_full = jnp.concatenate(
        [
            jnp.concatenate([o_s[i * D_HG + g] for g in range(D_HG)], axis=1)
            for i in range(D_IMGS)
        ],
        axis=0,
    )
    x2_s[...] = xd_s[...] + (nn(o_full, wo_ref[...]) + sh_o)
    xhat2, rstd2 = norm_stats(x2_s[...])
    a2 = (xhat2 * gain2 + sh2).astype(BF16)
    a2_s[...] = a2
    a2t_s[...] = jnp.transpose(a2_s[...])

    flat_s[pl.ds(0, D_IMGS * PATCHES), :] = cot_ref[...].astype(F32)
    rows = lax.broadcasted_iota(jnp.int32, (RP, DW), 0)
    for i in range(D_IMGS):
        part = flat_s[pl.ds(i * PATCHES, RP), :]
        gm_s[pl.ds(i * RP, RP), :] = jnp.where(rows < PATCHES, part, 0.0).astype(BF16)
    gmt_s[...] = jnp.transpose(gm_s[...])
    small_o[pl.ds(9, 1), :] += colsum(gm_s[...].astype(F32))

    y_s[...] = x2_s[...] + sh_d
    ga_s[...] = jnp.zeros_like(ga_s)

    def mlp_body(c, carry):
        wup = wup_ref[c]
        wdn = wdn_ref[c]
        u = nn(a2_s[...], wup) + hid_ref[c]
        hid, dgelu = gelu_both(u)
        hid = hid.astype(BF16)
        y_s[...] += nn(hid, wdn)
        gu = (nt(gm_s[...], wdn) * dgelu).astype(BF16)
        ga_s[...] += nt(gu, wup)
        adt[c] += nn(gmt_s[...], hid)
        aup[c] += nn(a2t_s[...], gu)
        ghid_o[c] += colsum(gu.astype(F32))
        return carry

    lax.fori_loop(0, DEC_CHUNKS, mlp_body, 0, unroll=True)

    for i in range(D_IMGS):
        flat_s[pl.ds(i * PATCHES, PATCHES), :] = y_s[pl.ds(i * RP, PATCHES), :]
    out_ref[...] = flat_s[pl.ds(0, D_IMGS * PATCHES), :].astype(BF16)

    ga2 = ga_s[...]
    xhat2, rstd2 = norm_stats(x2_s[...])
    small_o[pl.ds(2, 1), :] += colsum(ga2 * xhat2)
    small_o[pl.ds(5, 1), :] += colsum(ga2)
    gx2 = gm_s[...].astype(F32) + norm_back(xhat2, rstd2, gain2, ga2)
    x2_s[...] = gx2
    gpr = gx2.astype(BF16)
    small_o[pl.ds(8, 1), :] += colsum(gpr.astype(F32))
    go = nt(gpr, wo_ref[...]).astype(BF16)
    for i in range(D_IMGS):
        part = gpr[i * RP : (i + 1) * RP]
        ao[...] += nn(ot_s[pl.ds(i * D_HG, D_HG)].reshape(DW, RP), part)
        for g in range(D_HG):
            go_s[i * D_HG + g] = go[i * RP : (i + 1) * RP, g * 128 : (g + 1) * 128]

    def bwd_body(j, carry):
        gq, gk, gv = attend_bwd(
            q_s[j], k_s[j], v_s[j], go_s[j], DEC_HEAD, lambda h: pt_s[j * D_HPG + h]
        )
        gq_s[j] = gq
        gk_s[j] = gk
        gv_s[j] = gv
        return carry

    lax.fori_loop(0, D_IMGS * D_HG, bwd_body, 0, unroll=4)

    ga1 = None
    for src, w_ref, acc, row in ((gq_s, wq_ref, aq, 6), (gk_s, wk_ref, ak, None), (gv_s, wv_ref, av, 7)):
        full = jnp.concatenate(
            [
                jnp.concatenate([src[i * D_HG + g] for g in range(D_HG)], axis=1)
                for i in range(D_IMGS)
            ],
            axis=0,
        )
        if row is not None:
            small_o[pl.ds(row, 1), :] += colsum(full.astype(F32))
        acc[...] += nn(a1t_s[...], full)
        part = nt(full, w_ref[...])
        ga1 = part if ga1 is None else ga1 + part

    xhat1, rstd1 = norm_stats(xd_s[...])
    small_o[pl.ds(1, 1), :] += colsum(ga1 * xhat1)
    small_o[pl.ds(4, 1), :] += colsum(ga1)
    y_s[...] = x2_s[...] + norm_back(xhat1, rstd1, gain1, ga1)

    for i in range(D_IMGS):
        gx = y_s[pl.ds(i * RP, RP), :]
        cells = lax.broadcasted_iota(jnp.int32, (RP, VISIBLE), 0)
        hot = visr_ref[i] == cells
        present = jnp.max(jnp.where(hot, 1.0, 0.0), axis=1, keepdims=True)
        small_o[pl.ds(0, 1), :] += colsum(jnp.where(present > 0.5, 0.0, gx))
        cells_t = lax.broadcasted_iota(jnp.int32, (64, RP), 1)
        hot_t = jnp.where(visc_ref[i] == cells_t, 1.0, 0.0).astype(BF16)
        gz = nn(hot_t, gx.astype(BF16)).astype(BF16)
        small_o[pl.ds(3, 1), :] += colsum(gz.astype(F32))
        aemb[...] += lax.dot_general(
            recv_ref[i], gz[:VISIBLE], (((0,), (0,)), ((), ())), preferred_element_type=F32
        )
        gyl_ref[i] = nt(gz, emb_ref[...])[:VISIBLE].astype(BF16)

    @pl.when(step == last)
    def _():
        gq_o[...] = aq[...].astype(BF16)
        gk_o[...] = ak[...].astype(BF16)
        gv_o[...] = av[...].astype(BF16)
        go_o[...] = ao[...].astype(BF16)
        gup_o[...] = aup[...].astype(BF16)
        for c in range(DEC_CHUNKS):
            gdn_o[c] = jnp.transpose(adt[c]).astype(BF16)
        gemb_o[...] = aemb[...].astype(BF16)


def whole(shape):
    zeros = (0,) * len(shape)
    return pl.BlockSpec(shape, lambda *_: zeros, pipeline_mode=pl.Buffered(1))


def decoder(recv, visible, cot, pos, par, hid, wq, wk, wv, wo, wup, wdn, emb):
    images = recv.shape[0]
    visr = visible.reshape(images, 1, VISIBLE)
    visc = jnp.pad(visible, ((0, 0), (0, 64 - VISIBLE)), constant_values=-1).reshape(images, 64, 1)
    f, b = F32, BF16
    vm = pltpu.VMEM
    grp = D_IMGS * D_HG
    ins = [
        pl.BlockSpec((D_IMGS, VISIBLE, EW), lambda i: (i, 0, 0)),
        pl.BlockSpec((D_IMGS, 1, VISIBLE), lambda i: (i, 0, 0)),
        pl.BlockSpec((D_IMGS, 64, 1), lambda i: (i, 0, 0)),
        pl.BlockSpec((D_IMGS * PATCHES, DW), lambda i: (i, 0)),
    ] + [whole(a.shape) for a in (pos, par, hid, wq, wk, wv, wo, wup, wdn, emb)]
    square = jax.ShapeDtypeStruct((DW, DW), b)
    chunked = jax.ShapeDtypeStruct((DEC_CHUNKS, DW, DW), b)
    outs = [
        jax.ShapeDtypeStruct((images * PATCHES, DW), b),
        jax.ShapeDtypeStruct((images, VISIBLE, EW), b),
        square,
        square,
        square,
        square,
        chunked,
        chunked,
        jax.ShapeDtypeStruct((EW, DW), b),
        jax.ShapeDtypeStruct((16, DW), f),
        jax.ShapeDtypeStruct((DEC_CHUNKS, 1, DW), f),
    ]
    out_specs = [
        pl.BlockSpec((D_IMGS * PATCHES, DW), lambda i: (i, 0)),
        pl.BlockSpec((D_IMGS, VISIBLE, EW), lambda i: (i, 0, 0)),
    ] + [whole(o.shape) for o in outs[2:]]
    scratch = [
        vm((DM, DW), f),
        vm((DM, DW), f),
        vm((DM, DW), f),
        vm((DM, DW), f),
        vm((D_IMGS * PATCHES + 24, DW), f),
        vm((grp, RP, 128), b),
        vm((grp, RP, 128), b),
        vm((grp, RP, 128), b),
        vm((grp, RP, 128), b),
        vm((grp, 128, RP), b),
        vm((grp * D_HPG, RP, RP), b),
        vm((DM, DW), b),
        vm((DW, DM), b),
        vm((DM, DW), b),
        vm((DW, DM), b),
        vm((DM, DW), b),
        vm((DW, DM), b),
        vm((grp, RP, 128), b),
        vm((grp, RP, 128), b),
        vm((grp, RP, 128), b),
        vm((grp, RP, 128), b),
        vm((DW, DW), f),
        vm((DW, DW), f),
        vm((DW, DW), f),
        vm((DW, DW), f),
        vm((DEC_CHUNKS, DW, DW), f),
        vm((DEC_CHUNKS, DW, DW), f),
        vm((EW, DW), f),
    ]
    return pl.pallas_call(
        dec_kernel,
        grid=(images // D_IMGS,),
        in_specs=ins,
        out_specs=out_specs,
        out_shape=outs,
        scratch_shapes=scratch,
        compiler_params=pltpu.CompilerParams(
            dimension_semantics=("arbitrary",), vmem_limit_bytes=60 << 20
        ),
        cost_estimate=pl.CostEstimate(
            flops=225 * 10**9, transcendentals=0, bytes_accessed=250 * 10**6
        ),
        name="decoder",
    )(recv, visr, visc, cot, pos, par, hid, wq, wk, wv, wo, wup, wdn, emb)


EM = ENC_GROUPS * RP
E_HB = 3
E_J = ENC_GROUPS * 2
E_HPG = 128 // ENC_HEAD
GROUP_IMGS = IMG_DEV // ENC_GROUPS
WIN = 56


def seg_of(i):
    return (
        jnp.where(i >= VISIBLE, 1, 0)
        + jnp.where(i >= 2 * VISIBLE, 1, 0)
        + jnp.where(i >= 3 * VISIBLE, 1, 0)
        + jnp.where(i >= 4 * VISIBLE, 1, 0)
    )


def enc_attn_kernel(
    start_ref,
    x_ref,
    par_ref,
    parb_ref,
    wq_ref,
    wk_ref,
    wv_ref,
    wo_ref,
    xc_o,
    q_o,
    k_o,
    v_o,
    pt_o,
    ot_o,
    x2_o,
    xf_s,
    xc_s,
    a1_s,
    o_s,
    bias_s,
):
    step = pl.program_id(0)

    @pl.when(step == 0)
    def _():
        xf_s[pl.ds(0, ROWS_DEV), :] = x_ref[...].astype(F32)
        for grp in range(ENC_GROUPS):
            xc_s[pl.ds(grp * RP + PATCHES, RP - PATCHES), :] = jnp.zeros((RP - PATCHES, EW), F32)
            for i in range(GROUP_IMGS):
                start = start_ref[grp * GROUP_IMGS + i]
                shift = lax.rem(start, 8)
                base = pl.multiple_of(start - shift, 8)
                part = pltpu.roll(xf_s[pl.ds(base, WIN), :], WIN - shift, 0)
                xc_s[pl.ds(grp * RP + i * VISIBLE, VISIBLE), :] = part[:VISIBLE]
        x = xc_s[...]
        xc_o[...] = x.astype(BF16)
        xhat, _ = norm_stats(x)
        a1_s[...] = (xhat * par_ref[0:1] + par_ref[2:3]).astype(BF16)
        x2_o[...] = x + par_ref[6:7]
        keys = lax.broadcasted_iota(jnp.int32, (RP, RP), 0)
        queries = lax.broadcasted_iota(jnp.int32, (RP, RP), 1)
        same = (seg_of(keys) == seg_of(queries)) & (keys < PATCHES)
        bias_s[...] = jnp.where(same, 0.0, NEG)

    for w_ref, row, dst in ((wq_ref, 4, q_o), (wk_ref, None, k_o), (wv_ref, 5, v_o)):
        val = nn(a1_s[...], w_ref[...])
        if row is not None:
            val = val + parb_ref[row : row + 1]
        val = val.astype(BF16)
        for grp in range(ENC_GROUPS):
            for half in range(2):
                dst[0, grp * 2 + half] = val[
                    grp * RP : (grp + 1) * RP, half * 128 : (half + 1) * 128
                ]

    def loop(j, carry):
        def store(h, pt):
            pt_o[0, j * E_HPG + h] = pt

        ot = attend_fwd(
            q_o[0, j], k_o[0, j], v_o[0, j], ENC_HEAD, lambda st: st + bias_s[...], store
        )
        ot_o[0, j] = ot.astype(BF16)
        o_s[j] = jnp.transpose(ot).astype(BF16)
        return carry

    lax.fori_loop(0, E_J, loop, 0, unroll=4)
    o_full = jnp.concatenate(
        [
            jnp.concatenate([o_s[grp * 2], o_s[grp * 2 + 1]], axis=1)
            for grp in range(ENC_GROUPS)
        ],
        axis=0,
    )
    x2_o[...] += nn(o_full, wo_ref[...])


def enc_attn(starts, x, par, wq, wk, wv, wo):
    f, b = F32, BF16
    vm = pltpu.VMEM
    col = pl.BlockSpec((EW, 256), lambda i, s: (0, i))
    row = pl.BlockSpec((256, EW), lambda i, s: (i, 0))
    grp = pl.BlockSpec((1, E_J, RP, 128), lambda i, s: (i, 0, 0, 0))
    outs = [
        (jax.ShapeDtypeStruct((EM, EW), b), whole((EM, EW))),
        (jax.ShapeDtypeStruct((E_HB, E_J, RP, 128), b), grp),
        (jax.ShapeDtypeStruct((E_HB, E_J, RP, 128), b), grp),
        (jax.ShapeDtypeStruct((E_HB, E_J, RP, 128), b), grp),
        (
            jax.ShapeDtypeStruct((E_HB, E_J * E_HPG, RP, RP), b),
            pl.BlockSpec((1, E_J * E_HPG, RP, RP), lambda i, s: (i, 0, 0, 0)),
        ),
        (
            jax.ShapeDtypeStruct((E_HB, E_J, 128, RP), b),
            pl.BlockSpec((1, E_J, 128, RP), lambda i, s: (i, 0, 0, 0)),
        ),
        (jax.ShapeDtypeStruct((EM, EW), f), whole((EM, EW))),
    ]
    return pl.pallas_call(
        enc_attn_kernel,
        grid_spec=pltpu.PrefetchScalarGridSpec(
            num_scalar_prefetch=1,
            grid=(E_HB,),
            in_specs=[
                whole(x.shape),
                whole(par.shape),
                pl.BlockSpec((8, 256), lambda i, s: (0, i)),
                col,
                col,
                col,
                row,
            ],
            out_specs=[o[1] for o in outs],
            scratch_shapes=[
                vm((ROWS_DEV + 16, EW), f),
                vm((EM, EW), f),
                vm((EM, EW), b),
                vm((E_J, RP, 128), b),
                vm((RP, RP), f),
            ],
        ),
        out_shape=[o[0] for o in outs],
        compiler_params=pltpu.CompilerParams(
            dimension_semantics=("arbitrary",), vmem_limit_bytes=60 << 20
        ),
        cost_estimate=pl.CostEstimate(
            flops=27 * 10**9, transcendentals=0, bytes_accessed=30 * 10**6
        ),
        name="enc_attn",
    )(starts, x, par, par, wq, wk, wv, wo)


def enc_mlp_kernel(
    x2_ref, par_ref, hid_ref, wup_ref, wdn_ref, yl_o, hid_o, dg_o, a2_s, y_s
):
    step = pl.program_id(0)

    @pl.when(step == 0)
    def _():
        x2 = x2_ref[...]
        xhat, _ = norm_stats(x2)
        a2_s[...] = (xhat * par_ref[1:2] + par_ref[3:4]).astype(BF16)
        y_s[...] = x2 + par_ref[7:8]

    u = nn(a2_s[...], wup_ref[0]) + hid_ref[0]
    hid, dgelu = gelu_both(u)
    hid = hid.astype(BF16)
    hid_o[0] = hid
    dg_o[0] = dgelu.astype(BF16)
    y_s[...] += nn(hid, wdn_ref[0])

    @pl.when(step == pl.num_programs(0) - 1)
    def _():
        for grp in range(ENC_GROUPS):
            for i in range(GROUP_IMGS):
                part = y_s[pl.ds(grp * RP + i * VISIBLE, VISIBLE), :]
                yl_o[grp * GROUP_IMGS + i] = part.astype(BF16)


def enc_mlp(x2, par, hid, wup, wdn):
    f, b = F32, BF16
    chunk = pl.BlockSpec((1, EM, EW), lambda i: (i, 0, 0))
    wchunk = pl.BlockSpec((1, EW, EW), lambda i: (i, 0, 0))
    outs = [
        (jax.ShapeDtypeStruct((IMG_DEV, VISIBLE, EW), b), whole((IMG_DEV, VISIBLE, EW))),
        (jax.ShapeDtypeStruct((ENC_CHUNKS, EM, EW), b), chunk),
        (jax.ShapeDtypeStruct((ENC_CHUNKS, EM, EW), b), chunk),
    ]
    return pl.pallas_call(
        enc_mlp_kernel,
        grid=(ENC_CHUNKS,),
        in_specs=[
            whole(x2.shape),
            whole(par.shape),
            pl.BlockSpec((1, 1, EW), lambda i: (i, 0, 0)),
            wchunk,
            wchunk,
        ],
        out_specs=[o[1] for o in outs],
        out_shape=[o[0] for o in outs],
        scratch_shapes=[pltpu.VMEM((EM, EW), b), pltpu.VMEM((EM, EW), f)],
        compiler_params=pltpu.CompilerParams(
            dimension_semantics=("arbitrary",), vmem_limit_bytes=60 << 20
        ),
        cost_estimate=pl.CostEstimate(
            flops=21 * 10**9, transcendentals=0, bytes_accessed=24 * 10**6
        ),
        name="enc_mlp",
    )(x2, par, hid, wup, wdn)


def enc_mlp_back_kernel(
    gy_ref,
    x2_ref,
    par_ref,
    hid_ref,
    dg_ref,
    wup_ref,
    wdn_ref,
    gx2_o,
    gup_o,
    gdn_o,
    small_o,
    ghid_o,
    gf_s,
    gm_s,
    a2t_s,
    ga_s,
):
    step = pl.program_id(0)

    @pl.when(step == 0)
    def _():
        for grp in range(ENC_GROUPS):
            gf_s[pl.ds(grp * RP + PATCHES, RP - PATCHES), :] = jnp.zeros((RP - PATCHES, EW), F32)
            for i in range(GROUP_IMGS):
                part = gy_ref[grp * GROUP_IMGS + i].astype(F32)
                gf_s[pl.ds(grp * RP + i * VISIBLE, VISIBLE), :] = part
        gm_s[...] = gf_s[...].astype(BF16)
        xhat, _ = norm_stats(x2_ref[...])
        a2 = (xhat * par_ref[1:2] + par_ref[3:4]).astype(BF16)
        a2t_s[...] = jnp.transpose(a2)
        ga_s[...] = jnp.zeros_like(ga_s)
        small_o[...] = jnp.zeros_like(small_o)
        small_o[pl.ds(7, 1), :] = colsum(gf_s[...])

    gu = (nt(gm_s[...], wdn_ref[0]) * dg_ref[0].astype(F32)).astype(BF16)
    ga_s[...] += nt(gu, wup_ref[0])
    gup_o[0] = nn(a2t_s[...], gu).astype(BF16)
    gdn_o[0] = nn(jnp.transpose(hid_ref[0]), gm_s[...]).astype(BF16)
    ghid_o[0] = colsum(gu.astype(F32))

    @pl.when(step == pl.num_programs(0) - 1)
    def _():
        ga2 = ga_s[...]
        xhat, rstd = norm_stats(x2_ref[...])
        small_o[pl.ds(1, 1), :] = colsum(ga2 * xhat)
        small_o[pl.ds(3, 1), :] = colsum(ga2)
        gx2 = gf_s[...] + norm_back(xhat, rstd, par_ref[1:2], ga2)
        gx2_o[...] = gx2
        small_o[pl.ds(6, 1), :] = colsum(gx2.astype(BF16).astype(F32))


def enc_mlp_back(gy, x2, par, hid, dg, wup, wdn):
    f, b = F32, BF16
    chunk = pl.BlockSpec((1, EM, EW), lambda i: (i, 0, 0))
    wchunk = pl.BlockSpec((1, EW, EW), lambda i: (i, 0, 0))
    outs = [
        (jax.ShapeDtypeStruct((EM, EW), f), whole((EM, EW))),
        (jax.ShapeDtypeStruct((ENC_CHUNKS, EW, EW), b), wchunk),
        (jax.ShapeDtypeStruct((ENC_CHUNKS, EW, EW), b), wchunk),
        (jax.ShapeDtypeStruct((8, EW), f), whole((8, EW))),
        (
            jax.ShapeDtypeStruct((ENC_CHUNKS, 1, EW), f),
            pl.BlockSpec((1, 1, EW), lambda i: (i, 0, 0)),
        ),
    ]
    return pl.pallas_call(
        enc_mlp_back_kernel,
        grid=(ENC_CHUNKS,),
        in_specs=[whole(gy.shape), whole(x2.shape), whole(par.shape), chunk, chunk, wchunk, wchunk],
        out_specs=[o[1] for o in outs],
        out_shape=[o[0] for o in outs],
        scratch_shapes=[
            pltpu.VMEM((EM, EW), f),
            pltpu.VMEM((EM, EW), b),
            pltpu.VMEM((EW, EM), b),
            pltpu.VMEM((EM, EW), f),
        ],
        compiler_params=pltpu.CompilerParams(
            dimension_semantics=("arbitrary",), vmem_limit_bytes=60 << 20
        ),
        cost_estimate=pl.CostEstimate(
            flops=25 * 10**9, transcendentals=0, bytes_accessed=28 * 10**6
        ),
        name="enc_mlp_back",
    )(gy, x2, par, hid, dg, wup, wdn)


def enc_attn_back_kernel(
    start_ref,
    gx2_ref,
    xc_ref,
    par_ref,
    q_ref,
    k_ref,
    v_ref,
    pt_ref,
    ot_ref,
    wq_ref,
    wk_ref,
    wv_ref,
    wo_ref,
    gx_o,
    gwq_o,
    gwk_o,
    gwv_o,
    gwo_o,
    small_o,
    gb_o,
    gpr_s,
    a1t_s,
    ga_s,
    go_s,
    gq_s,
    gk_s,
    gv_s,
    gf_s,
):
    step = pl.program_id(0)

    @pl.when(step == 0)
    def _():
        gpr_s[...] = gx2_ref[...].astype(BF16)
        xhat, _ = norm_stats(xc_ref[...].astype(F32))
        a1 = (xhat * par_ref[0:1] + par_ref[2:3]).astype(BF16)
        a1t_s[...] = jnp.transpose(a1)
        ga_s[...] = jnp.zeros_like(ga_s)
        small_o[...] = jnp.zeros_like(small_o)

    go = nt(gpr_s[...], wo_ref[...]).astype(BF16)
    for half in range(2):
        acc = None
        for grp in range(ENC_GROUPS):
            rows = slice(grp * RP, (grp + 1) * RP)
            go_s[grp * 2 + half] = go[rows, half * 128 : (half + 1) * 128]
            part = nn(ot_ref[0, grp * 2 + half], gpr_s[pl.ds(grp * RP, RP), :])
            acc = part if acc is None else acc + part
        gwo_o[pl.ds(half * 128, 128), :] = acc.astype(BF16)

    def loop(j, carry):
        gq, gk, gv = attend_bwd(
            q_ref[0, j],
            k_ref[0, j],
            v_ref[0, j],
            go_s[j],
            ENC_HEAD,
            lambda h: pt_ref[0, j * E_HPG + h],
        )
        gq_s[j] = gq
        gk_s[j] = gk
        gv_s[j] = gv
        return carry

    lax.fori_loop(0, E_J, loop, 0, unroll=4)
    gb_o[...] = jnp.zeros_like(gb_o)
    ga1 = ga_s[...]
    for src, w_ref, dst, row in (
        (gq_s, wq_ref, gwq_o, 4),
        (gk_s, wk_ref, gwk_o, None),
        (gv_s, wv_ref, gwv_o, 5),
    ):
        full = jnp.concatenate(
            [
                jnp.concatenate([src[grp * 2], src[grp * 2 + 1]], axis=1)
                for grp in range(ENC_GROUPS)
            ],
            axis=0,
        )
        if row is not None:
            gb_o[pl.ds(row, 1), :] = colsum(full.astype(F32))
        dst[...] = nn(a1t_s[...], full).astype(BF16)
        ga1 = ga1 + nt(full, w_ref[...])
    ga_s[...] = ga1

    @pl.when(step == pl.num_programs(0) - 1)
    def _():
        ga = ga_s[...]
        xhat, rstd = norm_stats(xc_ref[...].astype(F32))
        small_o[pl.ds(0, 1), :] = colsum(ga * xhat)
        small_o[pl.ds(2, 1), :] = colsum(ga)
        ga_s[...] = gx2_ref[...] + norm_back(xhat, rstd, par_ref[0:1], ga)
        gf_s[...] = jnp.zeros_like(gf_s)
        rows = lax.broadcasted_iota(jnp.int32, (WIN, EW), 0)
        for grp in range(ENC_GROUPS):
            for i in range(GROUP_IMGS):
                start = start_ref[grp * GROUP_IMGS + i]
                shift = lax.rem(start, 8)
                base = pl.multiple_of(start - shift, 8)
                first = grp * RP + i * VISIBLE
                part = jnp.where(rows < VISIBLE, ga_s[pl.ds(first, WIN), :], 0.0)
                gf_s[pl.ds(base, WIN), :] += pltpu.roll(part, shift, 0)
        gx_o[...] = gf_s[pl.ds(0, ROWS_DEV), :]


def enc_attn_back(starts, gx2, xc, par, q, k, v, pt, ot, wq, wk, wv, wo):
    f, b = F32, BF16
    vm = pltpu.VMEM
    col = pl.BlockSpec((EW, 256), lambda i, s: (0, i))
    row = pl.BlockSpec((256, EW), lambda i, s: (i, 0))
    grp = pl.BlockSpec((1, E_J, RP, 128), lambda i, s: (i, 0, 0, 0))
    square = jax.ShapeDtypeStruct((EW, EW), b)
    outs = [
        (jax.ShapeDtypeStruct((ROWS_DEV, EW), f), whole((ROWS_DEV, EW))),
        (square, col),
        (square, col),
        (square, col),
        (square, row),
        (jax.ShapeDtypeStruct((8, EW), f), whole((8, EW))),
        (jax.ShapeDtypeStruct((8, EW), f), pl.BlockSpec((8, 256), lambda i, s: (0, i))),
    ]
    return pl.pallas_call(
        enc_attn_back_kernel,
        grid_spec=pltpu.PrefetchScalarGridSpec(
            num_scalar_prefetch=1,
            grid=(E_HB,),
            in_specs=[
                whole(gx2.shape),
                whole(xc.shape),
                whole(par.shape),
                grp,
                grp,
                grp,
                pl.BlockSpec((1, E_J * E_HPG, RP, RP), lambda i, s: (i, 0, 0, 0)),
                pl.BlockSpec((1, E_J, 128, RP), lambda i, s: (i, 0, 0, 0)),
                col,
                col,
                col,
                row,
            ],
            out_specs=[o[1] for o in outs],
            scratch_shapes=[
                vm((EM, EW), b),
                vm((EW, EM), b),
                vm((EM, EW), f),
                vm((E_J, RP, 128), b),
                vm((E_J, RP, 128), b),
                vm((E_J, RP, 128), b),
                vm((E_J, RP, 128), b),
                vm((ROWS_DEV + 16, EW), f),
            ],
        ),
        out_shape=[o[0] for o in outs],
        compiler_params=pltpu.CompilerParams(
            dimension_semantics=("arbitrary",), vmem_limit_bytes=60 << 20
        ),
        cost_estimate=pl.CostEstimate(
            flops=36 * 10**9, transcendentals=0, bytes_accessed=40 * 10**6
        ),
        name="enc_attn_back",
    )(starts, gx2, xc, par, q, k, v, pt, ot, wq, wk, wv, wo)


def position_rows():
    quarter = DW // 4
    frequency = 1.0 / 10000.0 ** (np.arange(quarter) / quarter)
    cells = np.arange(PATCHES)
    by_row = (cells // SIDE)[:, None] * frequency[None, :]
    by_col = (cells % SIDE)[:, None] * frequency[None, :]
    table = np.concatenate([np.sin(by_row), np.cos(by_row), np.sin(by_col), np.cos(by_col)], axis=1)
    return np.pad(table, ((0, RP - PATCHES), (0, 0))).astype(np.float32)


def small_rows(parts, width):
    flat = jnp.concatenate([p.reshape(-1) for p in parts])
    return jnp.pad(flat, (0, 8 * width - flat.shape[0])).reshape(8, width)


def col_blocks(w, width):
    return [w[:, i : i + width] for i in range(0, w.shape[1], width)]


def per_device(v, n):
    rows = v.shape[0]
    return v.reshape(rows, n, -1).transpose(1, 0, 2).reshape(n, -1)


def all_devices(v, rows):
    n = v.shape[0]
    return v.reshape(n, rows, -1).transpose(1, 0, 2).reshape(rows, -1)


def pairs(count, minor, flip_major, flip_minor):
    return [
        (i, (i // minor ^ flip_major) * minor + (i % minor ^ flip_minor)) for i in range(count)
    ]


def send(v, sizes, flip_dp=0, flip_fsdp=0):
    dp, fsdp = sizes
    return lax.ppermute(v, BOTH, pairs(dp * fsdp, fsdp, flip_dp, flip_fsdp))


def gather(v, sizes):
    dp, fsdp = sizes
    me = lax.axis_index("fsdp")
    parts = [v] + [send(v, sizes, 0, k) for k in range(1, fsdp)]
    bit = 1
    while bit < fsdp:
        odd = (me & bit) != 0
        parts = [jnp.where(odd, parts[i ^ bit], parts[i]) for i in range(fsdp)]
        bit *= 2
    block = jnp.concatenate(parts, axis=0)
    full = lax.all_gather(block, "dp", axis=0, tiled=True)
    return full.reshape(dp * fsdp, v.shape[0], v.shape[1])


def pick(v, index, axis=0):
    return lax.dynamic_index_in_dim(v, index, axis, keepdims=False)


def sum_fsdp(v, sizes):
    me = lax.axis_index("fsdp")
    total = pick(v, me).astype(F32)
    for k in range(1, sizes[1]):
        total = total + send(pick(v, me ^ k), sizes, 0, k).astype(F32)
    return total


def scatter_sum(packed, sizes):
    n, rows, width = packed.shape
    flat = lax.psum_scatter(
        packed.reshape(n * rows, width), "dp", scatter_dimension=0, tiled=True
    )
    return sum_fsdp(flat.reshape(sizes[1], rows, width), sizes)


def halve(v, sizes, axis, bit):
    mine = (lax.axis_index("dp") // bit) % 2
    other = send(pick(v, 1 - mine, axis), sizes, bit, 0)
    return (pick(v, mine, axis).astype(F32) + other.astype(F32)).astype(BF16)


def exchange_sum(packed, sizes):
    n, rows, width = packed.shape
    dp, fsdp = sizes
    bits = dp.bit_length() - 1
    v = packed.reshape((2,) * bits + (fsdp, rows, width))
    v = halve(v, sizes, bits - 1, 1)
    cut = rows // 16 * 8
    outs = []
    for part, order in ((v[..., :cut, :], "up"), (v[..., cut:, :], "down")):
        for step in range(bits - 1):
            left = bits - 1 - step
            if order == "up":
                part = halve(part, sizes, left - 1, 2 ** (step + 1))
            else:
                part = halve(part, sizes, 0, 2 ** left)
        outs.append(part)
    return sum_fsdp(jnp.concatenate(outs, axis=-2), sizes)


def make_body(sizes):
    n = sizes[0] * sizes[1]
    er, dr = EW // n, DW // n

    def body(
        patches,
        segments,
        send_slot,
        visible,
        enc_gain,
        enc_shift,
        enc_hidden,
        enc_qkv,
        enc_out,
        enc_up,
        enc_down,
        embedding,
        mask_token,
        dec_gain,
        dec_shift,
        dec_hidden,
        dec_qkv,
        dec_out,
        dec_up,
        dec_down,
        cotangent,
    ):
        pack_a = jnp.concatenate(
            col_blocks(enc_qkv, EW) + [enc_out, small_rows((enc_gain, enc_shift, enc_hidden), EW)]
        )
        pack_b = jnp.concatenate(col_blocks(enc_up, EW) + [enc_down])
        pack_d = jnp.concatenate(
            col_blocks(dec_qkv, DW)
            + [dec_out]
            + col_blocks(dec_up, DW)
            + [
                dec_down,
                embedding,
                small_rows((mask_token, dec_gain, dec_shift, dec_hidden), DW),
            ]
        )
        full_a = gather(pack_a, sizes)
        full_b = gather(pack_b, sizes)
        full_d = gather(pack_d, sizes)

        wq, wk, wv, wo = [full_a[:, i * er : (i + 1) * er].reshape(EW, EW) for i in range(4)]
        small = full_a[:, 4 * er :].reshape(n, -1).astype(F32)
        par = all_devices(small[:, : 8 * er], 8)
        hid = small[:, 8 * er : 12 * er].reshape(ENC_CHUNKS, 1, EW)
        wup = full_b[:, : 4 * er].reshape(n, 4, er, EW).transpose(1, 0, 2, 3).reshape(4, EW, EW)
        wdn = full_b[:, 4 * er :].reshape(4, EW, EW)

        row_ids = jnp.arange(ROWS_DEV, dtype=jnp.int32)
        image_ids = jnp.arange(IMG_DEV, dtype=jnp.int32)
        starts = jnp.min(
            jnp.where(segments[None, :] == image_ids[:, None], row_ids[None, :], ROWS_DEV), axis=1
        )
        hot = send_slot[0][None, :] == image_ids[:, None]
        slot_starts = jnp.sum(jnp.where(hot, starts[None, :], 0), axis=1).astype(jnp.int32)

        xc, q, k, v, pt, ot, x2 = enc_attn(slot_starts, patches, par, wq, wk, wv, wo)
        outgoing, hidden, dgelu = enc_mlp(x2, par, hid, wup, wdn)
        received = lax.all_to_all(outgoing, "dp", split_axis=0, concat_axis=0, tiled=True)

        dq, dk, dv, do = [full_d[:, i * dr : (i + 1) * dr].reshape(DW, DW) for i in range(4)]
        dup = (
            full_d[:, 4 * dr : 8 * dr]
            .reshape(n, 4, dr, DW)
            .transpose(1, 0, 2, 3)
            .reshape(4, DW, DW)
        )
        ddn = full_d[:, 8 * dr : 12 * dr].reshape(4, DW, DW)
        emb = full_d[:, 12 * dr : 12 * dr + er].reshape(EW, DW)
        dsmall = full_d[:, 12 * dr + er :].reshape(n, -1).astype(F32)
        dpar = jnp.concatenate([all_devices(dsmall[:, : 10 * dr], 10), jnp.zeros((6, DW), F32)])
        dhid = dsmall[:, 10 * dr : 14 * dr].reshape(DEC_CHUNKS, 1, DW)
        pos = jnp.asarray(position_rows())

        decoded, gyl, gdq, gdk, gdv, gdo, gdup, gddn, gemb, gdsmall, gdhid = decoder(
            received, visible, cotangent, pos, dpar, dhid, dq, dk, dv, do, dup, ddn, emb
        )
        returned = lax.all_to_all(gyl, "dp", split_axis=0, concat_axis=0, tiled=True)

        def rows_of(v, width):
            return v.reshape(n, -1, width)

        def small_pack(vals, width):
            flat = jnp.concatenate(vals, axis=1)
            flat = jnp.pad(flat, ((0, 0), (0, 8 * width - flat.shape[1])))
            return flat.astype(BF16).reshape(n, 8, width)

        dpacked = (
            jnp.concatenate(
                [rows_of(g, DW) for g in (gdq, gdk, gdv, gdo)]
                + [rows_of(gdup[i], DW) for i in range(4)]
                + [
                    rows_of(gddn, DW),
                    rows_of(gemb, DW),
                    small_pack(
                        [per_device(gdsmall[:10], n), gdhid.reshape(n, -1)],
                        DW,
                    ),
                ],
                axis=1,
            )
        )
        dpacked, returned = lax.optimization_barrier((dpacked, returned))
        dsum = scatter_sum(dpacked, sizes)

        gx2, gup, gdn, sm1, ghid = enc_mlp_back(returned, x2, par, hidden, dgelu, wup, wdn)
        bpacked = jnp.concatenate(
            [rows_of(gup[i], EW) for i in range(4)] + [rows_of(gdn, EW)], axis=1
        )
        bpacked, gx2 = lax.optimization_barrier((bpacked, gx2))
        bsum = scatter_sum(bpacked, sizes)
        gx, gwq, gwk, gwv, gwo, sm2, gb = enc_attn_back(
            slot_starts, gx2, xc, par, q, k, v, pt, ot, wq, wk, wv, wo
        )
        asum = exchange_sum(
            jnp.concatenate(
                [rows_of(g, EW) for g in (gwq, gwk, gwv, gwo)]
                + [small_pack([per_device(sm1 + sm2 + gb, n), ghid.reshape(n, -1)], EW)],
                axis=1,
            ),
            sizes,
        )

        def cut(v, r, count, first=0):
            return jnp.concatenate(
                [v[(first + i) * r : (first + i + 1) * r] for i in range(count)], axis=1
            )

        esm = asum[4 * er :].reshape(-1)
        dsm = dsum[12 * dr + er :].reshape(-1)
        return (
            decoded,
            gx,
            esm[: 2 * er].reshape(2, er),
            esm[2 * er : 8 * er].reshape(6, er),
            esm[8 * er : 12 * er],
            cut(asum, er, 3),
            asum[3 * er : 4 * er],
            cut(bsum, er, 4),
            bsum[4 * er :],
            dsum[12 * dr : 12 * dr + er],
            dsm[:dr],
            dsm[dr : 3 * dr].reshape(2, dr),
            dsm[3 * dr : 10 * dr].reshape(7, dr),
            dsm[10 * dr : 14 * dr],
            cut(dsum, dr, 3),
            dsum[3 * dr : 4 * dr],
            cut(dsum, dr, 4, 4),
            dsum[8 * dr : 12 * dr],
        )

    return body


def solution(mesh):
    sizes = (mesh.shape["dp"], mesh.shape["fsdp"])
    rows, vec, cols = P(BOTH, None), P(BOTH), P(None, BOTH)
    return jax.shard_map(
        make_body(sizes),
        mesh=mesh,
        in_specs=(rows, vec, rows, rows, cols, cols, vec, rows, rows, rows, rows)
        + (rows, vec, cols, cols, vec, rows, rows, rows, rows, rows),
        out_specs=(rows, rows, cols, cols, vec, rows, rows, rows, rows)
        + (rows, vec, cols, cols, vec, rows, rows, rows, rows),
        check_vma=False,
    )
```

```python
import math

import jax
import jax.numpy as jnp
import numpy as np
from jax import lax
from jax.experimental import pallas as pl
from jax.experimental.pallas import tpu as pltpu
from jax.sharding import PartitionSpec as P

ENC_HEAD = 64
DEC_HEAD = 32
SIDE = 14
VISIBLE = 49
ROWS_DEV = 1024
IMG_DEV = 16
EW = 768
DW = 512
PATCHES = 196
RP = 208
ENC_GROUPS = 4
ENC_CHUNKS = 4
DEC_CHUNKS = 4
NEG = -1e30
F32 = jnp.float32
BF16 = jnp.bfloat16
BOTH = ("dp", "fsdp")
EPS = 1e-06

ERF_P = 0.44
ERF_C = (
    0.2482209555836147,
    0.2488711484441078,
    0.21731375919172816,
    0.21581153367593472,
    -0.020179333598664445,
    0.2966860302544493,
    -0.2779471828654498,
    0.07122327097163224,
)


def nn(a, b):
    return lax.dot_general(a, b, (((1,), (0,)), ((), ())), preferred_element_type=F32)


def nt(a, b):
    return lax.dot_general(a, b, (((1,), (1,)), ((), ())), preferred_element_type=F32)


def colsum(v):
    return jnp.sum(v, axis=0, keepdims=True)


def gelu_both(u):
    t = 1.0 / (1.0 + (ERF_P / math.sqrt(2.0)) * jnp.abs(u))
    r = jnp.full_like(t, 0.5 * ERF_C[-1])
    for coef in ERF_C[-2::-1]:
        r = r * t + 0.5 * coef
    e = jnp.exp2((u * u) * (-0.5 * math.log2(math.e)))
    tail = (r * t) * e
    cdf = jnp.where(u >= 0, 1.0 - tail, tail)
    return u * cdf, cdf + (u * (1.0 / math.sqrt(2.0 * math.pi))) * e


def norm_stats(x):
    center = x - jnp.mean(x, axis=-1, keepdims=True)
    rstd = lax.rsqrt(jnp.mean(center * center, axis=-1, keepdims=True) + EPS)
    return center * rstd, rstd


def norm_back(xhat, rstd, gain, gy):
    d = gy * gain
    m1 = jnp.mean(d, axis=-1, keepdims=True)
    m2 = jnp.mean(d * xhat, axis=-1, keepdims=True)
    return rstd * (d - m1 - xhat * m2)


def lane_mask(shape, h, hd):
    lanes = lax.broadcasted_iota(jnp.int32, shape, 1)
    return (lanes >= h * hd) & (lanes < (h + 1) * hd)


def attend_fwd(q, k, v, hd, bias, pt_store):
    vt = jnp.transpose(v)
    heads = 128 // hd
    zero = jnp.zeros_like(q)
    c = hd ** (-0.5) * math.log2(math.e)
    pts = []
    for h in range(heads):
        sh = bias(nt(k, jnp.where(lane_mask(q.shape, h, hd), q, zero)))
        peak = jnp.max(sh, axis=0, keepdims=True)
        e = jnp.exp2((sh - peak) * c)
        inv = 1.0 / jnp.sum(e, axis=0, keepdims=True)
        pt = (e * inv).astype(BF16)
        pt_store(h, pt)
        pts.append(pt)
    outs = [nn(vt[h * hd : (h + 1) * hd], pts[h]) for h in range(heads)]
    return jnp.concatenate(outs, axis=0)


def attend_bwd(q, k, v, go, hd, pt_load):
    kt = jnp.transpose(k)
    heads = 128 // hd
    zero = jnp.zeros_like(q)
    scale = hd ** (-0.5)
    masks = [lane_mask(q.shape, h, hd) for h in range(heads)]
    vst = jnp.concatenate([jnp.where(m, v, zero) for m in masks], axis=0)
    gpt = nt(vst, go)
    gps = [gpt[h * RP : (h + 1) * RP] for h in range(heads)]
    gsts = []
    pts = [pt_load(h) for h in range(heads)]
    for h in range(heads):
        p32 = pts[h].astype(F32)
        dot = jnp.sum(p32 * gps[h], axis=0, keepdims=True)
        gsts.append((p32 * (gps[h] - dot)).astype(BF16))
    gv = gk = None
    for h in range(heads):
        gvh = nn(pts[h], go)
        gv = gvh if gv is None else jnp.where(masks[h], gvh, gv)
    for h in range(heads):
        gkh = nn(gsts[h], q)
        gk = gkh if gk is None else jnp.where(masks[h], gkh, gk)
    gqt = [nn(kt[h * hd : (h + 1) * hd], gsts[h]) for h in range(heads)]
    gq = jnp.transpose(jnp.concatenate(gqt, axis=0)) * scale
    return gq.astype(BF16), (gk * scale).astype(BF16), gv.astype(BF16)


D_IMGS = 2
DM = D_IMGS * RP
D_HG = DW // 128
D_HPG = 128 // DEC_HEAD


def dec_bias(st):
    head = st[: RP - 16]
    tail = st[RP - 16 :]
    keys = lax.broadcasted_iota(jnp.int32, tail.shape, 0) + (RP - 16)
    return jnp.concatenate([head, jnp.where(keys < PATCHES, tail, NEG)], axis=0)


def dec_kernel(
    recv_ref,
    visr_ref,
    visc_ref,
    cot_ref,
    pos_ref,
    par_ref,
    hid_ref,
    slab_ref,
    out_ref,
    gyl_ref,
    small_o,
    ghid_o,
    grad_o,
    xd_s,
    x2_s,
    y_s,
    ga_s,
    flat_s,
    q_s,
    k_s,
    v_s,
    o_s,
    ot_s,
    pt_s,
    a1_s,
    a1t_s,
    a2_s,
    a2t_s,
    gm_s,
    gmt_s,
    go_s,
    gq_s,
    gk_s,
    gv_s,
    aq,
    ak,
    av,
    ao,
    aup,
    adt,
    aemb,
    emb_s,
):
    step = pl.program_id(0)
    last = pl.num_programs(0) - 1
    slabs = slab_ref.shape[0]
    dr, er = DW // slabs, EW // slabs

    def weight(i):
        return slab_ref[:, i * dr : (i + 1) * dr].reshape(DW, DW)

    def down(c):
        part = slabs // DEC_CHUNKS
        return slab_ref[pl.ds(c * part, part), 8 * dr : 12 * dr].reshape(DW, DW)

    @pl.when(step == 0)
    def _():
        for ref in (aq, ak, av, ao, aup, adt, aemb, small_o, ghid_o):
            ref[...] = jnp.zeros_like(ref)
        flat_s[...] = jnp.zeros_like(flat_s)
        for d in range(slabs):
            emb_s[pl.ds(d * er, er), :] = slab_ref[d, 12 * dr : 12 * dr + er]

    mask_tok = par_ref[0:1]
    gain1, gain2 = par_ref[1:2], par_ref[2:3]
    sh_emb, sh1, sh2 = par_ref[3:4], par_ref[4:5], par_ref[5:6]
    sh_q, sh_v, sh_o, sh_d = par_ref[6:7], par_ref[7:8], par_ref[8:9], par_ref[9:10]

    for i in range(D_IMGS):
        cells = lax.broadcasted_iota(jnp.int32, (RP, VISIBLE), 0)
        hot = visr_ref[i] == cells
        present = jnp.max(jnp.where(hot, 1.0, 0.0), axis=1, keepdims=True)
        placed = nn(jnp.where(hot, 1.0, 0.0).astype(BF16), recv_ref[i]).astype(BF16)
        z = nn(placed, emb_s[...]) + sh_emb
        xd_s[pl.ds(i * RP, RP), :] = jnp.where(present > 0.5, z, mask_tok) + pos_ref[...]

    xhat1, rstd1 = norm_stats(xd_s[...])
    a1 = (xhat1 * gain1 + sh1).astype(BF16)
    a1_s[...] = a1
    for i_w, bias, dst in ((0, sh_q, q_s), (1, None, k_s), (2, sh_v, v_s)):
        val = nn(a1, weight(i_w))
        val = (val if bias is None else val + bias).astype(BF16)
        for i in range(D_IMGS):
            for g in range(D_HG):
                dst[i * D_HG + g] = val[i * RP : (i + 1) * RP, g * 128 : (g + 1) * 128]
    a1t_s[...] = jnp.transpose(a1_s[...])

    def fwd_body(j, carry):
        def store(h, pt):
            pt_s[j * D_HPG + h] = pt

        ot = attend_fwd(q_s[j], k_s[j], v_s[j], DEC_HEAD, dec_bias, store)
        ot_s[j] = ot.astype(BF16)
        o_s[j] = jnp.transpose(ot).astype(BF16)
        return carry

    lax.fori_loop(0, D_IMGS * D_HG, fwd_body, 0, unroll=4)

    o_full = jnp.concatenate(
        [
            jnp.concatenate([o_s[i * D_HG + g] for g in range(D_HG)], axis=1)
            for i in range(D_IMGS)
        ],
        axis=0,
    )
    x2_s[...] = xd_s[...] + (nn(o_full, weight(3)) + sh_o)
    xhat2, rstd2 = norm_stats(x2_s[...])
    a2 = (xhat2 * gain2 + sh2).astype(BF16)
    a2_s[...] = a2
    a2t_s[...] = jnp.transpose(a2_s[...])

    flat_s[pl.ds(0, D_IMGS * PATCHES), :] = cot_ref[...].astype(F32)
    rows = lax.broadcasted_iota(jnp.int32, (RP, DW), 0)
    for i in range(D_IMGS):
        part = flat_s[pl.ds(i * PATCHES, RP), :]
        gm_s[pl.ds(i * RP, RP), :] = jnp.where(rows < PATCHES, part, 0.0).astype(BF16)
    gmt_s[...] = jnp.transpose(gm_s[...])
    small_o[pl.ds(9, 1), :] += colsum(gm_s[...].astype(F32))

    y_s[...] = x2_s[...] + sh_d
    ga_s[...] = jnp.zeros_like(ga_s)

    def mlp_body(c, carry):
        wup = weight(4 + c)
        wdn = down(c)
        u = nn(a2_s[...], wup) + hid_ref[c]
        hid, dgelu = gelu_both(u)
        hid = hid.astype(BF16)
        y_s[...] += nn(hid, wdn)
        gu = (nt(gm_s[...], wdn) * dgelu).astype(BF16)
        ga_s[...] += nt(gu, wup)
        adt[c] += nn(gmt_s[...], hid)
        aup[c] += nn(a2t_s[...], gu)
        ghid_o[c] += colsum(gu.astype(F32))
        return carry

    for chunk in range(DEC_CHUNKS):
        mlp_body(chunk, 0)

    for i in range(D_IMGS):
        flat_s[pl.ds(i * PATCHES, PATCHES), :] = y_s[pl.ds(i * RP, PATCHES), :]
    out_ref[...] = flat_s[pl.ds(0, D_IMGS * PATCHES), :].astype(BF16)

    ga2 = ga_s[...]
    xhat2, rstd2 = norm_stats(x2_s[...])
    small_o[pl.ds(2, 1), :] += colsum(ga2 * xhat2)
    small_o[pl.ds(5, 1), :] += colsum(ga2)
    gx2 = gm_s[...].astype(F32) + norm_back(xhat2, rstd2, gain2, ga2)
    x2_s[...] = gx2
    gpr = gx2.astype(BF16)
    small_o[pl.ds(8, 1), :] += colsum(gpr.astype(F32))
    go = nt(gpr, weight(3)).astype(BF16)
    for i in range(D_IMGS):
        part = gpr[i * RP : (i + 1) * RP]
        ao[...] += nn(ot_s[pl.ds(i * D_HG, D_HG)].reshape(DW, RP), part)
        for g in range(D_HG):
            go_s[i * D_HG + g] = go[i * RP : (i + 1) * RP, g * 128 : (g + 1) * 128]

    def bwd_body(j, carry):
        gq, gk, gv = attend_bwd(
            q_s[j], k_s[j], v_s[j], go_s[j], DEC_HEAD, lambda h: pt_s[j * D_HPG + h]
        )
        gq_s[j] = gq
        gk_s[j] = gk
        gv_s[j] = gv
        return carry

    lax.fori_loop(0, D_IMGS * D_HG, bwd_body, 0, unroll=4)

    ga1 = None
    for src, i_w, acc, row in ((gq_s, 0, aq, 6), (gk_s, 1, ak, None), (gv_s, 2, av, 7)):
        full = jnp.concatenate(
            [
                jnp.concatenate([src[i * D_HG + g] for g in range(D_HG)], axis=1)
                for i in range(D_IMGS)
            ],
            axis=0,
        )
        if row is not None:
            small_o[pl.ds(row, 1), :] += colsum(full.astype(F32))
        acc[...] += nn(a1t_s[...], full)
        part = nt(full, weight(i_w))
        ga1 = part if ga1 is None else ga1 + part

    xhat1, rstd1 = norm_stats(xd_s[...])
    small_o[pl.ds(1, 1), :] += colsum(ga1 * xhat1)
    small_o[pl.ds(4, 1), :] += colsum(ga1)
    y_s[...] = x2_s[...] + norm_back(xhat1, rstd1, gain1, ga1)

    for i in range(D_IMGS):
        gx = y_s[pl.ds(i * RP, RP), :]
        cells = lax.broadcasted_iota(jnp.int32, (RP, VISIBLE), 0)
        hot = visr_ref[i] == cells
        present = jnp.max(jnp.where(hot, 1.0, 0.0), axis=1, keepdims=True)
        small_o[pl.ds(0, 1), :] += colsum(jnp.where(present > 0.5, 0.0, gx))
        cells_t = lax.broadcasted_iota(jnp.int32, (64, RP), 1)
        hot_t = jnp.where(visc_ref[i] == cells_t, 1.0, 0.0).astype(BF16)
        gz = nn(hot_t, gx.astype(BF16)).astype(BF16)
        small_o[pl.ds(3, 1), :] += colsum(gz.astype(F32))
        aemb[...] += lax.dot_general(
            recv_ref[i], gz[:VISIBLE], (((0,), (0,)), ((), ())), preferred_element_type=F32
        )
        gyl_ref[i] = nt(gz, emb_s[...])[:VISIBLE].astype(BF16)

    @pl.when(step == last)
    def _():
        n = slabs
        for i, ref in enumerate((aq, ak, av, ao)):
            grad_o[:, i * dr : (i + 1) * dr] = ref[...].reshape(n, dr, DW).astype(BF16)
        part = n // DEC_CHUNKS
        for c in range(DEC_CHUNKS):
            first = (4 + c) * dr
            grad_o[:, first : first + dr] = aup[c].reshape(n, dr, DW).astype(BF16)
            gdn = jnp.transpose(adt[c]).reshape(part, 4 * dr, DW)
            grad_o[c * part : (c + 1) * part, 8 * dr : 12 * dr] = gdn.astype(BF16)
        grad_o[:, 12 * dr :] = aemb[...].reshape(n, er, DW).astype(BF16)


def whole(shape):
    zeros = (0,) * len(shape)
    return pl.BlockSpec(shape, lambda *_: zeros, pipeline_mode=pl.Buffered(1))


def decoder(recv, visible, cot, pos, par, hid, slab):
    images = recv.shape[0]
    n = slab.shape[0]
    visr = visible.reshape(images, 1, VISIBLE)
    visc = jnp.pad(visible, ((0, 0), (0, 64 - VISIBLE)), constant_values=-1).reshape(images, 64, 1)
    f, b = F32, BF16
    vm = pltpu.VMEM
    grp = D_IMGS * D_HG
    ins = [
        pl.BlockSpec((D_IMGS, VISIBLE, EW), lambda i: (i, 0, 0)),
        pl.BlockSpec((D_IMGS, 1, VISIBLE), lambda i: (i, 0, 0)),
        pl.BlockSpec((D_IMGS, 64, 1), lambda i: (i, 0, 0)),
        pl.BlockSpec((D_IMGS * PATCHES, DW), lambda i: (i, 0)),
    ] + [whole(a.shape) for a in (pos, par, hid, slab)]
    outs = [
        jax.ShapeDtypeStruct((images * PATCHES, DW), b),
        jax.ShapeDtypeStruct((images, VISIBLE, EW), b),
        jax.ShapeDtypeStruct((16, DW), f),
        jax.ShapeDtypeStruct((DEC_CHUNKS, 1, DW), f),
        jax.ShapeDtypeStruct((n, (12 * DW + EW) // n, DW), b),
    ]
    out_specs = [
        pl.BlockSpec((D_IMGS * PATCHES, DW), lambda i: (i, 0)),
        pl.BlockSpec((D_IMGS, VISIBLE, EW), lambda i: (i, 0, 0)),
    ] + [whole(o.shape) for o in outs[2:]]
    scratch = [
        vm((DM, DW), f),
        vm((DM, DW), f),
        vm((DM, DW), f),
        vm((DM, DW), f),
        vm((D_IMGS * PATCHES + 24, DW), f),
        vm((grp, RP, 128), b),
        vm((grp, RP, 128), b),
        vm((grp, RP, 128), b),
        vm((grp, RP, 128), b),
        vm((grp, 128, RP), b),
        vm((grp * D_HPG, RP, RP), b),
        vm((DM, DW), b),
        vm((DW, DM), b),
        vm((DM, DW), b),
        vm((DW, DM), b),
        vm((DM, DW), b),
        vm((DW, DM), b),
        vm((grp, RP, 128), b),
        vm((grp, RP, 128), b),
        vm((grp, RP, 128), b),
        vm((grp, RP, 128), b),
        vm((DW, DW), f),
        vm((DW, DW), f),
        vm((DW, DW), f),
        vm((DW, DW), f),
        vm((DEC_CHUNKS, DW, DW), f),
        vm((DEC_CHUNKS, DW, DW), f),
        vm((EW, DW), f),
        vm((EW, DW), b),
    ]
    return pl.pallas_call(
        dec_kernel,
        grid=(images // D_IMGS,),
        in_specs=ins,
        out_specs=out_specs,
        out_shape=outs,
        scratch_shapes=scratch,
        compiler_params=pltpu.CompilerParams(
            dimension_semantics=("arbitrary",), vmem_limit_bytes=60 << 20
        ),
        cost_estimate=pl.CostEstimate(
            flops=225 * 10**9, transcendentals=0, bytes_accessed=250 * 10**6
        ),
        name="decoder",
    )(recv, visr, visc, cot, pos, par, hid, slab)


EM = ENC_GROUPS * RP
E_HB = 3
E_J = ENC_GROUPS * 2
E_HPG = 128 // ENC_HEAD
GROUP_IMGS = IMG_DEV // ENC_GROUPS
WIN = 56


def seg_of(i):
    return (
        jnp.where(i >= VISIBLE, 1, 0)
        + jnp.where(i >= 2 * VISIBLE, 1, 0)
        + jnp.where(i >= 3 * VISIBLE, 1, 0)
        + jnp.where(i >= 4 * VISIBLE, 1, 0)
    )


def enc_attn_kernel(
    start_ref,
    x_ref,
    par_ref,
    parb_ref,
    wq_ref,
    wk_ref,
    wv_ref,
    wo_ref,
    xc_o,
    q_o,
    k_o,
    v_o,
    pt_o,
    ot_o,
    x2_o,
    xf_s,
    xc_s,
    a1_s,
    o_s,
    bias_s,
):
    step = pl.program_id(0)

    @pl.when(step == 0)
    def _():
        xf_s[pl.ds(0, ROWS_DEV), :] = x_ref[...].astype(F32)
        for grp in range(ENC_GROUPS):
            xc_s[pl.ds(grp * RP + PATCHES, RP - PATCHES), :] = jnp.zeros((RP - PATCHES, EW), F32)
            for i in range(GROUP_IMGS):
                start = start_ref[grp * GROUP_IMGS + i]
                shift = lax.rem(start, 8)
                base = pl.multiple_of(start - shift, 8)
                part = pltpu.roll(xf_s[pl.ds(base, WIN), :], WIN - shift, 0)
                xc_s[pl.ds(grp * RP + i * VISIBLE, VISIBLE), :] = part[:VISIBLE]
        x = xc_s[...]
        xc_o[...] = x.astype(BF16)
        xhat, _ = norm_stats(x)
        a1_s[...] = (xhat * par_ref[0:1] + par_ref[2:3]).astype(BF16)
        x2_o[...] = x + par_ref[6:7]
        keys = lax.broadcasted_iota(jnp.int32, (RP, RP), 0)
        queries = lax.broadcasted_iota(jnp.int32, (RP, RP), 1)
        same = (seg_of(keys) == seg_of(queries)) & (keys < PATCHES)
        bias_s[...] = jnp.where(same, 0.0, NEG)

    for w_ref, row, dst in ((wq_ref, 4, q_o), (wk_ref, None, k_o), (wv_ref, 5, v_o)):
        val = nn(a1_s[...], w_ref[...])
        if row is not None:
            val = val + parb_ref[row : row + 1]
        val = val.astype(BF16)
        for grp in range(ENC_GROUPS):
            for half in range(2):
                dst[0, grp * 2 + half] = val[
                    grp * RP : (grp + 1) * RP, half * 128 : (half + 1) * 128
                ]

    def loop(j, carry):
        def store(h, pt):
            pt_o[0, j * E_HPG + h] = pt

        ot = attend_fwd(
            q_o[0, j], k_o[0, j], v_o[0, j], ENC_HEAD, lambda st: st + bias_s[...], store
        )
        ot_o[0, j] = ot.astype(BF16)
        o_s[j] = jnp.transpose(ot).astype(BF16)
        return carry

    lax.fori_loop(0, E_J, loop, 0, unroll=4)
    o_full = jnp.concatenate(
        [
            jnp.concatenate([o_s[grp * 2], o_s[grp * 2 + 1]], axis=1)
            for grp in range(ENC_GROUPS)
        ],
        axis=0,
    )
    x2_o[...] += nn(o_full, wo_ref[...])


def enc_attn(starts, x, par, wq, wk, wv, wo):
    f, b = F32, BF16
    vm = pltpu.VMEM
    col = pl.BlockSpec((EW, 256), lambda i, s: (0, i))
    row = pl.BlockSpec((256, EW), lambda i, s: (i, 0))
    grp = pl.BlockSpec((1, E_J, RP, 128), lambda i, s: (i, 0, 0, 0))
    outs = [
        (jax.ShapeDtypeStruct((EM, EW), b), whole((EM, EW))),
        (jax.ShapeDtypeStruct((E_HB, E_J, RP, 128), b), grp),
        (jax.ShapeDtypeStruct((E_HB, E_J, RP, 128), b), grp),
        (jax.ShapeDtypeStruct((E_HB, E_J, RP, 128), b), grp),
        (
            jax.ShapeDtypeStruct((E_HB, E_J * E_HPG, RP, RP), b),
            pl.BlockSpec((1, E_J * E_HPG, RP, RP), lambda i, s: (i, 0, 0, 0)),
        ),
        (
            jax.ShapeDtypeStruct((E_HB, E_J, 128, RP), b),
            pl.BlockSpec((1, E_J, 128, RP), lambda i, s: (i, 0, 0, 0)),
        ),
        (jax.ShapeDtypeStruct((EM, EW), f), whole((EM, EW))),
    ]
    return pl.pallas_call(
        enc_attn_kernel,
        grid_spec=pltpu.PrefetchScalarGridSpec(
            num_scalar_prefetch=1,
            grid=(E_HB,),
            in_specs=[
                whole(x.shape),
                whole(par.shape),
                pl.BlockSpec((8, 256), lambda i, s: (0, i)),
                col,
                col,
                col,
                row,
            ],
            out_specs=[o[1] for o in outs],
            scratch_shapes=[
                vm((ROWS_DEV + 16, EW), f),
                vm((EM, EW), f),
                vm((EM, EW), b),
                vm((E_J, RP, 128), b),
                vm((RP, RP), f),
            ],
        ),
        out_shape=[o[0] for o in outs],
        compiler_params=pltpu.CompilerParams(
            dimension_semantics=("arbitrary",), vmem_limit_bytes=60 << 20
        ),
        cost_estimate=pl.CostEstimate(
            flops=27 * 10**9, transcendentals=0, bytes_accessed=30 * 10**6
        ),
        name="enc_attn",
    )(starts, x, par, par, wq, wk, wv, wo)


def enc_mlp_kernel(
    x2_ref, par_ref, hid_ref, wup_ref, wdn_ref, yl_o, hid_o, dg_o, a2_s, y_s
):
    step = pl.program_id(0)

    @pl.when(step == 0)
    def _():
        x2 = x2_ref[...]
        xhat, _ = norm_stats(x2)
        a2_s[...] = (xhat * par_ref[1:2] + par_ref[3:4]).astype(BF16)
        y_s[...] = x2 + par_ref[7:8]

    u = nn(a2_s[...], wup_ref[0]) + hid_ref[0]
    hid, dgelu = gelu_both(u)
    hid = hid.astype(BF16)
    hid_o[0] = hid
    dg_o[0] = dgelu.astype(BF16)
    y_s[...] += nn(hid, wdn_ref[0])

    @pl.when(step == pl.num_programs(0) - 1)
    def _():
        for grp in range(ENC_GROUPS):
            for i in range(GROUP_IMGS):
                part = y_s[pl.ds(grp * RP + i * VISIBLE, VISIBLE), :]
                yl_o[grp * GROUP_IMGS + i] = part.astype(BF16)


def enc_mlp(x2, par, hid, wup, wdn):
    f, b = F32, BF16
    chunk = pl.BlockSpec((1, EM, EW), lambda i: (i, 0, 0))
    wchunk = pl.BlockSpec((1, EW, EW), lambda i: (i, 0, 0))
    outs = [
        (jax.ShapeDtypeStruct((IMG_DEV, VISIBLE, EW), b), whole((IMG_DEV, VISIBLE, EW))),
        (jax.ShapeDtypeStruct((ENC_CHUNKS, EM, EW), b), chunk),
        (jax.ShapeDtypeStruct((ENC_CHUNKS, EM, EW), b), chunk),
    ]
    return pl.pallas_call(
        enc_mlp_kernel,
        grid=(ENC_CHUNKS,),
        in_specs=[
            whole(x2.shape),
            whole(par.shape),
            pl.BlockSpec((1, 1, EW), lambda i: (i, 0, 0)),
            wchunk,
            wchunk,
        ],
        out_specs=[o[1] for o in outs],
        out_shape=[o[0] for o in outs],
        scratch_shapes=[pltpu.VMEM((EM, EW), b), pltpu.VMEM((EM, EW), f)],
        compiler_params=pltpu.CompilerParams(
            dimension_semantics=("arbitrary",), vmem_limit_bytes=60 << 20
        ),
        cost_estimate=pl.CostEstimate(
            flops=21 * 10**9, transcendentals=0, bytes_accessed=24 * 10**6
        ),
        name="enc_mlp",
    )(x2, par, hid, wup, wdn)


def enc_mlp_back_kernel(
    gy_ref,
    x2_ref,
    par_ref,
    hid_ref,
    dg_ref,
    wup_ref,
    wdn_ref,
    gx2_o,
    small_o,
    ghid_o,
    grad_o,
    gf_s,
    gm_s,
    a2t_s,
    ga_s,
    up_s,
    dn_s,
    sems,
):
    step = pl.program_id(0)

    @pl.when(step == 0)
    def _():
        for grp in range(ENC_GROUPS):
            gf_s[pl.ds(grp * RP + PATCHES, RP - PATCHES), :] = jnp.zeros((RP - PATCHES, EW), F32)
            for i in range(GROUP_IMGS):
                part = gy_ref[grp * GROUP_IMGS + i].astype(F32)
                gf_s[pl.ds(grp * RP + i * VISIBLE, VISIBLE), :] = part
        gm_s[...] = gf_s[...].astype(BF16)
        xhat, _ = norm_stats(x2_ref[...])
        a2 = (xhat * par_ref[1:2] + par_ref[3:4]).astype(BF16)
        a2t_s[...] = jnp.transpose(a2)
        ga_s[...] = jnp.zeros_like(ga_s)
        small_o[...] = jnp.zeros_like(small_o)
        small_o[pl.ds(7, 1), :] = colsum(gf_s[...])

    gu = (nt(gm_s[...], wdn_ref[0]) * dg_ref[0].astype(F32)).astype(BF16)
    ga_s[...] += nt(gu, wup_ref[0])
    n, er, _ = up_s.shape
    part = n // ENC_CHUNKS
    first = pl.multiple_of(step * er, 8)
    copies = (
        pltpu.make_async_copy(up_s, grad_o.at[:, pl.ds(first, er), :], sems.at[0]),
        pltpu.make_async_copy(
            dn_s, grad_o.at[pl.ds(step * part, part), pl.ds(4 * er, 4 * er), :], sems.at[1]
        ),
    )

    @pl.when(step > 0)
    def _():
        for copy in copies:
            copy.wait()

    up_s[...] = nn(a2t_s[...], gu).reshape(n, er, EW).astype(BF16)
    down = nn(jnp.transpose(hid_ref[0]), gm_s[...])
    dn_s[...] = down.reshape(part, 4 * er, EW).astype(BF16)
    for copy in copies:
        copy.start()
    ghid_o[0] = colsum(gu.astype(F32))

    @pl.when(step == pl.num_programs(0) - 1)
    def _():
        for copy in copies:
            copy.wait()
        ga2 = ga_s[...]
        xhat, rstd = norm_stats(x2_ref[...])
        small_o[pl.ds(1, 1), :] = colsum(ga2 * xhat)
        small_o[pl.ds(3, 1), :] = colsum(ga2)
        gx2 = gf_s[...] + norm_back(xhat, rstd, par_ref[1:2], ga2)
        gx2_o[...] = gx2
        small_o[pl.ds(6, 1), :] = colsum(gx2.astype(BF16).astype(F32))


def enc_mlp_back(n, gy, x2, par, hid, dg, wup, wdn):
    f, b = F32, BF16
    er = EW // n
    chunk = pl.BlockSpec((1, EM, EW), lambda i: (i, 0, 0))
    wchunk = pl.BlockSpec((1, EW, EW), lambda i: (i, 0, 0))
    outs = [
        (jax.ShapeDtypeStruct((EM, EW), f), whole((EM, EW))),
        (jax.ShapeDtypeStruct((8, EW), f), whole((8, EW))),
        (
            jax.ShapeDtypeStruct((ENC_CHUNKS, 1, EW), f),
            pl.BlockSpec((1, 1, EW), lambda i: (i, 0, 0)),
        ),
        (jax.ShapeDtypeStruct((n, 8 * er, EW), b), pl.BlockSpec(memory_space=pl.ANY)),
    ]
    return pl.pallas_call(
        enc_mlp_back_kernel,
        grid=(ENC_CHUNKS,),
        in_specs=[whole(gy.shape), whole(x2.shape), whole(par.shape), chunk, chunk, wchunk, wchunk],
        out_specs=[o[1] for o in outs],
        out_shape=[o[0] for o in outs],
        scratch_shapes=[
            pltpu.VMEM((EM, EW), f),
            pltpu.VMEM((EM, EW), b),
            pltpu.VMEM((EW, EM), b),
            pltpu.VMEM((EM, EW), f),
            pltpu.VMEM((n, er, EW), b),
            pltpu.VMEM((n // ENC_CHUNKS, 4 * er, EW), b),
            pltpu.SemaphoreType.DMA((2,)),
        ],
        compiler_params=pltpu.CompilerParams(
            dimension_semantics=("arbitrary",), vmem_limit_bytes=60 << 20
        ),
        cost_estimate=pl.CostEstimate(
            flops=25 * 10**9, transcendentals=0, bytes_accessed=28 * 10**6
        ),
        name="enc_mlp_back",
    )(gy, x2, par, hid, dg, wup, wdn)


def enc_attn_back_kernel(
    start_ref,
    gx2_ref,
    xc_ref,
    par_ref,
    q_ref,
    k_ref,
    v_ref,
    pt_ref,
    ot_ref,
    wq_ref,
    wk_ref,
    wv_ref,
    wo_ref,
    gx_o,
    gwq_o,
    gwk_o,
    gwv_o,
    gwo_o,
    small_o,
    gb_o,
    gpr_s,
    a1t_s,
    ga_s,
    go_s,
    gq_s,
    gk_s,
    gv_s,
    gf_s,
):
    step = pl.program_id(0)

    @pl.when(step == 0)
    def _():
        gpr_s[...] = gx2_ref[...].astype(BF16)
        xhat, _ = norm_stats(xc_ref[...].astype(F32))
        a1 = (xhat * par_ref[0:1] + par_ref[2:3]).astype(BF16)
        a1t_s[...] = jnp.transpose(a1)
        ga_s[...] = jnp.zeros_like(ga_s)
        small_o[...] = jnp.zeros_like(small_o)

    go = nt(gpr_s[...], wo_ref[...]).astype(BF16)
    for half in range(2):
        acc = None
        for grp in range(ENC_GROUPS):
            rows = slice(grp * RP, (grp + 1) * RP)
            go_s[grp * 2 + half] = go[rows, half * 128 : (half + 1) * 128]
            part = nn(ot_ref[0, grp * 2 + half], gpr_s[pl.ds(grp * RP, RP), :])
            acc = part if acc is None else acc + part
        gwo_o[pl.ds(half * 128, 128), :] = acc.astype(BF16)

    def loop(j, carry):
        gq, gk, gv = attend_bwd(
            q_ref[0, j],
            k_ref[0, j],
            v_ref[0, j],
            go_s[j],
            ENC_HEAD,
            lambda h: pt_ref[0, j * E_HPG + h],
        )
        gq_s[j] = gq
        gk_s[j] = gk
        gv_s[j] = gv
        return carry

    lax.fori_loop(0, E_J, loop, 0, unroll=4)
    gb_o[...] = jnp.zeros_like(gb_o)
    ga1 = ga_s[...]
    for src, w_ref, dst, row in (
        (gq_s, wq_ref, gwq_o, 4),
        (gk_s, wk_ref, gwk_o, None),
        (gv_s, wv_ref, gwv_o, 5),
    ):
        full = jnp.concatenate(
            [
                jnp.concatenate([src[grp * 2], src[grp * 2 + 1]], axis=1)
                for grp in range(ENC_GROUPS)
            ],
            axis=0,
        )
        if row is not None:
            gb_o[pl.ds(row, 1), :] = colsum(full.astype(F32))
        dst[...] = nn(a1t_s[...], full).astype(BF16)
        ga1 = ga1 + nt(full, w_ref[...])
    ga_s[...] = ga1

    @pl.when(step == pl.num_programs(0) - 1)
    def _():
        ga = ga_s[...]
        xhat, rstd = norm_stats(xc_ref[...].astype(F32))
        small_o[pl.ds(0, 1), :] = colsum(ga * xhat)
        small_o[pl.ds(2, 1), :] = colsum(ga)
        ga_s[...] = gx2_ref[...] + norm_back(xhat, rstd, par_ref[0:1], ga)
        gf_s[...] = jnp.zeros_like(gf_s)
        rows = lax.broadcasted_iota(jnp.int32, (WIN, EW), 0)
        for grp in range(ENC_GROUPS):
            for i in range(GROUP_IMGS):
                start = start_ref[grp * GROUP_IMGS + i]
                shift = lax.rem(start, 8)
                base = pl.multiple_of(start - shift, 8)
                first = grp * RP + i * VISIBLE
                part = jnp.where(rows < VISIBLE, ga_s[pl.ds(first, WIN), :], 0.0)
                gf_s[pl.ds(base, WIN), :] += pltpu.roll(part, shift, 0)
        gx_o[...] = gf_s[pl.ds(0, ROWS_DEV), :]


def enc_attn_back(starts, gx2, xc, par, q, k, v, pt, ot, wq, wk, wv, wo):
    f, b = F32, BF16
    vm = pltpu.VMEM
    col = pl.BlockSpec((EW, 256), lambda i, s: (0, i))
    row = pl.BlockSpec((256, EW), lambda i, s: (i, 0))
    grp = pl.BlockSpec((1, E_J, RP, 128), lambda i, s: (i, 0, 0, 0))
    square = jax.ShapeDtypeStruct((EW, EW), b)
    outs = [
        (jax.ShapeDtypeStruct((ROWS_DEV, EW), f), whole((ROWS_DEV, EW))),
        (square, col),
        (square, col),
        (square, col),
        (square, row),
        (jax.ShapeDtypeStruct((8, EW), f), whole((8, EW))),
        (jax.ShapeDtypeStruct((8, EW), f), pl.BlockSpec((8, 256), lambda i, s: (0, i))),
    ]
    return pl.pallas_call(
        enc_attn_back_kernel,
        grid_spec=pltpu.PrefetchScalarGridSpec(
            num_scalar_prefetch=1,
            grid=(E_HB,),
            in_specs=[
                whole(gx2.shape),
                whole(xc.shape),
                whole(par.shape),
                grp,
                grp,
                grp,
                pl.BlockSpec((1, E_J * E_HPG, RP, RP), lambda i, s: (i, 0, 0, 0)),
                pl.BlockSpec((1, E_J, 128, RP), lambda i, s: (i, 0, 0, 0)),
                col,
                col,
                col,
                row,
            ],
            out_specs=[o[1] for o in outs],
            scratch_shapes=[
                vm((EM, EW), b),
                vm((EW, EM), b),
                vm((EM, EW), f),
                vm((E_J, RP, 128), b),
                vm((E_J, RP, 128), b),
                vm((E_J, RP, 128), b),
                vm((E_J, RP, 128), b),
                vm((ROWS_DEV + 16, EW), f),
            ],
        ),
        out_shape=[o[0] for o in outs],
        compiler_params=pltpu.CompilerParams(
            dimension_semantics=("arbitrary",), vmem_limit_bytes=60 << 20
        ),
        cost_estimate=pl.CostEstimate(
            flops=36 * 10**9, transcendentals=0, bytes_accessed=40 * 10**6
        ),
        name="enc_attn_back",
    )(starts, gx2, xc, par, q, k, v, pt, ot, wq, wk, wv, wo)


def position_rows():
    quarter = DW // 4
    frequency = 1.0 / 10000.0 ** (np.arange(quarter) / quarter)
    cells = np.arange(PATCHES)
    by_row = (cells // SIDE)[:, None] * frequency[None, :]
    by_col = (cells % SIDE)[:, None] * frequency[None, :]
    table = np.concatenate([np.sin(by_row), np.cos(by_row), np.sin(by_col), np.cos(by_col)], axis=1)
    return np.pad(table, ((0, RP - PATCHES), (0, 0))).astype(np.float32)


def small_rows(parts, width):
    flat = jnp.concatenate([p.reshape(-1) for p in parts])
    return jnp.pad(flat, (0, 8 * width - flat.shape[0])).reshape(8, width)


def col_blocks(w, width):
    return [w[:, i : i + width] for i in range(0, w.shape[1], width)]


def per_device(v, n):
    rows = v.shape[0]
    return v.reshape(rows, n, -1).transpose(1, 0, 2).reshape(n, -1)


def all_devices(v, rows):
    n = v.shape[0]
    return v.reshape(n, rows, -1).transpose(1, 0, 2).reshape(rows, -1)


def pairs(count, minor, flip_major, flip_minor):
    return [
        (i, (i // minor ^ flip_major) * minor + (i % minor ^ flip_minor)) for i in range(count)
    ]


def send(v, sizes, flip_dp=0, flip_fsdp=0):
    dp, fsdp = sizes
    return lax.ppermute(v, BOTH, pairs(dp * fsdp, fsdp, flip_dp, flip_fsdp))


def gather_fsdp(v, sizes):
    fsdp = sizes[1]
    me = lax.axis_index("fsdp")
    parts = [v] + [send(v, sizes, 0, k) for k in range(1, fsdp)]
    bit = 1
    while bit < fsdp:
        odd = (me & bit) != 0
        parts = [jnp.where(odd, parts[i ^ bit], parts[i]) for i in range(fsdp)]
        bit *= 2
    return jnp.stack(parts)


def gather_dp(block):
    _, rows, width = block.shape
    full = lax.all_gather(block.reshape(-1, width), "dp", axis=0, tiled=True)
    return full.reshape(-1, rows, width)


def pick(v, index, axis=0):
    return lax.dynamic_index_in_dim(v, index, axis, keepdims=False)


def spread_fsdp(v, sizes):
    me = lax.axis_index("fsdp")
    others = [send(pick(v, me ^ k), sizes, 0, k) for k in range(1, sizes[1])]
    return pick(v, me), others


def total(mine, others):
    mine = mine.astype(F32)
    for other in others:
        mine = mine + other.astype(F32)
    return mine


def scatter_dp(packed, sizes):
    n, rows, width = packed.shape
    flat = lax.psum_scatter(
        packed.reshape(n * rows, width), "dp", scatter_dimension=0, tiled=True
    )
    return flat.reshape(sizes[1], rows, width)


def halves(v, sizes, axis, bit):
    mine = (lax.axis_index("dp") // bit) % 2
    return pick(v, mine, axis), send(pick(v, 1 - mine, axis), sizes, bit, 0)


def add(pair):
    return (pair[0].astype(F32) + pair[1].astype(F32)).astype(BF16)


def low_high(lows, highs, sizes, step):
    left = sizes[0].bit_length() - 2 - step
    return (
        halves(lows, sizes, left - 1, 2 ** (step + 1)),
        halves(highs, sizes, 0, 2 ** left),
    )


def make_body(sizes):
    n = sizes[0] * sizes[1]
    bits = sizes[0].bit_length() - 1
    er, dr = EW // n, DW // n

    def body(
        patches,
        segments,
        send_slot,
        visible,
        enc_gain,
        enc_shift,
        enc_hidden,
        enc_qkv,
        enc_out,
        enc_up,
        enc_down,
        embedding,
        mask_token,
        dec_gain,
        dec_shift,
        dec_hidden,
        dec_qkv,
        dec_out,
        dec_up,
        dec_down,
        cotangent,
    ):
        pack_a = jnp.concatenate(
            col_blocks(enc_qkv, EW) + [enc_out, small_rows((enc_gain, enc_shift, enc_hidden), EW)]
        )
        pack_b = jnp.concatenate(col_blocks(enc_up, EW) + [enc_down])
        pack_d = jnp.concatenate(
            col_blocks(dec_qkv, DW)
            + [dec_out]
            + col_blocks(dec_up, DW)
            + [
                dec_down,
                embedding,
                small_rows((mask_token, dec_gain, dec_shift, dec_hidden), DW),
            ]
        )
        block_a = gather_fsdp(pack_a, sizes)
        block_a, pack_b = lax.optimization_barrier((block_a, pack_b))
        full_a = gather_dp(block_a)
        block_b = gather_fsdp(pack_b, sizes)
        full_b = gather_dp(block_b)
        full_a, pack_d = lax.optimization_barrier((full_a, pack_d))
        block_d = gather_fsdp(pack_d, sizes)
        full_d = gather_dp(block_d)

        wq, wk, wv, wo = [full_a[:, i * er : (i + 1) * er].reshape(EW, EW) for i in range(4)]
        small = full_a[:, 4 * er :].reshape(n, -1).astype(F32)
        par = all_devices(small[:, : 8 * er], 8)
        hid = small[:, 8 * er : 12 * er].reshape(ENC_CHUNKS, 1, EW)
        wup = full_b[:, : 4 * er].reshape(n, 4, er, EW).transpose(1, 0, 2, 3).reshape(4, EW, EW)
        wdn = full_b[:, 4 * er :].reshape(4, EW, EW)

        row_ids = jnp.arange(ROWS_DEV, dtype=jnp.int32)
        image_ids = jnp.arange(IMG_DEV, dtype=jnp.int32)
        starts = jnp.min(
            jnp.where(segments[None, :] == image_ids[:, None], row_ids[None, :], ROWS_DEV), axis=1
        )
        hot = send_slot[0][None, :] == image_ids[:, None]
        slot_starts = jnp.sum(jnp.where(hot, starts[None, :], 0), axis=1).astype(jnp.int32)

        xc, q, k, v, pt, ot, x2 = enc_attn(slot_starts, patches, par, wq, wk, wv, wo)
        outgoing, hidden, dgelu = enc_mlp(x2, par, hid, wup, wdn)
        received = lax.all_to_all(outgoing, "dp", split_axis=0, concat_axis=0, tiled=True)

        dsmall = full_d[:, 12 * dr + er :].reshape(n, -1).astype(F32)
        dpar = jnp.concatenate([all_devices(dsmall[:, : 10 * dr], 10), jnp.zeros((6, DW), F32)])
        dhid = dsmall[:, 10 * dr : 14 * dr].reshape(DEC_CHUNKS, 1, DW)
        pos = jnp.asarray(position_rows())

        whole_slabs = er % 8 == 0 and dr % 8 == 0
        slabs = n if whole_slabs else 32
        pieces_d = [DW] * 8 + [4 * DW, EW]

        def regroup(v, pieces, count):
            if v.shape[0] == count:
                return v
            outs, at = [], 0
            for total_rows in pieces:
                rows = total_rows // v.shape[0]
                outs.append(v[:, at : at + rows].reshape(count, -1, v.shape[-1]))
                at += rows
            return jnp.concatenate(outs, axis=1)

        decoded, gyl, gdsmall, gdhid, dpacked = decoder(
            received, visible, cotangent, pos, dpar, dhid, regroup(full_d, pieces_d, slabs)
        )
        returned = lax.all_to_all(gyl, "dp", split_axis=0, concat_axis=0, tiled=True)

        def rows_of(v, width):
            return v.reshape(n, -1, width)

        def small_pack(vals, width):
            flat = jnp.concatenate(vals, axis=1)
            flat = jnp.pad(flat, ((0, 0), (0, 8 * width - flat.shape[1])))
            return flat.astype(BF16).reshape(n, 8, width)

        dpacked = regroup(dpacked, pieces_d, n)
        dpart = scatter_dp(dpacked, sizes)
        gx2, sm1, ghid, bpacked = enc_mlp_back(
            slabs, returned, x2, par, hidden, dgelu, wup, wdn
        )
        bpacked = regroup(bpacked, [EW] * 4 + [4 * EW], n)
        bpart = scatter_dp(bpacked, sizes)
        gx, gwq, gwk, gwv, gwo, sm2, gb = enc_attn_back(
            slot_starts, gx2, xc, par, q, k, v, pt, ot, wq, wk, wv, wo
        )
        apacked = jnp.concatenate(
            [rows_of(g, EW) for g in (gwq, gwk, gwv, gwo)]
            + [
                small_pack(
                    [
                        per_device(sm1 + sm2 + gb, n),
                        ghid.reshape(n, -1),
                        per_device(gdsmall[:10], n),
                        gdhid.reshape(n, -1),
                    ],
                    EW,
                )
            ],
            axis=1,
        )
        barrier = lax.optimization_barrier
        apart = add(halves(apacked.reshape((2,) * bits + (sizes[1], -1, EW)), sizes, bits - 1, 1))
        apart, dpart = barrier((apart, dpart))
        acut = apart.shape[-2] // 16 * 8
        alow, ahigh = apart[..., :acut, :], apart[..., acut:, :]
        for step in range(bits - 1):
            pairs_a = low_high(alow, ahigh, sizes, step)
            if step == 0:
                spread_d = spread_fsdp(dpart, sizes)
                pairs_a, spread_d = barrier((pairs_a, spread_d))
            alow, ahigh = add(pairs_a[0]), add(pairs_a[1])
        dsum = total(*spread_d)
        spread_a = spread_fsdp(jnp.concatenate([alow, ahigh], axis=-2), sizes)
        spread_a, bpart = barrier((spread_a, bpart))
        asum = total(*spread_a)
        bsum = total(*spread_fsdp(bpart, sizes))

        def cut(v, r, count, first=0):
            return jnp.concatenate(
                [v[(first + i) * r : (first + i + 1) * r] for i in range(count)], axis=1
            )

        esm = asum[4 * er :].reshape(-1)
        dsm = esm[12 * er :]
        return (
            decoded,
            gx,
            esm[: 2 * er].reshape(2, er),
            esm[2 * er : 8 * er].reshape(6, er),
            esm[8 * er : 12 * er],
            cut(asum, er, 3),
            asum[3 * er : 4 * er],
            cut(bsum, er, 4),
            bsum[4 * er :],
            dsum[12 * dr : 12 * dr + er],
            dsm[:dr],
            dsm[dr : 3 * dr].reshape(2, dr),
            dsm[3 * dr : 10 * dr].reshape(7, dr),
            dsm[10 * dr : 14 * dr],
            cut(dsum, dr, 3),
            dsum[3 * dr : 4 * dr],
            cut(dsum, dr, 4, 4),
            dsum[8 * dr : 12 * dr],
        )

    return body


def solution(mesh):
    sizes = (mesh.shape["dp"], mesh.shape["fsdp"])
    rows, vec, cols = P(BOTH, None), P(BOTH), P(None, BOTH)
    return jax.shard_map(
        make_body(sizes),
        mesh=mesh,
        in_specs=(rows, vec, rows, rows, cols, cols, vec, rows, rows, rows, rows)
        + (rows, vec, cols, cols, vec, rows, rows, rows, rows, rows),
        out_specs=(rows, rows, cols, cols, vec, rows, rows, rows, rows)
        + (rows, vec, cols, cols, vec, rows, rows, rows, rows),
        check_vma=False,
    )
```

```python
import math

import jax
import jax.numpy as jnp
import numpy as np
from jax import lax
from jax.experimental import pallas as pl
from jax.experimental.pallas import tpu as pltpu
from jax.sharding import PartitionSpec as P

ENC_HEAD = 64
DEC_HEAD = 32
SIDE = 14
VISIBLE = 49
ROWS_DEV = 1024
IMG_DEV = 16
EW = 768
DW = 512
PATCHES = 196
RP = 208
ENC_GROUPS = 4
ENC_CHUNKS = 4
DEC_CHUNKS = 4
NEG = -1e30
F32 = jnp.float32
BF16 = jnp.bfloat16
BOTH = ("dp", "fsdp")
EPS = 1e-06

ERF_P = 0.44
ERF_C = (
    0.2482209555836147,
    0.2488711484441078,
    0.21731375919172816,
    0.21581153367593472,
    -0.020179333598664445,
    0.2966860302544493,
    -0.2779471828654498,
    0.07122327097163224,
)


def nn(a, b):
    return lax.dot_general(a, b, (((1,), (0,)), ((), ())), preferred_element_type=F32)


def nt(a, b):
    return lax.dot_general(a, b, (((1,), (1,)), ((), ())), preferred_element_type=F32)


def colsum(v):
    return jnp.sum(v, axis=0, keepdims=True)


def gelu_both(u):
    t = 1.0 / (1.0 + (ERF_P / math.sqrt(2.0)) * jnp.abs(u))
    r = jnp.full_like(t, 0.5 * ERF_C[-1])
    for coef in ERF_C[-2::-1]:
        r = r * t + 0.5 * coef
    e = jnp.exp2((u * u) * (-0.5 * math.log2(math.e)))
    tail = (r * t) * e
    cdf = jnp.where(u >= 0, 1.0 - tail, tail)
    return u * cdf, cdf + (u * (1.0 / math.sqrt(2.0 * math.pi))) * e


def norm_stats(x):
    center = x - jnp.mean(x, axis=-1, keepdims=True)
    rstd = lax.rsqrt(jnp.mean(center * center, axis=-1, keepdims=True) + EPS)
    return center * rstd, rstd


def norm_back(xhat, rstd, gain, gy):
    d = gy * gain
    m1 = jnp.mean(d, axis=-1, keepdims=True)
    m2 = jnp.mean(d * xhat, axis=-1, keepdims=True)
    return rstd * (d - m1 - xhat * m2)


def lane_mask(shape, h, hd):
    lanes = lax.broadcasted_iota(jnp.int32, shape, 1)
    return (lanes >= h * hd) & (lanes < (h + 1) * hd)


def attend_fwd(q, k, v, hd, bias, pt_store):
    vt = jnp.transpose(v)
    heads = 128 // hd
    zero = jnp.zeros_like(q)
    c = hd ** (-0.5) * math.log2(math.e)
    pts = []
    for h in range(heads):
        sh = bias(nt(k, jnp.where(lane_mask(q.shape, h, hd), q, zero)))
        peak = jnp.max(sh, axis=0, keepdims=True)
        e = jnp.exp2((sh - peak) * c)
        inv = 1.0 / jnp.sum(e, axis=0, keepdims=True)
        pt = (e * inv).astype(BF16)
        pt_store(h, pt)
        pts.append(pt)
    outs = [nn(vt[h * hd : (h + 1) * hd], pts[h]) for h in range(heads)]
    return jnp.concatenate(outs, axis=0)


def attend_bwd(q, k, v, go, hd, pt_load):
    kt = jnp.transpose(k)
    heads = 128 // hd
    zero = jnp.zeros_like(q)
    scale = hd ** (-0.5)
    masks = [lane_mask(q.shape, h, hd) for h in range(heads)]
    vst = jnp.concatenate([jnp.where(m, v, zero) for m in masks], axis=0)
    gpt = nt(vst, go)
    gps = [gpt[h * RP : (h + 1) * RP] for h in range(heads)]
    gsts = []
    pts = [pt_load(h) for h in range(heads)]
    for h in range(heads):
        p32 = pts[h].astype(F32)
        dot = jnp.sum(p32 * gps[h], axis=0, keepdims=True)
        gsts.append((p32 * (gps[h] - dot)).astype(BF16))
    gv = gk = None
    for h in range(heads):
        gvh = nn(pts[h], go)
        gv = gvh if gv is None else jnp.where(masks[h], gvh, gv)
    for h in range(heads):
        gkh = nn(gsts[h], q)
        gk = gkh if gk is None else jnp.where(masks[h], gkh, gk)
    gqt = [nn(kt[h * hd : (h + 1) * hd], gsts[h]) for h in range(heads)]
    gq = jnp.transpose(jnp.concatenate(gqt, axis=0)) * scale
    return gq.astype(BF16), (gk * scale).astype(BF16), gv.astype(BF16)


D_IMGS = 2
DM = D_IMGS * RP
D_HG = DW // 128
D_HPG = 128 // DEC_HEAD


def dec_bias(st):
    head = st[: RP - 16]
    tail = st[RP - 16 :]
    keys = lax.broadcasted_iota(jnp.int32, tail.shape, 0) + (RP - 16)
    return jnp.concatenate([head, jnp.where(keys < PATCHES, tail, NEG)], axis=0)


def dec_kernel(
    recv_ref,
    visr_ref,
    visc_ref,
    cot_ref,
    pos_ref,
    par_ref,
    hid_ref,
    slab_ref,
    out_ref,
    gyl_ref,
    small_o,
    ghid_o,
    grad_o,
    xd_s,
    x2_s,
    y_s,
    ga_s,
    flat_s,
    q_s,
    k_s,
    v_s,
    o_s,
    ot_s,
    pt_s,
    a1_s,
    a1t_s,
    a2_s,
    a2t_s,
    gm_s,
    gmt_s,
    go_s,
    gq_s,
    gk_s,
    gv_s,
    aq,
    ak,
    av,
    ao,
    aup,
    adt,
    aemb,
    emb_s,
):
    step = pl.program_id(0)
    last = pl.num_programs(0) - 1
    slabs = slab_ref.shape[0]
    dr, er = DW // slabs, EW // slabs

    def weight(i):
        return slab_ref[:, i * dr : (i + 1) * dr].reshape(DW, DW)

    def down(c):
        part = slabs // DEC_CHUNKS
        return slab_ref[pl.ds(c * part, part), 8 * dr : 12 * dr].reshape(DW, DW)

    @pl.when(step == 0)
    def _():
        for ref in (aq, ak, av, ao, aup, adt, aemb, small_o, ghid_o):
            ref[...] = jnp.zeros_like(ref)
        flat_s[...] = jnp.zeros_like(flat_s)
        for d in range(slabs):
            emb_s[pl.ds(d * er, er), :] = slab_ref[d, 12 * dr : 12 * dr + er]

    mask_tok = par_ref[0:1]
    gain1, gain2 = par_ref[1:2], par_ref[2:3]
    sh_emb, sh1, sh2 = par_ref[3:4], par_ref[4:5], par_ref[5:6]
    sh_q, sh_v, sh_o, sh_d = par_ref[6:7], par_ref[7:8], par_ref[8:9], par_ref[9:10]

    for i in range(D_IMGS):
        cells = lax.broadcasted_iota(jnp.int32, (RP, VISIBLE), 0)
        hot = visr_ref[i] == cells
        present = jnp.max(jnp.where(hot, 1.0, 0.0), axis=1, keepdims=True)
        placed = nn(jnp.where(hot, 1.0, 0.0).astype(BF16), recv_ref[i]).astype(BF16)
        z = nn(placed, emb_s[...]) + sh_emb
        xd_s[pl.ds(i * RP, RP), :] = jnp.where(present > 0.5, z, mask_tok) + pos_ref[...]

    xhat1, rstd1 = norm_stats(xd_s[...])
    a1 = (xhat1 * gain1 + sh1).astype(BF16)
    a1_s[...] = a1
    for i_w, bias, dst in ((0, sh_q, q_s), (1, None, k_s), (2, sh_v, v_s)):
        val = nn(a1, weight(i_w))
        val = (val if bias is None else val + bias).astype(BF16)
        for i in range(D_IMGS):
            for g in range(D_HG):
                dst[i * D_HG + g] = val[i * RP : (i + 1) * RP, g * 128 : (g + 1) * 128]
    a1t_s[...] = jnp.transpose(a1_s[...])

    def fwd_body(j, carry):
        def store(h, pt):
            pt_s[j * D_HPG + h] = pt

        ot = attend_fwd(q_s[j], k_s[j], v_s[j], DEC_HEAD, dec_bias, store)
        ot_s[j] = ot.astype(BF16)
        o_s[j] = jnp.transpose(ot).astype(BF16)
        return carry

    lax.fori_loop(0, D_IMGS * D_HG, fwd_body, 0, unroll=4)

    o_full = jnp.concatenate(
        [
            jnp.concatenate([o_s[i * D_HG + g] for g in range(D_HG)], axis=1)
            for i in range(D_IMGS)
        ],
        axis=0,
    )
    x2_s[...] = xd_s[...] + (nn(o_full, weight(3)) + sh_o)
    xhat2, rstd2 = norm_stats(x2_s[...])
    a2 = (xhat2 * gain2 + sh2).astype(BF16)
    a2_s[...] = a2
    a2t_s[...] = jnp.transpose(a2_s[...])

    flat_s[pl.ds(0, D_IMGS * PATCHES), :] = cot_ref[...].astype(F32)
    rows = lax.broadcasted_iota(jnp.int32, (RP, DW), 0)
    for i in range(D_IMGS):
        part = flat_s[pl.ds(i * PATCHES, RP), :]
        gm_s[pl.ds(i * RP, RP), :] = jnp.where(rows < PATCHES, part, 0.0).astype(BF16)
    gmt_s[...] = jnp.transpose(gm_s[...])
    small_o[pl.ds(9, 1), :] += colsum(gm_s[...].astype(F32))

    y_s[...] = x2_s[...] + sh_d
    ga_s[...] = jnp.zeros_like(ga_s)

    def mlp_body(c, carry):
        wup = weight(4 + c)
        wdn = down(c)
        u = nn(a2_s[...], wup) + hid_ref[c]
        hid, dgelu = gelu_both(u)
        hid = hid.astype(BF16)
        y_s[...] += nn(hid, wdn)
        gu = (nt(gm_s[...], wdn) * dgelu).astype(BF16)
        ga_s[...] += nt(gu, wup)
        adt[c] += nn(gmt_s[...], hid)
        aup[c] += nn(a2t_s[...], gu)
        ghid_o[c] += colsum(gu.astype(F32))
        return carry

    for chunk in range(DEC_CHUNKS):
        mlp_body(chunk, 0)

    for i in range(D_IMGS):
        flat_s[pl.ds(i * PATCHES, PATCHES), :] = y_s[pl.ds(i * RP, PATCHES), :]
    out_ref[...] = flat_s[pl.ds(0, D_IMGS * PATCHES), :].astype(BF16)

    ga2 = ga_s[...]
    xhat2, rstd2 = norm_stats(x2_s[...])
    small_o[pl.ds(2, 1), :] += colsum(ga2 * xhat2)
    small_o[pl.ds(5, 1), :] += colsum(ga2)
    gx2 = gm_s[...].astype(F32) + norm_back(xhat2, rstd2, gain2, ga2)
    x2_s[...] = gx2
    gpr = gx2.astype(BF16)
    small_o[pl.ds(8, 1), :] += colsum(gpr.astype(F32))
    go = nt(gpr, weight(3)).astype(BF16)
    for i in range(D_IMGS):
        part = gpr[i * RP : (i + 1) * RP]
        ao[...] += nn(ot_s[pl.ds(i * D_HG, D_HG)].reshape(DW, RP), part)
        for g in range(D_HG):
            go_s[i * D_HG + g] = go[i * RP : (i + 1) * RP, g * 128 : (g + 1) * 128]

    def bwd_body(j, carry):
        gq, gk, gv = attend_bwd(
            q_s[j], k_s[j], v_s[j], go_s[j], DEC_HEAD, lambda h: pt_s[j * D_HPG + h]
        )
        gq_s[j] = gq
        gk_s[j] = gk
        gv_s[j] = gv
        return carry

    lax.fori_loop(0, D_IMGS * D_HG, bwd_body, 0, unroll=4)

    ga1 = None
    for src, i_w, acc, row in ((gq_s, 0, aq, 6), (gk_s, 1, ak, None), (gv_s, 2, av, 7)):
        full = jnp.concatenate(
            [
                jnp.concatenate([src[i * D_HG + g] for g in range(D_HG)], axis=1)
                for i in range(D_IMGS)
            ],
            axis=0,
        )
        if row is not None:
            small_o[pl.ds(row, 1), :] += colsum(full.astype(F32))
        acc[...] += nn(a1t_s[...], full)
        part = nt(full, weight(i_w))
        ga1 = part if ga1 is None else ga1 + part

    xhat1, rstd1 = norm_stats(xd_s[...])
    small_o[pl.ds(1, 1), :] += colsum(ga1 * xhat1)
    small_o[pl.ds(4, 1), :] += colsum(ga1)
    y_s[...] = x2_s[...] + norm_back(xhat1, rstd1, gain1, ga1)

    for i in range(D_IMGS):
        gx = y_s[pl.ds(i * RP, RP), :]
        cells = lax.broadcasted_iota(jnp.int32, (RP, VISIBLE), 0)
        hot = visr_ref[i] == cells
        present = jnp.max(jnp.where(hot, 1.0, 0.0), axis=1, keepdims=True)
        small_o[pl.ds(0, 1), :] += colsum(jnp.where(present > 0.5, 0.0, gx))
        cells_t = lax.broadcasted_iota(jnp.int32, (64, RP), 1)
        hot_t = jnp.where(visc_ref[i] == cells_t, 1.0, 0.0).astype(BF16)
        gz = nn(hot_t, gx.astype(BF16)).astype(BF16)
        small_o[pl.ds(3, 1), :] += colsum(gz.astype(F32))
        aemb[...] += lax.dot_general(
            recv_ref[i], gz[:VISIBLE], (((0,), (0,)), ((), ())), preferred_element_type=F32
        )
        gyl_ref[i] = nt(gz, emb_s[...])[:VISIBLE].astype(BF16)

    @pl.when(step == last)
    def _():
        n = slabs
        for i, ref in enumerate((aq, ak, av, ao)):
            grad_o[:, i * dr : (i + 1) * dr] = ref[...].reshape(n, dr, DW).astype(BF16)
        part = n // DEC_CHUNKS
        for c in range(DEC_CHUNKS):
            first = (4 + c) * dr
            grad_o[:, first : first + dr] = aup[c].reshape(n, dr, DW).astype(BF16)
            gdn = jnp.transpose(adt[c]).reshape(part, 4 * dr, DW)
            grad_o[c * part : (c + 1) * part, 8 * dr : 12 * dr] = gdn.astype(BF16)
        grad_o[:, 12 * dr :] = aemb[...].reshape(n, er, DW).astype(BF16)


def whole(shape):
    zeros = (0,) * len(shape)
    return pl.BlockSpec(shape, lambda *_: zeros, pipeline_mode=pl.Buffered(1))


def decoder(recv, visible, cot, pos, par, hid, slab):
    images = recv.shape[0]
    n = slab.shape[0]
    visr = visible.reshape(images, 1, VISIBLE)
    visc = jnp.pad(visible, ((0, 0), (0, 64 - VISIBLE)), constant_values=-1).reshape(images, 64, 1)
    f, b = F32, BF16
    vm = pltpu.VMEM
    grp = D_IMGS * D_HG
    ins = [
        pl.BlockSpec((D_IMGS, VISIBLE, EW), lambda i: (i, 0, 0)),
        pl.BlockSpec((D_IMGS, 1, VISIBLE), lambda i: (i, 0, 0)),
        pl.BlockSpec((D_IMGS, 64, 1), lambda i: (i, 0, 0)),
        pl.BlockSpec((D_IMGS * PATCHES, DW), lambda i: (i, 0)),
    ] + [whole(a.shape) for a in (pos, par, hid, slab)]
    outs = [
        jax.ShapeDtypeStruct((images * PATCHES, DW), b),
        jax.ShapeDtypeStruct((images, VISIBLE, EW), b),
        jax.ShapeDtypeStruct((16, DW), f),
        jax.ShapeDtypeStruct((DEC_CHUNKS, 1, DW), f),
        jax.ShapeDtypeStruct((n, (12 * DW + EW) // n, DW), b),
    ]
    out_specs = [
        pl.BlockSpec((D_IMGS * PATCHES, DW), lambda i: (i, 0)),
        pl.BlockSpec((D_IMGS, VISIBLE, EW), lambda i: (i, 0, 0)),
    ] + [whole(o.shape) for o in outs[2:]]
    scratch = [
        vm((DM, DW), f),
        vm((DM, DW), f),
        vm((DM, DW), f),
        vm((DM, DW), f),
        vm((D_IMGS * PATCHES + 24, DW), f),
        vm((grp, RP, 128), b),
        vm((grp, RP, 128), b),
        vm((grp, RP, 128), b),
        vm((grp, RP, 128), b),
        vm((grp, 128, RP), b),
        vm((grp * D_HPG, RP, RP), b),
        vm((DM, DW), b),
        vm((DW, DM), b),
        vm((DM, DW), b),
        vm((DW, DM), b),
        vm((DM, DW), b),
        vm((DW, DM), b),
        vm((grp, RP, 128), b),
        vm((grp, RP, 128), b),
        vm((grp, RP, 128), b),
        vm((grp, RP, 128), b),
        vm((DW, DW), f),
        vm((DW, DW), f),
        vm((DW, DW), f),
        vm((DW, DW), f),
        vm((DEC_CHUNKS, DW, DW), f),
        vm((DEC_CHUNKS, DW, DW), f),
        vm((EW, DW), f),
        vm((EW, DW), b),
    ]
    return pl.pallas_call(
        dec_kernel,
        grid=(images // D_IMGS,),
        in_specs=ins,
        out_specs=out_specs,
        out_shape=outs,
        scratch_shapes=scratch,
        compiler_params=pltpu.CompilerParams(
            dimension_semantics=("arbitrary",), vmem_limit_bytes=60 << 20
        ),
        cost_estimate=pl.CostEstimate(
            flops=225 * 10**9, transcendentals=0, bytes_accessed=250 * 10**6
        ),
        name="decoder",
    )(recv, visr, visc, cot, pos, par, hid, slab)


EM = ENC_GROUPS * RP
E_HB = 3
E_J = ENC_GROUPS * 2
E_HPG = 128 // ENC_HEAD
GROUP_IMGS = IMG_DEV // ENC_GROUPS
WIN = 56


def seg_of(i):
    return (
        jnp.where(i >= VISIBLE, 1, 0)
        + jnp.where(i >= 2 * VISIBLE, 1, 0)
        + jnp.where(i >= 3 * VISIBLE, 1, 0)
        + jnp.where(i >= 4 * VISIBLE, 1, 0)
    )


def enc_attn_kernel(
    start_ref,
    x_ref,
    par_ref,
    parb_ref,
    wq_ref,
    wk_ref,
    wv_ref,
    wo_ref,
    xc_o,
    q_o,
    k_o,
    v_o,
    pt_o,
    ot_o,
    x2_o,
    xf_s,
    xc_s,
    a1_s,
    o_s,
    bias_s,
):
    step = pl.program_id(0)

    @pl.when(step == 0)
    def _():
        xf_s[pl.ds(0, ROWS_DEV), :] = x_ref[...].astype(F32)
        for grp in range(ENC_GROUPS):
            xc_s[pl.ds(grp * RP + PATCHES, RP - PATCHES), :] = jnp.zeros((RP - PATCHES, EW), F32)
            for i in range(GROUP_IMGS):
                start = start_ref[grp * GROUP_IMGS + i]
                shift = lax.rem(start, 8)
                base = pl.multiple_of(start - shift, 8)
                part = pltpu.roll(xf_s[pl.ds(base, WIN), :], WIN - shift, 0)
                xc_s[pl.ds(grp * RP + i * VISIBLE, VISIBLE), :] = part[:VISIBLE]
        x = xc_s[...]
        xc_o[...] = x.astype(BF16)
        xhat, _ = norm_stats(x)
        a1_s[...] = (xhat * par_ref[0:1] + par_ref[2:3]).astype(BF16)
        x2_o[...] = x + par_ref[6:7]
        keys = lax.broadcasted_iota(jnp.int32, (RP, RP), 0)
        queries = lax.broadcasted_iota(jnp.int32, (RP, RP), 1)
        same = (seg_of(keys) == seg_of(queries)) & (keys < PATCHES)
        bias_s[...] = jnp.where(same, 0.0, NEG)

    for w_ref, row, dst in ((wq_ref, 4, q_o), (wk_ref, None, k_o), (wv_ref, 5, v_o)):
        val = nn(a1_s[...], w_ref[...])
        if row is not None:
            val = val + parb_ref[row : row + 1]
        val = val.astype(BF16)
        for grp in range(ENC_GROUPS):
            for half in range(2):
                dst[0, grp * 2 + half] = val[
                    grp * RP : (grp + 1) * RP, half * 128 : (half + 1) * 128
                ]

    def loop(j, carry):
        def store(h, pt):
            pt_o[0, j * E_HPG + h] = pt

        ot = attend_fwd(
            q_o[0, j], k_o[0, j], v_o[0, j], ENC_HEAD, lambda st: st + bias_s[...], store
        )
        ot_o[0, j] = ot.astype(BF16)
        o_s[j] = jnp.transpose(ot).astype(BF16)
        return carry

    lax.fori_loop(0, E_J, loop, 0, unroll=4)
    o_full = jnp.concatenate(
        [
            jnp.concatenate([o_s[grp * 2], o_s[grp * 2 + 1]], axis=1)
            for grp in range(ENC_GROUPS)
        ],
        axis=0,
    )
    x2_o[...] += nn(o_full, wo_ref[...])


def enc_attn(starts, x, par, wq, wk, wv, wo):
    f, b = F32, BF16
    vm = pltpu.VMEM
    col = pl.BlockSpec((EW, 256), lambda i, s: (0, i))
    row = pl.BlockSpec((256, EW), lambda i, s: (i, 0))
    grp = pl.BlockSpec((1, E_J, RP, 128), lambda i, s: (i, 0, 0, 0))
    outs = [
        (jax.ShapeDtypeStruct((EM, EW), b), whole((EM, EW))),
        (jax.ShapeDtypeStruct((E_HB, E_J, RP, 128), b), grp),
        (jax.ShapeDtypeStruct((E_HB, E_J, RP, 128), b), grp),
        (jax.ShapeDtypeStruct((E_HB, E_J, RP, 128), b), grp),
        (
            jax.ShapeDtypeStruct((E_HB, E_J * E_HPG, RP, RP), b),
            pl.BlockSpec((1, E_J * E_HPG, RP, RP), lambda i, s: (i, 0, 0, 0)),
        ),
        (
            jax.ShapeDtypeStruct((E_HB, E_J, 128, RP), b),
            pl.BlockSpec((1, E_J, 128, RP), lambda i, s: (i, 0, 0, 0)),
        ),
        (jax.ShapeDtypeStruct((EM, EW), f), whole((EM, EW))),
    ]
    return pl.pallas_call(
        enc_attn_kernel,
        grid_spec=pltpu.PrefetchScalarGridSpec(
            num_scalar_prefetch=1,
            grid=(E_HB,),
            in_specs=[
                whole(x.shape),
                whole(par.shape),
                pl.BlockSpec((8, 256), lambda i, s: (0, i)),
                col,
                col,
                col,
                row,
            ],
            out_specs=[o[1] for o in outs],
            scratch_shapes=[
                vm((ROWS_DEV + 16, EW), f),
                vm((EM, EW), f),
                vm((EM, EW), b),
                vm((E_J, RP, 128), b),
                vm((RP, RP), f),
            ],
        ),
        out_shape=[o[0] for o in outs],
        compiler_params=pltpu.CompilerParams(
            dimension_semantics=("arbitrary",), vmem_limit_bytes=60 << 20
        ),
        cost_estimate=pl.CostEstimate(
            flops=27 * 10**9, transcendentals=0, bytes_accessed=30 * 10**6
        ),
        name="enc_attn",
    )(starts, x, par, par, wq, wk, wv, wo)


def enc_mlp_kernel(
    x2_ref, par_ref, hid_ref, wup_ref, wdn_ref, yl_o, hid_o, dg_o, a2_s, y_s
):
    step = pl.program_id(0)

    @pl.when(step == 0)
    def _():
        x2 = x2_ref[...]
        xhat, _ = norm_stats(x2)
        a2_s[...] = (xhat * par_ref[1:2] + par_ref[3:4]).astype(BF16)
        y_s[...] = x2 + par_ref[7:8]

    u = nn(a2_s[...], wup_ref[0]) + hid_ref[0]
    hid, dgelu = gelu_both(u)
    hid = hid.astype(BF16)
    hid_o[0] = hid
    dg_o[0] = dgelu.astype(BF16)
    y_s[...] += nn(hid, wdn_ref[0])

    @pl.when(step == pl.num_programs(0) - 1)
    def _():
        for grp in range(ENC_GROUPS):
            for i in range(GROUP_IMGS):
                part = y_s[pl.ds(grp * RP + i * VISIBLE, VISIBLE), :]
                yl_o[grp * GROUP_IMGS + i] = part.astype(BF16)


def enc_mlp(x2, par, hid, wup, wdn):
    f, b = F32, BF16
    chunk = pl.BlockSpec((1, EM, EW), lambda i: (i, 0, 0))
    wchunk = pl.BlockSpec((1, EW, EW), lambda i: (i, 0, 0))
    outs = [
        (jax.ShapeDtypeStruct((IMG_DEV, VISIBLE, EW), b), whole((IMG_DEV, VISIBLE, EW))),
        (jax.ShapeDtypeStruct((ENC_CHUNKS, EM, EW), b), chunk),
        (jax.ShapeDtypeStruct((ENC_CHUNKS, EM, EW), b), chunk),
    ]
    return pl.pallas_call(
        enc_mlp_kernel,
        grid=(ENC_CHUNKS,),
        in_specs=[
            whole(x2.shape),
            whole(par.shape),
            pl.BlockSpec((1, 1, EW), lambda i: (i, 0, 0)),
            wchunk,
            wchunk,
        ],
        out_specs=[o[1] for o in outs],
        out_shape=[o[0] for o in outs],
        scratch_shapes=[pltpu.VMEM((EM, EW), b), pltpu.VMEM((EM, EW), f)],
        compiler_params=pltpu.CompilerParams(
            dimension_semantics=("arbitrary",), vmem_limit_bytes=60 << 20
        ),
        cost_estimate=pl.CostEstimate(
            flops=21 * 10**9, transcendentals=0, bytes_accessed=24 * 10**6
        ),
        name="enc_mlp",
    )(x2, par, hid, wup, wdn)


def enc_mlp_back_kernel(
    gy_ref,
    x2_ref,
    par_ref,
    hid_ref,
    dg_ref,
    wup_ref,
    wdn_ref,
    gx2_o,
    small_o,
    ghid_o,
    grad_o,
    gf_s,
    gm_s,
    a2t_s,
    ga_s,
    up_s,
    dn_s,
    sems,
):
    step = pl.program_id(0)

    @pl.when(step == 0)
    def _():
        for grp in range(ENC_GROUPS):
            gf_s[pl.ds(grp * RP + PATCHES, RP - PATCHES), :] = jnp.zeros((RP - PATCHES, EW), F32)
            for i in range(GROUP_IMGS):
                part = gy_ref[grp * GROUP_IMGS + i].astype(F32)
                gf_s[pl.ds(grp * RP + i * VISIBLE, VISIBLE), :] = part
        gm_s[...] = gf_s[...].astype(BF16)
        xhat, _ = norm_stats(x2_ref[...])
        a2 = (xhat * par_ref[1:2] + par_ref[3:4]).astype(BF16)
        a2t_s[...] = jnp.transpose(a2)
        ga_s[...] = jnp.zeros_like(ga_s)
        small_o[...] = jnp.zeros_like(small_o)
        small_o[pl.ds(7, 1), :] = colsum(gf_s[...])

    gu = (nt(gm_s[...], wdn_ref[0]) * dg_ref[0].astype(F32)).astype(BF16)
    ga_s[...] += nt(gu, wup_ref[0])
    n, er, _ = up_s.shape
    part = n // ENC_CHUNKS
    first = pl.multiple_of(step * er, 8)
    copies = (
        pltpu.make_async_copy(up_s, grad_o.at[:, pl.ds(first, er), :], sems.at[0]),
        pltpu.make_async_copy(
            dn_s, grad_o.at[pl.ds(step * part, part), pl.ds(4 * er, 4 * er), :], sems.at[1]
        ),
    )

    @pl.when(step > 0)
    def _():
        for copy in copies:
            copy.wait()

    up_s[...] = nn(a2t_s[...], gu).reshape(n, er, EW).astype(BF16)
    down = nn(jnp.transpose(hid_ref[0]), gm_s[...])
    dn_s[...] = down.reshape(part, 4 * er, EW).astype(BF16)
    for copy in copies:
        copy.start()
    ghid_o[0] = colsum(gu.astype(F32))

    @pl.when(step == pl.num_programs(0) - 1)
    def _():
        for copy in copies:
            copy.wait()
        ga2 = ga_s[...]
        xhat, rstd = norm_stats(x2_ref[...])
        small_o[pl.ds(1, 1), :] = colsum(ga2 * xhat)
        small_o[pl.ds(3, 1), :] = colsum(ga2)
        gx2 = gf_s[...] + norm_back(xhat, rstd, par_ref[1:2], ga2)
        gx2_o[...] = gx2
        small_o[pl.ds(6, 1), :] = colsum(gx2.astype(BF16).astype(F32))


def enc_mlp_back(n, gy, x2, par, hid, dg, wup, wdn):
    f, b = F32, BF16
    er = EW // n
    chunk = pl.BlockSpec((1, EM, EW), lambda i: (i, 0, 0))
    wchunk = pl.BlockSpec((1, EW, EW), lambda i: (i, 0, 0))
    outs = [
        (jax.ShapeDtypeStruct((EM, EW), f), whole((EM, EW))),
        (jax.ShapeDtypeStruct((8, EW), f), whole((8, EW))),
        (
            jax.ShapeDtypeStruct((ENC_CHUNKS, 1, EW), f),
            pl.BlockSpec((1, 1, EW), lambda i: (i, 0, 0)),
        ),
        (jax.ShapeDtypeStruct((n, 8 * er, EW), b), pl.BlockSpec(memory_space=pl.ANY)),
    ]
    return pl.pallas_call(
        enc_mlp_back_kernel,
        grid=(ENC_CHUNKS,),
        in_specs=[whole(gy.shape), whole(x2.shape), whole(par.shape), chunk, chunk, wchunk, wchunk],
        out_specs=[o[1] for o in outs],
        out_shape=[o[0] for o in outs],
        scratch_shapes=[
            pltpu.VMEM((EM, EW), f),
            pltpu.VMEM((EM, EW), b),
            pltpu.VMEM((EW, EM), b),
            pltpu.VMEM((EM, EW), f),
            pltpu.VMEM((n, er, EW), b),
            pltpu.VMEM((n // ENC_CHUNKS, 4 * er, EW), b),
            pltpu.SemaphoreType.DMA((2,)),
        ],
        compiler_params=pltpu.CompilerParams(
            dimension_semantics=("arbitrary",), vmem_limit_bytes=60 << 20
        ),
        cost_estimate=pl.CostEstimate(
            flops=25 * 10**9, transcendentals=0, bytes_accessed=28 * 10**6
        ),
        name="enc_mlp_back",
    )(gy, x2, par, hid, dg, wup, wdn)


def enc_attn_back_kernel(
    start_ref,
    gx2_ref,
    xc_ref,
    par_ref,
    q_ref,
    k_ref,
    v_ref,
    pt_ref,
    ot_ref,
    wq_ref,
    wk_ref,
    wv_ref,
    wo_ref,
    gx_o,
    gwq_o,
    gwk_o,
    gwv_o,
    gwo_o,
    small_o,
    gb_o,
    gpr_s,
    a1t_s,
    ga_s,
    go_s,
    gq_s,
    gk_s,
    gv_s,
    gf_s,
):
    step = pl.program_id(0)

    @pl.when(step == 0)
    def _():
        gpr_s[...] = gx2_ref[...].astype(BF16)
        xhat, _ = norm_stats(xc_ref[...].astype(F32))
        a1 = (xhat * par_ref[0:1] + par_ref[2:3]).astype(BF16)
        a1t_s[...] = jnp.transpose(a1)
        ga_s[...] = jnp.zeros_like(ga_s)
        small_o[...] = jnp.zeros_like(small_o)

    go = nt(gpr_s[...], wo_ref[...]).astype(BF16)
    for half in range(2):
        acc = None
        for grp in range(ENC_GROUPS):
            rows = slice(grp * RP, (grp + 1) * RP)
            go_s[grp * 2 + half] = go[rows, half * 128 : (half + 1) * 128]
            part = nn(ot_ref[0, grp * 2 + half], gpr_s[pl.ds(grp * RP, RP), :])
            acc = part if acc is None else acc + part
        gwo_o[pl.ds(half * 128, 128), :] = acc.astype(BF16)

    def loop(j, carry):
        gq, gk, gv = attend_bwd(
            q_ref[0, j],
            k_ref[0, j],
            v_ref[0, j],
            go_s[j],
            ENC_HEAD,
            lambda h: pt_ref[0, j * E_HPG + h],
        )
        gq_s[j] = gq
        gk_s[j] = gk
        gv_s[j] = gv
        return carry

    lax.fori_loop(0, E_J, loop, 0, unroll=4)
    gb_o[...] = jnp.zeros_like(gb_o)
    ga1 = ga_s[...]
    for src, w_ref, dst, row in (
        (gq_s, wq_ref, gwq_o, 4),
        (gk_s, wk_ref, gwk_o, None),
        (gv_s, wv_ref, gwv_o, 5),
    ):
        full = jnp.concatenate(
            [
                jnp.concatenate([src[grp * 2], src[grp * 2 + 1]], axis=1)
                for grp in range(ENC_GROUPS)
            ],
            axis=0,
        )
        if row is not None:
            gb_o[pl.ds(row, 1), :] = colsum(full.astype(F32))
        dst[...] = nn(a1t_s[...], full).astype(BF16)
        ga1 = ga1 + nt(full, w_ref[...])
    ga_s[...] = ga1

    @pl.when(step == pl.num_programs(0) - 1)
    def _():
        ga = ga_s[...]
        xhat, rstd = norm_stats(xc_ref[...].astype(F32))
        small_o[pl.ds(0, 1), :] = colsum(ga * xhat)
        small_o[pl.ds(2, 1), :] = colsum(ga)
        ga_s[...] = gx2_ref[...] + norm_back(xhat, rstd, par_ref[0:1], ga)
        gf_s[...] = jnp.zeros_like(gf_s)
        rows = lax.broadcasted_iota(jnp.int32, (WIN, EW), 0)
        for grp in range(ENC_GROUPS):
            for i in range(GROUP_IMGS):
                start = start_ref[grp * GROUP_IMGS + i]
                shift = lax.rem(start, 8)
                base = pl.multiple_of(start - shift, 8)
                first = grp * RP + i * VISIBLE
                part = jnp.where(rows < VISIBLE, ga_s[pl.ds(first, WIN), :], 0.0)
                gf_s[pl.ds(base, WIN), :] += pltpu.roll(part, shift, 0)
        gx_o[...] = gf_s[pl.ds(0, ROWS_DEV), :]


def enc_attn_back(starts, gx2, xc, par, q, k, v, pt, ot, wq, wk, wv, wo):
    f, b = F32, BF16
    vm = pltpu.VMEM
    col = pl.BlockSpec((EW, 256), lambda i, s: (0, i))
    row = pl.BlockSpec((256, EW), lambda i, s: (i, 0))
    grp = pl.BlockSpec((1, E_J, RP, 128), lambda i, s: (i, 0, 0, 0))
    square = jax.ShapeDtypeStruct((EW, EW), b)
    outs = [
        (jax.ShapeDtypeStruct((ROWS_DEV, EW), f), whole((ROWS_DEV, EW))),
        (square, col),
        (square, col),
        (square, col),
        (square, row),
        (jax.ShapeDtypeStruct((8, EW), f), whole((8, EW))),
        (jax.ShapeDtypeStruct((8, EW), f), pl.BlockSpec((8, 256), lambda i, s: (0, i))),
    ]
    return pl.pallas_call(
        enc_attn_back_kernel,
        grid_spec=pltpu.PrefetchScalarGridSpec(
            num_scalar_prefetch=1,
            grid=(E_HB,),
            in_specs=[
                whole(gx2.shape),
                whole(xc.shape),
                whole(par.shape),
                grp,
                grp,
                grp,
                pl.BlockSpec((1, E_J * E_HPG, RP, RP), lambda i, s: (i, 0, 0, 0)),
                pl.BlockSpec((1, E_J, 128, RP), lambda i, s: (i, 0, 0, 0)),
                col,
                col,
                col,
                row,
            ],
            out_specs=[o[1] for o in outs],
            scratch_shapes=[
                vm((EM, EW), b),
                vm((EW, EM), b),
                vm((EM, EW), f),
                vm((E_J, RP, 128), b),
                vm((E_J, RP, 128), b),
                vm((E_J, RP, 128), b),
                vm((E_J, RP, 128), b),
                vm((ROWS_DEV + 16, EW), f),
            ],
        ),
        out_shape=[o[0] for o in outs],
        compiler_params=pltpu.CompilerParams(
            dimension_semantics=("arbitrary",), vmem_limit_bytes=60 << 20
        ),
        cost_estimate=pl.CostEstimate(
            flops=36 * 10**9, transcendentals=0, bytes_accessed=40 * 10**6
        ),
        name="enc_attn_back",
    )(starts, gx2, xc, par, q, k, v, pt, ot, wq, wk, wv, wo)


def position_rows():
    quarter = DW // 4
    frequency = 1.0 / 10000.0 ** (np.arange(quarter) / quarter)
    cells = np.arange(PATCHES)
    by_row = (cells // SIDE)[:, None] * frequency[None, :]
    by_col = (cells % SIDE)[:, None] * frequency[None, :]
    table = np.concatenate([np.sin(by_row), np.cos(by_row), np.sin(by_col), np.cos(by_col)], axis=1)
    return np.pad(table, ((0, RP - PATCHES), (0, 0))).astype(np.float32)


def small_rows(parts, width):
    flat = jnp.concatenate([p.reshape(-1) for p in parts])
    return jnp.pad(flat, (0, 8 * width - flat.shape[0])).reshape(8, width)


def col_blocks(w, width):
    return [w[:, i : i + width] for i in range(0, w.shape[1], width)]


def per_device(v, n):
    rows = v.shape[0]
    return v.reshape(rows, n, -1).transpose(1, 0, 2).reshape(n, -1)


def all_devices(v, rows):
    n = v.shape[0]
    return v.reshape(n, rows, -1).transpose(1, 0, 2).reshape(rows, -1)


def pairs(count, minor, flip_major, flip_minor):
    return [
        (i, (i // minor ^ flip_major) * minor + (i % minor ^ flip_minor)) for i in range(count)
    ]


def send(v, sizes, flip_dp=0, flip_fsdp=0):
    dp, fsdp = sizes
    return lax.ppermute(v, BOTH, pairs(dp * fsdp, fsdp, flip_dp, flip_fsdp))


def gather_fsdp(v, sizes):
    fsdp = sizes[1]
    me = lax.axis_index("fsdp")
    parts = [v] + [send(v, sizes, 0, k) for k in range(1, fsdp)]
    bit = 1
    while bit < fsdp:
        odd = (me & bit) != 0
        parts = [jnp.where(odd, parts[i ^ bit], parts[i]) for i in range(fsdp)]
        bit *= 2
    return jnp.stack(parts)


def gather_dp(block):
    _, rows, width = block.shape
    full = lax.all_gather(block.reshape(-1, width), "dp", axis=0, tiled=True)
    return full.reshape(-1, rows, width)


def pick(v, index, axis=0):
    return lax.dynamic_index_in_dim(v, index, axis, keepdims=False)


def spread_fsdp(v, sizes):
    me = lax.axis_index("fsdp")
    others = [send(pick(v, me ^ k), sizes, 0, k) for k in range(1, sizes[1])]
    return pick(v, me), others


def total(mine, others):
    mine = mine.astype(F32)
    for other in others:
        mine = mine + other.astype(F32)
    return mine


def scatter_dp(packed, sizes):
    n, rows, width = packed.shape
    flat = lax.psum_scatter(
        packed.reshape(n * rows, width), "dp", scatter_dimension=0, tiled=True
    )
    return flat.reshape(sizes[1], rows, width)


def scatter_chips(v, sizes):
    dp, fsdp = sizes
    groups = [list(range(core, dp, 2)) for core in range(2)]
    rows, width = v.shape[-2:]
    flat = lax.psum_scatter(
        v.reshape(-1, width), "dp", scatter_dimension=0, axis_index_groups=groups, tiled=True
    )
    return flat.reshape(fsdp, rows, width)


def halves(v, sizes, axis, bit):
    mine = (lax.axis_index("dp") // bit) % 2
    return pick(v, mine, axis), send(pick(v, 1 - mine, axis), sizes, bit, 0)


def add(pair):
    return (pair[0].astype(F32) + pair[1].astype(F32)).astype(BF16)


def low_high(lows, highs, sizes, step):
    left = sizes[0].bit_length() - 2 - step
    return (
        halves(lows, sizes, left - 1, 2 ** (step + 1)),
        halves(highs, sizes, 0, 2 ** left),
    )


def make_body(sizes):
    n = sizes[0] * sizes[1]
    bits = sizes[0].bit_length() - 1
    er, dr = EW // n, DW // n

    def body(
        patches,
        segments,
        send_slot,
        visible,
        enc_gain,
        enc_shift,
        enc_hidden,
        enc_qkv,
        enc_out,
        enc_up,
        enc_down,
        embedding,
        mask_token,
        dec_gain,
        dec_shift,
        dec_hidden,
        dec_qkv,
        dec_out,
        dec_up,
        dec_down,
        cotangent,
    ):
        pack_a = jnp.concatenate(
            col_blocks(enc_qkv, EW) + [enc_out, small_rows((enc_gain, enc_shift, enc_hidden), EW)]
        )
        pack_b = jnp.concatenate(col_blocks(enc_up, EW) + [enc_down])
        pack_d = jnp.concatenate(
            col_blocks(dec_qkv, DW)
            + [dec_out]
            + col_blocks(dec_up, DW)
            + [
                dec_down,
                embedding,
                small_rows((mask_token, dec_gain, dec_shift, dec_hidden), DW),
            ]
        )
        block_a = gather_fsdp(pack_a, sizes)
        block_a, pack_b = lax.optimization_barrier((block_a, pack_b))
        full_a = gather_dp(block_a)
        block_b = gather_fsdp(pack_b, sizes)
        full_b = gather_dp(block_b)
        full_a, pack_d = lax.optimization_barrier((full_a, pack_d))
        block_d = gather_fsdp(pack_d, sizes)
        full_d = gather_dp(block_d)

        wq, wk, wv, wo = [full_a[:, i * er : (i + 1) * er].reshape(EW, EW) for i in range(4)]
        small = full_a[:, 4 * er :].reshape(n, -1).astype(F32)
        par = all_devices(small[:, : 8 * er], 8)
        hid = small[:, 8 * er : 12 * er].reshape(ENC_CHUNKS, 1, EW)
        wup = full_b[:, : 4 * er].reshape(n, 4, er, EW).transpose(1, 0, 2, 3).reshape(4, EW, EW)
        wdn = full_b[:, 4 * er :].reshape(4, EW, EW)

        row_ids = jnp.arange(ROWS_DEV, dtype=jnp.int32)
        image_ids = jnp.arange(IMG_DEV, dtype=jnp.int32)
        starts = jnp.min(
            jnp.where(segments[None, :] == image_ids[:, None], row_ids[None, :], ROWS_DEV), axis=1
        )
        hot = send_slot[0][None, :] == image_ids[:, None]
        slot_starts = jnp.sum(jnp.where(hot, starts[None, :], 0), axis=1).astype(jnp.int32)

        xc, q, k, v, pt, ot, x2 = enc_attn(slot_starts, patches, par, wq, wk, wv, wo)
        outgoing, hidden, dgelu = enc_mlp(x2, par, hid, wup, wdn)
        received = lax.all_to_all(outgoing, "dp", split_axis=0, concat_axis=0, tiled=True)

        dsmall = full_d[:, 12 * dr + er :].reshape(n, -1).astype(F32)
        dpar = jnp.concatenate([all_devices(dsmall[:, : 10 * dr], 10), jnp.zeros((6, DW), F32)])
        dhid = dsmall[:, 10 * dr : 14 * dr].reshape(DEC_CHUNKS, 1, DW)
        pos = jnp.asarray(position_rows())

        whole_slabs = er % 8 == 0 and dr % 8 == 0
        slabs = n if whole_slabs else 32
        pieces_d = [DW] * 8 + [4 * DW, EW]

        def regroup(v, pieces, count):
            if v.shape[0] == count:
                return v
            outs, at = [], 0
            for total_rows in pieces:
                rows = total_rows // v.shape[0]
                outs.append(v[:, at : at + rows].reshape(count, -1, v.shape[-1]))
                at += rows
            return jnp.concatenate(outs, axis=1)

        decoded, gyl, gdsmall, gdhid, dpacked = decoder(
            received, visible, cotangent, pos, dpar, dhid, regroup(full_d, pieces_d, slabs)
        )
        returned = lax.all_to_all(gyl, "dp", split_axis=0, concat_axis=0, tiled=True)

        def rows_of(v, width):
            return v.reshape(n, -1, width)

        def small_pack(vals, width):
            flat = jnp.concatenate(vals, axis=1)
            flat = jnp.pad(flat, ((0, 0), (0, 8 * width - flat.shape[1])))
            return flat.astype(BF16).reshape(n, 8, width)

        dpacked = regroup(dpacked, pieces_d, n)
        dpart = scatter_dp(dpacked, sizes)
        gx2, sm1, ghid, bpacked = enc_mlp_back(
            slabs, returned, x2, par, hidden, dgelu, wup, wdn
        )
        bpacked = regroup(bpacked, [EW] * 4 + [4 * EW], n)
        bhalf = add(halves(bpacked.reshape((2,) * bits + (sizes[1], -1, EW)), sizes, bits - 1, 1))
        bhalf, gx2 = lax.optimization_barrier((bhalf, gx2))
        bpart = scatter_chips(bhalf, sizes)
        gx, gwq, gwk, gwv, gwo, sm2, gb = enc_attn_back(
            slot_starts, gx2, xc, par, q, k, v, pt, ot, wq, wk, wv, wo
        )
        apacked = jnp.concatenate(
            [rows_of(g, EW) for g in (gwq, gwk, gwv, gwo)]
            + [
                small_pack(
                    [
                        per_device(sm1 + sm2 + gb, n),
                        ghid.reshape(n, -1),
                        per_device(gdsmall[:10], n),
                        gdhid.reshape(n, -1),
                    ],
                    EW,
                )
            ],
            axis=1,
        )
        barrier = lax.optimization_barrier
        apart = add(halves(apacked.reshape((2,) * bits + (sizes[1], -1, EW)), sizes, bits - 1, 1))
        apart, dpart = barrier((apart, dpart))
        acut = apart.shape[-2] // 16 * 8
        alow, ahigh = apart[..., :acut, :], apart[..., acut:, :]
        for step in range(bits - 1):
            pairs_a = low_high(alow, ahigh, sizes, step)
            if step == 0:
                spread_d = spread_fsdp(dpart, sizes)
                pairs_a, spread_d = barrier((pairs_a, spread_d))
            if step == 1:
                spread_b = spread_fsdp(bpart, sizes)
                pairs_a, spread_b = barrier((pairs_a, spread_b))
            alow, ahigh = add(pairs_a[0]), add(pairs_a[1])
        dsum = total(*spread_d)
        spread_a = spread_fsdp(jnp.concatenate([alow, ahigh], axis=-2), sizes)
        asum = total(*spread_a)
        bsum = total(*spread_b)

        def cut(v, r, count, first=0):
            return jnp.concatenate(
                [v[(first + i) * r : (first + i + 1) * r] for i in range(count)], axis=1
            )

        esm = asum[4 * er :].reshape(-1)
        dsm = esm[12 * er :]
        return (
            decoded,
            gx,
            esm[: 2 * er].reshape(2, er),
            esm[2 * er : 8 * er].reshape(6, er),
            esm[8 * er : 12 * er],
            cut(asum, er, 3),
            asum[3 * er : 4 * er],
            cut(bsum, er, 4),
            bsum[4 * er :],
            dsum[12 * dr : 12 * dr + er],
            dsm[:dr],
            dsm[dr : 3 * dr].reshape(2, dr),
            dsm[3 * dr : 10 * dr].reshape(7, dr),
            dsm[10 * dr : 14 * dr],
            cut(dsum, dr, 3),
            dsum[3 * dr : 4 * dr],
            cut(dsum, dr, 4, 4),
            dsum[8 * dr : 12 * dr],
        )

    return body


def solution(mesh):
    sizes = (mesh.shape["dp"], mesh.shape["fsdp"])
    rows, vec, cols = P(BOTH, None), P(BOTH), P(None, BOTH)
    return jax.shard_map(
        make_body(sizes),
        mesh=mesh,
        in_specs=(rows, vec, rows, rows, cols, cols, vec, rows, rows, rows, rows)
        + (rows, vec, cols, cols, vec, rows, rows, rows, rows, rows),
        out_specs=(rows, rows, cols, cols, vec, rows, rows, rows, rows)
        + (rows, vec, cols, cols, vec, rows, rows, rows, rows),
        check_vma=False,
    )
```
